32 devices in a mesh: dp: 8 (over z, core), tensor: 4 (over y, x).
Axes of the slice: x: 2, y: 2, z: 4, core: 2. Of those that a mesh axis runs over, the one named last changes fastest.
Arguments:
- tokens: bfloat16 [16384, 1152], P(('dp', 'tensor')), may hold values from -6 to 6
- norm_gains: float32 [2, 1152], P(None, ('dp', 'tensor')), may hold values from 0.5 to 1.5
- row_biases: float32 [4, 1152], P(None, ('dp', 'tensor')), may hold values from -3 to 3
- w_qkv: bfloat16 [3, 1152, 1152], P(None, 'dp', 'tensor'), may hold values from -1 to 1
- head_bias: float32 [2, 1152], P(None, 'tensor'), may hold values from -3 to 3
- w_out: bfloat16 [1152, 1152], P('tensor', 'dp'), may hold values from -1.5 to 1.5
- w_fc1: bfloat16 [1152, 4304], P('dp', 'tensor'), may hold values from -0.1875 to 0.1875
- fc1_bias: float32 [4304], P('tensor'), may hold values from -3 to 3
- w_fc2: bfloat16 [4304, 1152], P('tensor', 'dp'), may hold values from -0.09375 to 0.09375
- cotangent: bfloat16 [16384, 1152], P(('dp', 'tensor')), may hold values from -6 to 6
Outputs:
- output: float32 [16384, 1152], P(('dp', 'tensor'))
- grad_tokens: float32 [16384, 1152], P(('dp', 'tensor'))
- grad_norm_gains: float32 [2, 1152], P(None, ('dp', 'tensor'))
- grad_row_biases: float32 [4, 1152], P(None, ('dp', 'tensor'))
- grad_w_qkv: float32 [3, 1152, 1152], P(None, 'dp', 'tensor')
- grad_head_bias: float32 [2, 1152], P(None, 'tensor')
- grad_w_out: float32 [1152, 1152], P('tensor', 'dp')
- grad_w_fc1: float32 [1152, 4304], P('dp', 'tensor')
- grad_fc1_bias: float32 [4304], P('tensor')
- grad_w_fc2: float32 [4304, 1152], P('tensor', 'dp')
The draws below stay inside these ranges and needn't reach their ends.
All inputs are finite; a program needn't handle non-finite values.
Results may differ from the reference program's by a relative error of at most 0.04.
Values may be sent and summed in bfloat16 or wider, within the bound.
No kernel may reach another device: no remote copies, remote signals or barrier semaphores. Data moves between devices by JAX's collectives and lax.ppermute only.
A program may use at most 192 MiB of HBM per device.

```python
import jax
import jax.numpy as jnp
from jax import lax

D = 1152
HEADS = 16
HD = 72
FF = 4304
SEQ = 256
IMG_DEV = 2
HW = 1152
TOKENS = 16384
N_DP = 8
N_TENSOR = 4


def draw_w_qkv(key, part):
    key_one = jax.random.fold_in(key, 0)
    base_draw = jax.random.normal(key_one, (3, D, HW), jnp.float32) * D ** (-0.5)
    return jnp.clip(base_draw, -1.0, 1.0).astype(jnp.bfloat16)


def levels(key, extent, pieces, smallest, high):
    def one(position, parts):
        heights = jax.random.uniform(jax.random.fold_in(jax.random.fold_in(key, 6), position), (parts,), jnp.float32, smallest / len(pieces), high / len(pieces))
        return jnp.repeat(jnp.exp(heights), extent[position] // parts).reshape((-1,) + (1,) * (len(extent) - position - 1))

    gain = one(*pieces[0])
    for cut in pieces[1:]:
        gain = gain * one(*cut)
    return gain


def centred(stream_key, extent, scale, limit, cuts=(), held_as=jnp.bfloat16):
    drawn = scale * jax.random.normal(stream_key, extent, jnp.float32)
    if cuts:
        drawn = drawn * levels(stream_key, extent, cuts, -0.22, 0.18)
    return jnp.clip(drawn, -limit, limit).astype(held_as)


def setup_inputs(seed: int = 0) -> dict:
    splits = jax.random.split(jax.random.key(seed), 11)
    tokens = centred(splits[0], (TOKENS, D), 1.0, 6.0, ((0, 32),))
    norm_gains = jnp.clip(1.0 + 0.1 * jax.random.normal(splits[1], (2, D), jnp.float32), 0.5, 1.5)
    row_biases = centred(splits[2], (4, D), 0.5, 3.0, ((1, 32),), jnp.float32)
    w_qkv = draw_w_qkv(jax.random.fold_in(splits[10], 71), 0)
    head_bias = centred(splits[4], (2, HW), 0.5, 3.0, ((1, 4),), jnp.float32)
    w_out = centred(splits[5], (HW, D), (max(1, HW * 4 // SEQ)) ** -0.5, 1.5, ((0, 4), (1, 8)))
    w_fc1 = centred(splits[6], (D, FF), D ** -0.5, 0.1875, ((0, 8), (1, 4)))
    fc1_bias = centred(splits[7], (FF,), 0.5, 3.0, ((0, 4),), jnp.float32)
    w_fc2 = centred(splits[8], (FF, D), FF ** -0.5, 0.09375, ((0, 4), (1, 8)))
    cotangent = centred(splits[9], (TOKENS, D), 1.0, 6.0, ((0, 32),))
    return {"tokens": tokens, "norm_gains": norm_gains, "row_biases": row_biases, "w_qkv": w_qkv, "head_bias": head_bias, "w_out": w_out, "w_fc1": w_fc1, "fc1_bias": fc1_bias, "w_fc2": w_fc2, "cotangent": cotangent}


EPS = 1e-06

def norm_rows(values, gain_row, shifts):
    center = values - lax.optimization_barrier(jnp.mean(values, axis=-1, keepdims=True))
    spread = lax.rsqrt(lax.optimization_barrier(jnp.mean(center * center, axis=-1, keepdims=True)) + EPS)
    normed = center * spread
    return (normed * gain_row + shifts, normed, spread)

def norm_back(grad_rows, normed, spread, gain_row):
    scaled = grad_rows * gain_row
    return spread * (scaled - lax.optimization_barrier(jnp.mean(scaled, axis=-1, keepdims=True)) - normed * lax.optimization_barrier(jnp.mean(scaled * normed, axis=-1, keepdims=True)))

def rounded(values):
    return lax.optimization_barrier(values.astype(jnp.bfloat16)).astype(jnp.float32)

def split_sum(left_side, right_side):
    row_total = left_side.shape[0]
    inner_size = left_side.shape[1] // N_TENSOR
    left_groups = left_side.astype(jnp.float32).reshape(row_total, N_TENSOR, inner_size)
    right_groups = right_side.astype(jnp.float32).reshape(N_TENSOR, inner_size, right_side.shape[1])
    partial_value = jnp.einsum('rtk,tkm->trm', left_groups, right_groups)
    return lax.optimization_barrier(jnp.sum(rounded(partial_value), axis=0))

def gelu_tanh(pre_act):
    return jax.nn.gelu(pre_act, approximate=True)

def split_heads(values, images):
    return values.astype(jnp.float32).reshape(images, SEQ, HEADS, HD)

def group_pass(inputs_in, cot_in, norm_gains, row_biases, w_qkv, head_bias, w_out, w_fc1, fc1_bias, w_fc2):
    row_total = inputs_in.shape[0]
    images = row_total // SEQ
    inv_root = HD ** (-0.5)
    inputs_f = inputs_in.astype(jnp.float32)
    first_f, normed_one, spread_one = norm_rows(inputs_f, norm_gains[0], row_biases[0])
    first_in = first_f.astype(jnp.bfloat16)
    query_rows = ((jnp.dot(first_in, w_qkv[0], preferred_element_type=jnp.float32) + head_bias[0]) * inv_root).astype(jnp.bfloat16)
    keys_rows = jnp.dot(first_in, w_qkv[1], preferred_element_type=jnp.float32).astype(jnp.bfloat16)
    vals_rows = (jnp.dot(first_in, w_qkv[2], preferred_element_type=jnp.float32) + head_bias[1]).astype(jnp.bfloat16)
    query_h = split_heads(query_rows, images)
    keys_h = split_heads(keys_rows, images)
    vals_h = split_heads(vals_rows, images)
    scores = jnp.einsum('gqhe,gkhe->ghqk', query_h, keys_h)
    top_score = lax.optimization_barrier(jnp.max(scores, axis=-1, keepdims=True))
    log_norm = top_score + jnp.log(lax.optimization_barrier(jnp.sum(jnp.exp(scores - top_score), axis=-1, keepdims=True)))
    probs_f = jnp.exp(scores - log_norm)
    probs_b = probs_f.astype(jnp.bfloat16).astype(jnp.float32)
    mixed = jnp.einsum('ghqk,gkhe->gqhe', probs_b, vals_h).reshape(row_total, HW).astype(jnp.bfloat16)
    hidden_one = inputs_f + split_sum(mixed, w_out) + row_biases[1]
    second_f, normed_two, spread_two = norm_rows(hidden_one, norm_gains[1], row_biases[2])
    second_in = second_f.astype(jnp.bfloat16)
    pre_act = jnp.dot(second_in, w_fc1, preferred_element_type=jnp.float32) + fc1_bias
    act_out, gelu_back = jax.vjp(gelu_tanh, pre_act)
    act_in = act_out.astype(jnp.bfloat16)
    output = hidden_one + split_sum(act_in, w_fc2) + row_biases[3]
    cot_f = cot_in.astype(jnp.float32)
    grad_fc2 = jnp.dot(act_in.T, cot_in, preferred_element_type=jnp.float32)
    grad_act = jnp.dot(cot_in, w_fc2.T, preferred_element_type=jnp.float32)
    grad_pre = gelu_back(grad_act)[0]
    grad_fc1_bias = lax.optimization_barrier(jnp.sum(grad_pre, axis=0))
    grad_pre_in = grad_pre.astype(jnp.bfloat16)
    grad_fc1 = jnp.dot(second_in.T, grad_pre_in, preferred_element_type=jnp.float32)
    grad_second = split_sum(grad_pre_in, w_fc1.T)
    gain_two = lax.optimization_barrier(jnp.sum(grad_second * normed_two, axis=0))
    shift_two = lax.optimization_barrier(jnp.sum(grad_second, axis=0))
    grad_hidden = cot_f + norm_back(grad_second, normed_two, spread_two, norm_gains[1])
    shift_out = lax.optimization_barrier(jnp.sum(grad_hidden, axis=0))
    shift_fc2 = lax.optimization_barrier(jnp.sum(cot_f, axis=0))
    grad_hidden_in = grad_hidden.astype(jnp.bfloat16)
    grad_wout = jnp.dot(mixed.T, grad_hidden_in, preferred_element_type=jnp.float32)
    grad_mixed = jnp.dot(grad_hidden_in, w_out.T, preferred_element_type=jnp.float32).astype(jnp.bfloat16)
    grad_mixed_h = split_heads(grad_mixed, images)
    grad_vals = jnp.einsum('ghqk,gqhe->gkhe', probs_b, grad_mixed_h)
    grad_probs = jnp.einsum('gqhe,gkhe->ghqk', grad_mixed_h, vals_h)
    grad_scores = probs_f * (grad_probs - lax.optimization_barrier(jnp.sum(probs_f * grad_probs, axis=-1, keepdims=True)))
    grad_scores_b = grad_scores.astype(jnp.bfloat16).astype(jnp.float32)
    grad_query = jnp.einsum('ghqk,gkhe->gqhe', grad_scores_b, keys_h) * inv_root
    grad_keys = jnp.einsum('ghqk,gqhe->gkhe', grad_scores_b, query_h)
    grad_query = grad_query.reshape(row_total, HW)
    grad_keys = grad_keys.reshape(row_total, HW)
    grad_vals = grad_vals.reshape(row_total, HW)
    grad_head = jnp.stack([lax.optimization_barrier(jnp.sum(grad_query, axis=0)), lax.optimization_barrier(jnp.sum(grad_vals, axis=0))])
    grad_proj = jnp.stack([grad_query, grad_keys, grad_vals]).astype(jnp.bfloat16)
    grad_qkv = jnp.stack([jnp.dot(first_in.T, grad_proj[index], preferred_element_type=jnp.float32) for index in range(3)])
    inner_size = HW // N_TENSOR
    left_groups = grad_proj.astype(jnp.float32).reshape(3, row_total, N_TENSOR, inner_size)
    right_groups = w_qkv.astype(jnp.float32).reshape(3, D, N_TENSOR, inner_size)
    grad_first = lax.optimization_barrier(jnp.sum(rounded(jnp.einsum('irtk,idtk->trd', left_groups, right_groups)), axis=0))
    gain_one = lax.optimization_barrier(jnp.sum(grad_first * normed_one, axis=0))
    shift_one = lax.optimization_barrier(jnp.sum(grad_first, axis=0))
    grad_tokens = grad_hidden + norm_back(grad_first, normed_one, spread_one, norm_gains[0])
    grads = (jnp.stack([gain_one, gain_two]), jnp.stack([shift_one, shift_out, shift_two, shift_fc2]), grad_qkv, grad_head, grad_wout, grad_fc1, grad_fc1_bias, grad_fc2)
    return (output, grad_tokens, grads)

def reference(tokens, norm_gains, row_biases, w_qkv, head_bias, w_out, w_fc1, fc1_bias, w_fc2, cotangent):
    group_rows = IMG_DEV * N_TENSOR * SEQ
    token_groups = tokens.reshape(N_DP, group_rows, D)
    cot_groups = cotangent.reshape(N_DP, group_rows, D)
    zeros_init = (jnp.zeros((2, D), jnp.float32), jnp.zeros((4, D), jnp.float32), jnp.zeros((3, D, HW), jnp.float32), jnp.zeros((2, HW), jnp.float32), jnp.zeros((HW, D), jnp.float32), jnp.zeros((D, FF), jnp.float32), jnp.zeros((FF,), jnp.float32), jnp.zeros((FF, D), jnp.float32))

    def group_step(totals, inputs):
        inputs_in, cot_in = inputs
        output, grad_tokens, grads = group_pass(inputs_in, cot_in, norm_gains, row_biases, w_qkv, head_bias, w_out, w_fc1, fc1_bias, w_fc2)
        totals = jax.tree.map(lambda total_one, extra_one: total_one + extra_one, totals, grads)
        return (totals, (output, grad_tokens))
    totals, (outputs, grad_ins) = lax.scan(group_step, zeros_init, (token_groups, cot_groups))
    return (outputs.reshape(TOKENS, D), grad_ins.reshape(TOKENS, D), totals[0], totals[1], totals[2], totals[3], totals[4], totals[5], totals[6], totals[7])
```

```python
import functools

import jax
import jax.numpy as jnp
from jax import lax
from jax.experimental import pallas as pl
from jax.experimental.pallas import tpu as pltpu
from jax.sharding import PartitionSpec as P

HD = 72
SEQ = 256
EPS = 1e-06
F32 = jnp.float32
BF16 = jnp.bfloat16
AXES = ("dp", "tensor")


def norm_rows(values, gain_row, shifts):
    center = values - jnp.mean(values, axis=-1, keepdims=True)
    spread = lax.rsqrt(jnp.mean(center * center, axis=-1, keepdims=True) + EPS)
    normed = center * spread
    return (normed * gain_row + shifts, normed, spread)


def norm_back(grad_rows, normed, spread, gain_row):
    scaled = grad_rows * gain_row
    return spread * (
        scaled
        - jnp.mean(scaled, axis=-1, keepdims=True)
        - normed * jnp.mean(scaled * normed, axis=-1, keepdims=True)
    )


def gelu_tanh(pre_act):
    return jax.nn.gelu(pre_act, approximate=True)


def dot_nn(a, b):
    return lax.dot_general(a, b, (((1,), (0,)), ((), ())), preferred_element_type=F32)


def dot_nt(a, b):
    return lax.dot_general(a, b, (((1,), (1,)), ((), ())), preferred_element_type=F32)


def dot_tn(a, b):
    return lax.dot_general(a, b, (((0,), (0,)), ((), ())), preferred_element_type=F32)


def attend_kernel(heads, rows_ref, w_ref, bias_ref, qkv_ref, mixed_ref, lse_ref):
    hh = heads * HD
    proj = dot_nn(rows_ref[...], w_ref[:, : 3 * hh])
    query = ((proj[:, :hh] + bias_ref[0:1, :]) * HD ** (-0.5)).astype(BF16)
    keys = proj[:, hh : 2 * hh].astype(BF16)
    vals = (proj[:, 2 * hh :] + bias_ref[1:2, :]).astype(BF16)
    qkv_ref[:, :hh] = query
    qkv_ref[:, hh : 2 * hh] = keys
    qkv_ref[:, 2 * hh :] = vals
    outs = []
    for h in range(heads):
        sl = slice(h * HD, (h + 1) * HD)
        scores = dot_nt(query[:, sl], keys[:, sl])
        top = jnp.max(scores, axis=-1, keepdims=True)
        log_norm = top + jnp.log(jnp.sum(jnp.exp(scores - top), axis=-1, keepdims=True))
        probs = jnp.exp(scores - log_norm).astype(BF16)
        outs.append(dot_nn(probs, vals[:, sl]).astype(BF16))
        lse_ref[:, h : h + 1] = log_norm
    mixed_ref[...] = jnp.concatenate(outs, axis=1)


def attend(rows, weight, bias):
    total, width = rows.shape
    hh = weight.shape[1] // 4
    heads = hh // HD
    grid = (total // SEQ,)
    flops = 2 * total * width * 3 * hh + 4 * total * SEQ * hh
    return pl.pallas_call(
        functools.partial(attend_kernel, heads),
        grid=grid,
        in_specs=[
            pl.BlockSpec((SEQ, width), lambda i: (i, 0)),
            pl.BlockSpec(weight.shape, lambda i: (0, 0)),
            pl.BlockSpec(bias.shape, lambda i: (0, 0)),
        ],
        out_specs=[
            pl.BlockSpec((SEQ, 3 * hh), lambda i: (i, 0)),
            pl.BlockSpec((SEQ, hh), lambda i: (i, 0)),
            pl.BlockSpec((SEQ, heads), lambda i: (i, 0)),
        ],
        out_shape=[
            jax.ShapeDtypeStruct((total, 3 * hh), BF16),
            jax.ShapeDtypeStruct((total, hh), BF16),
            jax.ShapeDtypeStruct((total, heads), F32),
        ],
        cost_estimate=pl.CostEstimate(
            flops=flops,
            bytes_accessed=2 * (total * (width + 4 * hh) + weight.size),
            transcendentals=2 * total * SEQ * heads,
        ),
        name="attend",
    )(rows, weight, bias)


def attend_back_kernel(
    heads, images, grad_ref, rows_ref, w_ref, qkv_ref, mixed_ref, lse_ref,
    proj_ref, gw_ref, sums_ref, acc,
):
    hh = heads * HD
    step = pl.program_id(0)
    gh = grad_ref[...]
    gmix = dot_nn(gh, w_ref[:, 3 * hh :]).astype(BF16)
    gq, gk, gv = [], [], []
    for h in range(heads):
        sl = slice(h * HD, (h + 1) * HD)
        query = qkv_ref[:, h * HD : (h + 1) * HD]
        keys = qkv_ref[:, hh + h * HD : hh + (h + 1) * HD]
        vals = qkv_ref[:, 2 * hh + h * HD : 2 * hh + (h + 1) * HD]
        gm = gmix[:, sl]
        probs_f = jnp.exp(dot_nt(query, keys) - lse_ref[:, h : h + 1])
        gv.append(dot_tn(probs_f.astype(BF16), gm))
        dprob = dot_nt(gm, vals)
        inner = jnp.sum(probs_f * dprob, axis=-1, keepdims=True)
        dscore = (probs_f * (dprob - inner)).astype(BF16)
        gq.append(dot_nn(dscore, keys) * HD ** (-0.5))
        gk.append(dot_tn(dscore, query))
    grad_q = jnp.concatenate(gq, axis=1)
    grad_v = jnp.concatenate(gv, axis=1)
    sums = jnp.concatenate(
        [jnp.sum(grad_q, axis=0, keepdims=True), jnp.sum(grad_v, axis=0, keepdims=True)], axis=0
    )
    proj = jnp.concatenate(gq + gk + gv, axis=1).astype(BF16)
    proj_ref[...] = proj
    gw_qkv = dot_tn(rows_ref[...], proj)
    gw_out = dot_tn(gh, mixed_ref[...])

    @pl.when(step == 0)
    def _():
        acc[:, : 3 * hh] = gw_qkv
        acc[:, 3 * hh :] = gw_out
        sums_ref[...] = sums

    @pl.when(step > 0)
    def _():
        acc[:, : 3 * hh] += gw_qkv
        acc[:, 3 * hh :] += gw_out
        sums_ref[...] += sums

    @pl.when(step == images - 1)
    def _():
        gw_ref[...] = acc[...].astype(BF16)


def attend_back(grad_rows, rows, weight, qkv, mixed, lse):
    total, width = rows.shape
    hh = weight.shape[1] // 4
    heads = hh // HD
    images = total // SEQ
    flops = 2 * total * width * 5 * hh + 10 * total * SEQ * hh
    return pl.pallas_call(
        functools.partial(attend_back_kernel, heads, images),
        grid=(images,),
        in_specs=[
            pl.BlockSpec((SEQ, width), lambda i: (i, 0)),
            pl.BlockSpec((SEQ, width), lambda i: (i, 0)),
            pl.BlockSpec(weight.shape, lambda i: (0, 0)),
            pl.BlockSpec((SEQ, 3 * hh), lambda i: (i, 0)),
            pl.BlockSpec((SEQ, hh), lambda i: (i, 0)),
            pl.BlockSpec((SEQ, heads), lambda i: (i, 0)),
        ],
        out_specs=[
            pl.BlockSpec((SEQ, 3 * hh), lambda i: (i, 0)),
            pl.BlockSpec(weight.shape, lambda i: (0, 0)),
            pl.BlockSpec((2, hh), lambda i: (0, 0)),
        ],
        out_shape=[
            jax.ShapeDtypeStruct((total, 3 * hh), BF16),
            jax.ShapeDtypeStruct(weight.shape, BF16),
            jax.ShapeDtypeStruct((2, hh), F32),
        ],
        scratch_shapes=[pltpu.VMEM(weight.shape, F32)],
        cost_estimate=pl.CostEstimate(
            flops=flops,
            bytes_accessed=2 * (2 * total * width + 7 * total * hh + 2 * weight.size),
            transcendentals=total * SEQ * heads,
        ),
        name="attend_back",
    )(grad_rows, rows, weight, qkv, mixed, lse)


def sum_nt_kernel(count, low, high, *refs):
    lefts, rights, out_ref = refs[:count], refs[count : 2 * count], refs[2 * count]
    total = dot_nt(lefts[0][...], rights[0][:, low:high])
    for left, right in zip(lefts[1:], rights[1:]):
        total += dot_nt(left[...], right[:, low:high])
    out_ref[...] = total.astype(BF16)


def sum_nt(lefts, rights, low, high):
    count = len(lefts)
    total, inner = lefts[0].shape
    width = rights[0].shape[0]
    return pl.pallas_call(
        functools.partial(sum_nt_kernel, count, low, high),
        grid=(total // SEQ,),
        in_specs=[pl.BlockSpec((SEQ, inner), lambda i: (i, 0))] * count
        + [pl.BlockSpec(rights[0].shape, lambda i: (0, 0))] * count,
        out_specs=pl.BlockSpec((SEQ, width), lambda i: (i, 0)),
        out_shape=jax.ShapeDtypeStruct((total, width), BF16),
        cost_estimate=pl.CostEstimate(
            flops=2 * total * inner * width * count,
            bytes_accessed=2 * (count * (total * inner + rights[0].size) + total * width),
            transcendentals=0,
        ),
        name="sum_nt",
    )(*lefts, *rights)


def make_body(ndp, nt):
    nz = ndp // 2
    bits = nt.bit_length() - 1
    top = nt // 2
    low = nt // 2

    def perm(move):
        pairs = []
        for d in range(ndp):
            for t in range(nt):
                d2, t2 = move(d, t)
                pairs.append((d * nt + t, d2 * nt + t2))
        return pairs

    def send(value, move):
        return lax.ppermute(value, AXES, perm(move))

    def swap_core(value):
        return send(value, lambda d, t: (d ^ 1, t))

    def swap_tensor(value, i):
        return send(value, lambda d, t: (d, t ^ i))

    def shift_z(value, k):
        return send(value, lambda d, t: ((d + 2 * k) % ndp, t))

    def stage(value, i):
        return send(
            value, lambda d, t: (d, t ^ ((1 << i) if d % 2 == 0 else (1 << (bits - 1 - i))))
        )

    def reverse_bits(p):
        return sum(((p >> i) & 1) << (bits - 1 - i) for i in range(bits))

    def swap_top(value):
        return send(value, lambda d, t: (d, t if d % 2 == 0 else t ^ top))

    def gather_z(value, z):
        out = jnp.zeros((nz,) + value.shape, value.dtype)
        out = lax.dynamic_update_slice_in_dim(out, value[None], z, 0)
        for k in range(1, nz):
            got = shift_z(value, k)
            out = lax.dynamic_update_slice_in_dim(out, got[None], lax.rem(z - k + nz, nz), 0)
        return out

    def scatter_z(value, z):
        total = lax.dynamic_index_in_dim(value, z, 0, keepdims=False).astype(F32)
        for k in range(1, nz):
            piece = lax.dynamic_index_in_dim(value, lax.rem(z + k, nz), 0, keepdims=False)
            total += shift_z(piece, k).astype(F32)
        return total

    def pick(selector, items):
        total = jnp.where(selector == 0, items[0], 0)
        for i in range(1, len(items)):
            total = total + jnp.where(selector == i, items[i], 0)
        return total

    def body(
        tokens, norm_gains, row_biases, w_qkv, head_bias, w_out, w_fc1, fc1_bias, w_fc2, cotangent
    ):
        d = lax.axis_index("dp")
        t = lax.axis_index("tensor")
        z, c = d // 2, d % 2
        core0 = c == 0
        rows, width = tokens.shape
        block = w_qkv.shape[2]
        hh = block // 2
        part = w_qkv.shape[1]
        ff = w_fc1.shape[1]

        def by_core(zero, one):
            return jnp.where(core0, zero, one)

        w_out_t = w_out.T

        def half(h):
            sl = slice(h * hh, (h + 1) * hh)
            return jnp.concatenate(
                [w_qkv[0][:, sl], w_qkv[1][:, sl], w_qkv[2][:, sl], w_out_t[:, sl]], axis=1
            )

        first_half, second_half = half(0), half(1)
        kept = by_core(first_half, second_half)
        got = swap_core(by_core(second_half, first_half))
        shard = jnp.stack([by_core(kept, got), by_core(got, kept)])
        blocks = [gather_z(shard, z)]
        for i in range(bits):
            blocks = blocks + [stage(b, i) for b in blocks]
        attn_w = [b.reshape(width, 4 * hh) for b in blocks]

        gain_count, shift_count = norm_gains.shape[0], row_biases.shape[0]
        vec_count = gain_count + shift_count
        piece = norm_gains.shape[1]
        small = jnp.concatenate(
            [norm_gains.reshape(-1), row_biases.reshape(-1), head_bias.reshape(-1), fc1_bias]
        )
        smalls = [small] + [swap_tensor(small, i) for i in range(1, nt)]
        vec_size = vec_count * piece
        vecs = jnp.stack(
            [pick(t ^ i, [s[:vec_size] for s in smalls]) for i in range(nt)]
        )
        vecs = gather_z(vecs, z)
        vecs_other = swap_core(vecs)
        vecs = jnp.stack([by_core(vecs, vecs_other), by_core(vecs_other, vecs)], axis=1)
        vecs = vecs.reshape(nz * 2 * nt, vec_count, piece).transpose(1, 0, 2)
        vecs = vecs.reshape(vec_count, width)
        gain_rows, shifts = vecs[:gain_count], vecs[gain_count:]
        head_biases = [s[vec_size : vec_size + 2 * block].reshape(2, block) for s in smalls]
        unit_bias = []
        for p in range(nt):
            full = by_core(head_biases[p], head_biases[reverse_bits(p)])
            unit_bias.append(by_core(full[:, :hh], full[:, hh:]))
        ff_bias = by_core(smalls[0][vec_size + 2 * block :], smalls[top][vec_size + 2 * block :])

        def gather_ff(own):
            mine = gather_z(own, z)
            other = swap_core(mine)
            full = jnp.stack([by_core(mine, other), by_core(other, mine)], axis=1)
            return swap_top(full.reshape(width, ff))

        fc1 = gather_ff(w_fc1)
        fc2_t = gather_ff(w_fc2.T)

        inputs_f = tokens.astype(F32)
        first_f, normed_one, spread_one = norm_rows(inputs_f, gain_rows[0], shifts[0])
        first = first_f.astype(BF16)
        first_chip = jnp.concatenate([first, swap_core(first)], axis=0)

        def gather_rows(own):
            got = [own] + [swap_tensor(own, i) for i in range(1, low)]
            return jnp.concatenate(got + [swap_core(g) for g in got], axis=0)

        cot_rows = gather_rows(cotangent)

        saved = [attend(first_chip, attn_w[p], unit_bias[p]) for p in range(nt)]
        mixed = [s[1] for s in saved]
        attn_part = sum_nt(mixed, attn_w, 3 * hh, 4 * hh)
        attention = attn_part[:rows].astype(F32) + swap_core(attn_part[rows:]).astype(F32)
        hidden_one = inputs_f + attention + shifts[1]
        second_f, normed_two, spread_two = norm_rows(hidden_one, gain_rows[1], shifts[2])

        second_rows = gather_rows(second_f.astype(BF16))
        pre_act = dot_nn(second_rows, fc1) + ff_bias
        act_out, gelu_back = jax.vjp(gelu_tanh, pre_act)
        act_in = act_out.astype(BF16)
        grad_act = dot_nn(cot_rows, fc2_t)
        grad_pre = gelu_back(grad_act)[0]
        grad_fc1_bias = jnp.sum(grad_pre, axis=0)
        grad_pre_in = grad_pre.astype(BF16)

        def scatter_rows(partial):
            mine = partial[: low * rows].astype(F32) + swap_core(partial[low * rows :]).astype(F32)
            total = mine[:rows]
            for i in range(1, low):
                total += swap_tensor(mine[i * rows : (i + 1) * rows].astype(BF16), i).astype(F32)
            return total

        grad_second = scatter_rows(dot_nt(grad_pre_in, fc1).astype(BF16))
        mlp_out = scatter_rows(dot_nt(act_in, fc2_t).astype(BF16))
        output = hidden_one + mlp_out + shifts[3]
        grad_fc2_t = dot_tn(cot_rows, act_in).astype(BF16)
        grad_fc1 = dot_tn(second_rows, grad_pre_in).astype(BF16)

        def scatter_ff(partial):
            full = swap_top(partial).reshape(nz, 2, part, ff)
            other = by_core(full[:, 1], full[:, 0])
            mine = by_core(full[:, 0], full[:, 1])
            mine = (mine.astype(F32) + swap_core(other).astype(F32)).astype(BF16)
            return scatter_z(mine, z)

        grad_fc2_own = scatter_ff(grad_fc2_t).T
        grad_fc1_own = scatter_ff(grad_fc1)

        cot_f = cotangent.astype(F32)
        gain_two = jnp.sum(grad_second * normed_two, axis=0)
        shift_two = jnp.sum(grad_second, axis=0)
        grad_hidden = cot_f + norm_back(grad_second, normed_two, spread_two, gain_rows[1])
        shift_out = jnp.sum(grad_hidden, axis=0)
        shift_fc2 = jnp.sum(cot_f, axis=0)
        hidden_in = grad_hidden.astype(BF16)
        hidden_chip = jnp.concatenate([hidden_in, swap_core(hidden_in)], axis=0)
        order = list(range(nt - 1, -1, -1))
        back = {
            p: attend_back(hidden_chip, first_chip, attn_w[p], saved[p][0], mixed[p], saved[p][2])
            for p in order
        }
        grad_w = [back[p][1] for p in range(nt)]
        for i in reversed(range(bits)):
            span = 1 << i
            got = [stage(g, i) for g in grad_w[span:]]
            grad_w = [
                (a.astype(F32) + b.astype(F32)).astype(BF16) for a, b in zip(grad_w[:span], got)
            ]
        own_half = scatter_z(grad_w[0].reshape(nz, 2 * part, 4 * hh), z)
        own_half = own_half.reshape(2, part, 4 * hh)
        kept = by_core(own_half[0], own_half[1])
        got = swap_core(by_core(own_half[1], own_half[0]).astype(BF16)).astype(F32)
        halves = [by_core(kept, got), by_core(got, kept)]
        grad_qkv_own = jnp.stack(
            [
                jnp.concatenate([g[:, k * hh : (k + 1) * hh] for g in halves], axis=1)
                for k in range(3)
            ]
        )
        grad_out_own = jnp.concatenate([g[:, 3 * hh :] for g in halves], axis=1).T

        first_part = sum_nt([back[p][0] for p in range(nt)], attn_w, 0, 3 * hh)
        grad_first = first_part[:rows].astype(F32) + swap_core(first_part[rows:]).astype(F32)
        gain_one = jnp.sum(grad_first * normed_one, axis=0)
        shift_one = jnp.sum(grad_first, axis=0)
        grad_tokens = grad_hidden + norm_back(grad_first, normed_one, spread_one, gain_rows[0])

        zero_half = jnp.zeros((2, hh), F32)
        unit_sums = []
        for p in range(nt):
            sums = back[p][2]
            unit_sums.append(
                jnp.concatenate(
                    [by_core(sums, zero_half), by_core(zero_half, sums)], axis=1
                ).reshape(-1)
            )
        head_rel = [by_core(unit_sums[j], unit_sums[reverse_bits(j)]) for j in range(nt)]
        head_all = jnp.stack([pick(t ^ i, head_rel) for i in range(nt)])
        ff_block = by_core(t, t ^ top)
        bias_all = jnp.stack([jnp.where(ff_block == i, grad_fc1_bias, 0) for i in range(nt)])
        vec_all = jnp.stack([gain_one, gain_two, shift_one, shift_out, shift_two, shift_fc2])
        total = jnp.concatenate([vec_all.reshape(-1), head_all.reshape(-1), bias_all.reshape(-1)])
        total = functools.reduce(
            jnp.add, [swap_tensor(total, i) for i in range(1, nt)], total
        )
        total = functools.reduce(jnp.add, [shift_z(total, k) for k in range(1, nz)], total)
        total = total + swap_core(total)
        vec_total = total[: vec_count * width].reshape(vec_count, width)
        own = lax.dynamic_slice_in_dim(vec_total, (d * nt + t) * piece, piece, axis=1)
        rest = total[vec_count * width :]
        head_total = lax.dynamic_index_in_dim(
            rest[: nt * 2 * block].reshape(nt, 2, block), t, 0, keepdims=False
        )
        bias_total = lax.dynamic_index_in_dim(
            rest[nt * 2 * block :].reshape(nt, ff), t, 0, keepdims=False
        )
        return (
            output,
            grad_tokens,
            own[:gain_count],
            own[gain_count:],
            grad_qkv_own,
            head_total,
            grad_out_own,
            grad_fc1_own,
            bias_total,
            grad_fc2_own,
        )

    return body


def solution(mesh):
    in_specs = (
        P(("dp", "tensor"), None),
        P(None, ("dp", "tensor")),
        P(None, ("dp", "tensor")),
        P(None, "dp", "tensor"),
        P(None, "tensor"),
        P("tensor", "dp"),
        P("dp", "tensor"),
        P("tensor"),
        P("tensor", "dp"),
        P(("dp", "tensor"), None),
    )
    out_specs = (
        P(("dp", "tensor"), None),
        P(("dp", "tensor"), None),
        P(None, ("dp", "tensor")),
        P(None, ("dp", "tensor")),
        P(None, "dp", "tensor"),
        P(None, "tensor"),
        P("tensor", "dp"),
        P("dp", "tensor"),
        P("tensor"),
        P("tensor", "dp"),
    )
    body = make_body(mesh.shape["dp"], mesh.shape["tensor"])
    return jax.shard_map(body, mesh=mesh, in_specs=in_specs, out_specs=out_specs, check_vma=False)
```

```python
import functools

import jax
import jax.numpy as jnp
from jax import lax
from jax.experimental import pallas as pl
from jax.experimental.pallas import tpu as pltpu
from jax.sharding import PartitionSpec as P


HD = 72
SEQ = 256
EPS = 1e-06
F32 = jnp.float32
BF16 = jnp.bfloat16
AXES = ("dp", "tensor")


def norm_rows(values, gain_row, shifts):
    center = values - jnp.mean(values, axis=-1, keepdims=True)
    spread = lax.rsqrt(jnp.mean(center * center, axis=-1, keepdims=True) + EPS)
    normed = center * spread
    return (normed * gain_row + shifts, normed, spread)


def norm_back(grad_rows, normed, spread, gain_row):
    scaled = grad_rows * gain_row
    return spread * (
        scaled
        - jnp.mean(scaled, axis=-1, keepdims=True)
        - normed * jnp.mean(scaled * normed, axis=-1, keepdims=True)
    )


def tie(value, *others):
    return lax.optimization_barrier((value, *others))[0]


def dot_nn(a, b):
    return lax.dot_general(a, b, (((1,), (0,)), ((), ())), preferred_element_type=F32)


def dot_nt(a, b):
    return lax.dot_general(a, b, (((1,), (1,)), ((), ())), preferred_element_type=F32)


def dot_tn(a, b):
    return lax.dot_general(a, b, (((0,), (0,)), ((), ())), preferred_element_type=F32)


LANES = 128


def padded(size):
    return -(-size // LANES) * LANES


def segments(heads):
    return [
        (kind * heads * HD + h * HD, (kind * heads + h) * LANES)
        for kind in range(4)
        for h in range(heads)
    ]


def attend_kernel(heads, images, rows_ref, w_ref, bias_ref, qkv_ref, mixed_ref, lse_ref, wide_ref):
    hp = heads * LANES

    @pl.when(pl.program_id(0) == 0)
    def _():
        lane = lax.broadcasted_iota(jnp.int32, (1, LANES), 1)
        for src, dst in segments(heads):
            piece = w_ref[:, src : src + LANES]
            wide_ref[:, dst : dst + LANES] = jnp.where(lane < HD, piece, jnp.zeros_like(piece))

    proj = dot_nn(rows_ref[...], wide_ref[:, : 3 * hp])
    query = ((proj[:, :hp] + bias_ref[0:1, :]) * HD ** (-0.5)).astype(BF16)
    keys = proj[:, hp : 2 * hp].astype(BF16)
    vals = (proj[:, 2 * hp :] + bias_ref[1:2, :]).astype(BF16)
    qkv_ref[:, :hp] = query
    qkv_ref[:, hp : 2 * hp] = keys
    qkv_ref[:, 2 * hp :] = vals
    units = [(m, h) for m in range(images) for h in range(heads)]

    def cut(array, m, h):
        return array[m * SEQ : (m + 1) * SEQ, h * LANES : (h + 1) * LANES]

    scores = [dot_nt(cut(query, m, h), cut(keys, m, h)) for m, h in units]
    tops = [jnp.max(s, axis=-1, keepdims=True) for s in scores]
    exps = [jnp.exp(s - top) for s, top in zip(scores, tops)]
    sums = [jnp.sum(e, axis=-1, keepdims=True) for e in exps]
    probs = [(e * (1.0 / total)).astype(BF16) for e, total in zip(exps, sums)]
    for (m, h), p, top, total in zip(units, probs, tops, sums):
        rows = slice(m * SEQ, (m + 1) * SEQ)
        mixed_ref[rows, h * LANES : (h + 1) * LANES] = dot_nn(p, cut(vals, m, h)).astype(BF16)
        lse_ref[rows, h : h + 1] = top + jnp.log(total)


def attend(rows, weight, bias, images=2):
    total, width = rows.shape
    heads = bias.shape[1] // LANES
    hp = heads * LANES
    tile = images * SEQ
    return pl.pallas_call(
        functools.partial(attend_kernel, heads, images),
        grid=(total // tile,),
        in_specs=[
            pl.BlockSpec((tile, width), lambda i: (i, 0)),
            pl.BlockSpec(weight.shape, lambda i: (0, 0)),
            pl.BlockSpec(bias.shape, lambda i: (0, 0)),
        ],
        out_specs=[
            pl.BlockSpec((tile, 3 * hp), lambda i: (i, 0)),
            pl.BlockSpec((tile, hp), lambda i: (i, 0)),
            pl.BlockSpec((tile, heads), lambda i: (i, 0)),
            pl.BlockSpec((width, 4 * hp), lambda i: (0, 0)),
        ],
        out_shape=[
            jax.ShapeDtypeStruct((total, 3 * hp), BF16),
            jax.ShapeDtypeStruct((total, hp), BF16),
            jax.ShapeDtypeStruct((total, heads), F32),
            jax.ShapeDtypeStruct((width, 4 * hp), BF16),
        ],
        cost_estimate=pl.CostEstimate(
            flops=2 * total * width * 3 * hp + 4 * total * SEQ * hp,
            bytes_accessed=2 * (total * (width + 4 * hp) + 2 * weight.size),
            transcendentals=total * SEQ * heads,
        ),
        compiler_params=pltpu.CompilerParams(vmem_limit_bytes=24 << 20),
        name="attend",
    )(rows, weight, bias)


def attend_back_kernel(
    heads, images, grad_ref, rows_ref, wide_ref, qkv_ref, mixed_ref, lse_ref,
    proj_ref, gw_ref, sums_ref, acc,
):
    hp = heads * LANES
    step = pl.program_id(0)
    gh = grad_ref[...]
    gmix = dot_nn(gh, wide_ref[...]).astype(BF16)
    units = [(m, h) for m in range(images) for h in range(heads)]

    def cut(array, m, h, kind=0):
        lo = (kind * heads + h) * LANES
        return array[m * SEQ : (m + 1) * SEQ, lo : lo + LANES]

    query = [cut(qkv_ref, m, h, 0) for m, h in units]
    keys = [cut(qkv_ref, m, h, 1) for m, h in units]
    vals = [cut(qkv_ref, m, h, 2) for m, h in units]
    gm = [cut(gmix, m, h) for m, h in units]
    lse = [lse_ref[m * SEQ : (m + 1) * SEQ, h : h + 1] for m, h in units]
    probs = [jnp.exp(dot_nt(q, k) - top) for q, k, top in zip(query, keys, lse)]
    dprobs = [dot_nt(g, v) for g, v in zip(gm, vals)]
    dots = [jnp.sum(p * dp, axis=-1, keepdims=True) for p, dp in zip(probs, dprobs)]
    dscores = [(p * (dp - dt)).astype(BF16) for p, dp, dt in zip(probs, dprobs, dots)]
    sums = [[None] * heads for _ in range(2)]
    for n, (m, h) in enumerate(units):
        rows = slice(m * SEQ, (m + 1) * SEQ)
        grad_v = dot_tn(probs[n].astype(BF16), gm[n])
        grad_q = dot_nn(dscores[n], keys[n]) * HD ** (-0.5)
        grad_k = dot_tn(dscores[n], query[n])
        for kind, value in enumerate((grad_q, grad_k, grad_v)):
            lo = (kind * heads + h) * LANES
            proj_ref[rows, lo : lo + LANES] = value.astype(BF16)
        for kind, value in enumerate((grad_q, grad_v)):
            column = jnp.sum(value, axis=0, keepdims=True)
            sums[kind][h] = column if sums[kind][h] is None else sums[kind][h] + column
    sums = jnp.concatenate([jnp.concatenate(s, axis=1) for s in sums], axis=0)
    gw_qkv = dot_tn(rows_ref[...], proj_ref[...])
    gw_out = dot_tn(gh, mixed_ref[...])

    @pl.when(step == 0)
    def _():
        acc[:, : 3 * hp] = gw_qkv
        acc[:, 3 * hp :] = gw_out
        sums_ref[...] = sums

    @pl.when(step > 0)
    def _():
        acc[:, : 3 * hp] += gw_qkv
        acc[:, 3 * hp :] += gw_out
        sums_ref[...] += sums

    @pl.when(step == pl.num_programs(0) - 1)
    def _():
        gw_ref[...] = jnp.zeros_like(gw_ref)
        for dst, src in segments(heads):
            gw_ref[:, dst : dst + HD] = acc[:, src : src + HD].astype(BF16)


def attend_back(grad_rows, rows, wide, qkv, mixed, lse, packed, images=2):
    total, width = rows.shape
    heads = lse.shape[1]
    hp = heads * LANES
    tile = images * SEQ
    return pl.pallas_call(
        functools.partial(attend_back_kernel, heads, images),
        grid=(total // tile,),
        in_specs=[
            pl.BlockSpec((tile, width), lambda i: (i, 0)),
            pl.BlockSpec((tile, width), lambda i: (i, 0)),
            pl.BlockSpec((width, hp), lambda i: (0, 3)),
            pl.BlockSpec((tile, 3 * hp), lambda i: (i, 0)),
            pl.BlockSpec((tile, hp), lambda i: (i, 0)),
            pl.BlockSpec((tile, heads), lambda i: (i, 0)),
        ],
        out_specs=[
            pl.BlockSpec((tile, 3 * hp), lambda i: (i, 0)),
            pl.BlockSpec((width, packed), lambda i: (0, 0)),
            pl.BlockSpec((2, hp), lambda i: (0, 0)),
        ],
        out_shape=[
            jax.ShapeDtypeStruct((total, 3 * hp), BF16),
            jax.ShapeDtypeStruct((width, packed), BF16),
            jax.ShapeDtypeStruct((2, hp), F32),
        ],
        scratch_shapes=[pltpu.VMEM((width, 4 * hp), F32)],
        cost_estimate=pl.CostEstimate(
            flops=2 * total * width * 5 * hp + 10 * total * SEQ * hp,
            bytes_accessed=2 * (2 * total * width + 7 * total * hp + width * (hp + packed)),
            transcendentals=total * SEQ * heads,
        ),
        compiler_params=pltpu.CompilerParams(vmem_limit_bytes=30 << 20),
        name="attend_back",
    )(grad_rows, rows, wide, qkv, mixed, lse)


def sum_nt_kernel(count, half_steps, *refs):
    lefts, rights = refs[:count], refs[count : 2 * count]
    mine_ref, other_ref = refs[2 * count :]
    total = dot_nt(lefts[0][...], rights[0][...])
    for left, right in zip(lefts[1:], rights[1:]):
        total += dot_nt(left[...], right[...])
    value = total.astype(BF16)
    step = pl.program_id(0)

    @pl.when(step < half_steps)
    def _():
        other_ref[...] = value

    @pl.when(step >= half_steps)
    def _():
        mine_ref[...] = value


def sum_nt(lefts, rights, column, tile=SEQ):
    count = len(lefts)
    total, inner = lefts[0].shape
    width = rights[0].shape[0]
    half = total // 2 // tile
    return pl.pallas_call(
        functools.partial(sum_nt_kernel, count, half),
        grid=(2 * half,),
        in_specs=[pl.BlockSpec((tile, inner), lambda i: (lax.rem(i + half, 2 * half), 0))] * count
        + [
            pl.BlockSpec((width, inner), lambda i: (0, column), pipeline_mode=pl.Buffered(1))
        ]
        * count,
        out_specs=[
            pl.BlockSpec((tile, width), lambda i: (jnp.maximum(i - half, 0), 0)),
            pl.BlockSpec((tile, width), lambda i: (jnp.minimum(i, half - 1), 0)),
        ],
        out_shape=[jax.ShapeDtypeStruct((total // 2, width), BF16)] * 2,
        cost_estimate=pl.CostEstimate(
            flops=2 * total * inner * width * count,
            bytes_accessed=2 * (count * (total + width) * inner + total * width),
            transcendentals=0,
        ),
        compiler_params=pltpu.CompilerParams(vmem_limit_bytes=24 << 20),
        name="sum_nt",
    )(*lefts, *rights)


def fetch_weights(core_ref, own, got, kept, sems):
    def fetch(sources):
        copies = [
            pltpu.make_async_copy(source, target, sems.at[i])
            for i, (source, target) in enumerate(zip(sources, kept))
        ]
        for copy in copies:
            copy.start()
        for copy in copies:
            copy.wait()

    @pl.when(core_ref[0] == 0)
    def _():
        fetch(own)

    @pl.when(core_ref[0] != 0)
    def _():
        fetch(got)


def feed_in_kernel(
    half, core_ref, rows0, rows1, w1_own, w1_got, bias_ref, rows_ref, act_ref, slope_ref, w1, sems
):
    step = pl.program_id(0)

    @pl.when(step == 0)
    def _():
        fetch_weights(core_ref, [w1_own], [w1_got], [w1], sems)

    rows = jnp.where(step < half, rows0[...], rows1[...])
    rows_ref[...] = rows
    pre = dot_nn(rows, w1[...]) + bias_ref[...]
    root = (2.0 / jnp.pi) ** 0.5
    square = pre * pre
    tanh = jnp.tanh(root * (pre + 0.044715 * (pre * square)))
    gate = 0.5 * (1.0 + tanh)
    slope = gate + 0.5 * pre * (1.0 - tanh * tanh) * (root * (1.0 + 3 * 0.044715 * square))
    act_ref[...] = (pre * gate).astype(BF16)
    slope_ref[...] = slope.astype(BF16)


def feed_in(core, rows, weights, bias, tile=SEQ):
    count, width = rows[0].shape
    ff = weights[0].shape[1]
    half = count // tile
    step = lambda i: (i, 0)
    anywhere = pl.BlockSpec(memory_space=pl.ANY)
    return pl.pallas_call(
        functools.partial(feed_in_kernel, half),
        grid=(2 * half,),
        in_specs=[
            pl.BlockSpec(memory_space=pltpu.SMEM),
            pl.BlockSpec((tile, width), lambda i: (jnp.minimum(i, half - 1), 0)),
            pl.BlockSpec((tile, width), lambda i: (jnp.maximum(i - half, 0), 0)),
            anywhere,
            anywhere,
            pl.BlockSpec((1, ff), lambda i: (0, 0)),
        ],
        out_specs=[
            pl.BlockSpec((tile, width), step),
            pl.BlockSpec((tile, ff), step),
            pl.BlockSpec((tile, ff), step),
        ],
        out_shape=[
            jax.ShapeDtypeStruct((2 * count, width), BF16),
            jax.ShapeDtypeStruct((2 * count, ff), BF16),
            jax.ShapeDtypeStruct((2 * count, ff), BF16),
        ],
        scratch_shapes=[pltpu.VMEM((width, ff), BF16), pltpu.SemaphoreType.DMA((1,))],
        compiler_params=pltpu.CompilerParams(vmem_limit_bytes=24 << 20),
        cost_estimate=pl.CostEstimate(
            flops=4 * count * width * ff,
            bytes_accessed=2 * (width * ff + 4 * count * (width + ff)),
            transcendentals=2 * count * ff,
        ),
        name="feed_in",
    )(core, *rows, *weights, bias)


def feed_out_kernel(
    half, core_ref, cot0, cot1, act_ref, slope_ref, w1_own, w1_got, w2_own, w2_got,
    gpre_ref, out0, out1, grad0, grad1, sums_ref, w1, w2, sems,
):
    step = pl.program_id(0)

    @pl.when(step == 0)
    def _():
        fetch_weights(core_ref, [w1_own, w2_own], [w1_got, w2_got], [w1, w2], sems)

    first = step < half
    cot = jnp.where(first, cot0[...], cot1[...])
    grad_pre = dot_nn(cot, w2[...]) * slope_ref[...].astype(F32)
    sums = jnp.sum(grad_pre, axis=0, keepdims=True)
    grad_in = grad_pre.astype(BF16)
    gpre_ref[...] = grad_in
    grad = dot_nt(grad_in, w1[...]).astype(BF16)
    out = dot_nt(act_ref[...], w2[...]).astype(BF16)

    @pl.when(step == 0)
    def _():
        sums_ref[...] = sums

    @pl.when(step > 0)
    def _():
        sums_ref[...] += sums

    @pl.when(first)
    def _():
        out0[...] = out
        grad0[...] = grad

    @pl.when(jnp.logical_not(first))
    def _():
        out1[...] = out
        grad1[...] = grad


def feed_out(core, cots, act, slope, weights, tile=SEQ):
    count, width = cots[0].shape
    ff = act.shape[1]
    half = count // tile
    low = lambda i: (jnp.minimum(i, half - 1), 0)
    high = lambda i: (jnp.maximum(i - half, 0), 0)
    step = lambda i: (i, 0)
    anywhere = pl.BlockSpec(memory_space=pl.ANY)
    return pl.pallas_call(
        functools.partial(feed_out_kernel, half),
        grid=(2 * half,),
        in_specs=[
            pl.BlockSpec(memory_space=pltpu.SMEM),
            pl.BlockSpec((tile, width), low),
            pl.BlockSpec((tile, width), high),
            pl.BlockSpec((tile, ff), step),
            pl.BlockSpec((tile, ff), step),
        ]
        + [anywhere] * 4,
        out_specs=[
            pl.BlockSpec((tile, ff), step),
            pl.BlockSpec((tile, width), low),
            pl.BlockSpec((tile, width), high),
            pl.BlockSpec((tile, width), low),
            pl.BlockSpec((tile, width), high),
            pl.BlockSpec((1, ff), lambda i: (0, 0)),
        ],
        out_shape=[jax.ShapeDtypeStruct((2 * count, ff), BF16)]
        + [jax.ShapeDtypeStruct((count, width), BF16)] * 4
        + [jax.ShapeDtypeStruct((1, ff), F32)],
        scratch_shapes=[
            pltpu.VMEM((width, ff), BF16),
            pltpu.VMEM((width, ff), BF16),
            pltpu.SemaphoreType.DMA((2,)),
        ],
        compiler_params=pltpu.CompilerParams(vmem_limit_bytes=30 << 20),
        cost_estimate=pl.CostEstimate(
            flops=12 * count * width * ff,
            bytes_accessed=2 * (2 * width * ff + 2 * count * (3 * width + 3 * ff)),
            transcendentals=0,
        ),
        name="feed_out",
    )(core, *cots, act, slope, *weights)


def pack_kernel(count, where_ref, *refs):
    out_ref = refs[-1]
    vectors, units, bias_ref = refs[:count], refs[count:-2], refs[-2]
    out_ref[...] = jnp.zeros_like(out_ref)
    for i, vector in enumerate(vectors):
        out_ref[0, i : i + 1, : vector.shape[1]] = vector[...]
    core = where_ref[0]
    for n, unit in enumerate(units):
        hp = unit.shape[1]
        spot = 1 + where_ref[2 + n]

        @pl.when(core == 0)
        def _():
            out_ref[spot, 1:3, :hp] = unit[...]

        @pl.when(core != 0)
        def _():
            out_ref[spot, 3:5, :hp] = unit[...]

    out_ref[1 + where_ref[1], 0:1, : bias_ref.shape[1]] = bias_ref[...]


def pack_small(where, vectors, units, bias, spots):
    lanes = max(x.shape[1] for x in [*vectors, *units, bias])
    return pl.pallas_call(
        functools.partial(pack_kernel, len(vectors)),
        in_specs=[pl.BlockSpec(memory_space=pltpu.SMEM)]
        + [pl.BlockSpec(memory_space=pltpu.VMEM)] * (len(vectors) + len(units) + 1),
        out_specs=pl.BlockSpec(memory_space=pltpu.VMEM),
        out_shape=jax.ShapeDtypeStruct((1 + spots, 8, lanes), F32),
        name="pack_small",
    )(where, *vectors, *units, bias)


def make_body(ndp, nt):
    nz = ndp // 2
    bits = nt.bit_length() - 1
    top = nt // 2
    low = nt // 2

    def perm(move):
        pairs = []
        for d in range(ndp):
            for t in range(nt):
                d2, t2 = move(d, t)
                pairs.append((d * nt + t, d2 * nt + t2))
        return pairs

    def send(value, move):
        return lax.ppermute(value, AXES, perm(move))

    def swap_core(value):
        return send(value, lambda d, t: (d ^ 1, t))

    def swap_tensor(value, i):
        return send(value, lambda d, t: (d, t ^ i))

    def shift_z(value, k):
        return send(value, lambda d, t: ((d + 2 * k) % ndp, t))

    def stage(value, i):
        return send(
            value, lambda d, t: (d, t ^ ((1 << i) if d % 2 == 0 else (1 << (bits - 1 - i))))
        )

    def reverse_bits(p):
        return sum(((p >> i) & 1) << (bits - 1 - i) for i in range(bits))

    def swap_top(value):
        pairs = [(d * nt + t, d * nt + (t ^ top)) for d in range(1, ndp, 2) for t in range(nt)]
        return lax.ppermute(value, AXES, pairs)

    def gather_z(value, z):
        out = jnp.zeros((nz,) + value.shape, value.dtype)
        out = lax.dynamic_update_slice_in_dim(out, value[None], z, 0)
        for k in range(1, nz):
            got = shift_z(value, k)
            out = lax.dynamic_update_slice_in_dim(out, got[None], lax.rem(z - k + nz, nz), 0)
        return out

    def pick(selector, items):
        total = jnp.where(selector == 0, items[0], 0)
        for i in range(1, len(items)):
            total = total + jnp.where(selector == i, items[i], 0)
        return total

    def body(
        tokens, norm_gains, row_biases, w_qkv, head_bias, w_out, w_fc1, fc1_bias, w_fc2, cotangent
    ):
        d = lax.axis_index("dp")
        t = lax.axis_index("tensor")
        z, c = d // 2, d % 2
        core0 = c == 0
        _, width = tokens.shape
        block = w_qkv.shape[2]
        hh = block // 2
        part = w_qkv.shape[1]
        ff = w_fc1.shape[1]

        def by_core(zero, one):
            return jnp.where(core0, zero, one)

        w_out_t = w_out.T

        packed = padded(4 * hh)
        heads = hh // HD
        wide = padded(ff)

        def half(h):
            sl = slice(h * hh, (h + 1) * hh)
            cols = [w_qkv[0][:, sl], w_qkv[1][:, sl], w_qkv[2][:, sl], w_out_t[:, sl]]
            return jnp.pad(jnp.concatenate(cols, axis=1), ((0, 0), (0, packed - 4 * hh)))

        gathered = lax.all_gather(jnp.stack([half(0), half(1)]), "dp", axis=1, tiled=True)
        far = range(1, low)
        cot_far = [swap_tensor(cotangent, i) for i in far]
        own_half = lax.dynamic_index_in_dim(gathered, c, 0, keepdims=False)
        attn_w = [tie(own_half, *cot_far)]
        for i in range(bits):
            attn_w = attn_w + [stage(b, i) for b in attn_w]

        def gather_ff(own):
            return lax.all_gather(
                jnp.pad(own, ((0, 0), (0, wide - ff))), "dp", axis=0, tiled=True
            )

        fc1_own, fc2_own = gather_ff(w_fc1), gather_ff(w_fc2.T)

        gain_count, shift_count = norm_gains.shape[0], row_biases.shape[0]
        vec_count = gain_count + shift_count
        piece = norm_gains.shape[1]
        small = jnp.concatenate(
            [norm_gains.reshape(-1), row_biases.reshape(-1), head_bias.reshape(-1), fc1_bias]
        )
        smalls = [small] + [swap_tensor(small, i) for i in range(1, nt)]
        vec_size = vec_count * piece
        vecs = jnp.stack([pick(t ^ i, [s[:vec_size] for s in smalls]) for i in range(nt)])
        vecs = gather_z(vecs, z)
        vecs_other = swap_core(vecs)
        vecs = jnp.stack([by_core(vecs, vecs_other), by_core(vecs_other, vecs)], axis=1)
        vecs = vecs.reshape(nz * 2 * nt, vec_count, piece).transpose(1, 0, 2)
        vecs = vecs.reshape(vec_count, width)
        gain_rows, shifts = vecs[:gain_count], vecs[gain_count:]
        head_biases = jnp.stack([s[vec_size : vec_size + 2 * block] for s in smalls])
        turned = jnp.stack(
            [smalls[reverse_bits(p)][vec_size : vec_size + 2 * block] for p in range(nt)]
        )
        unit_bias = by_core(head_biases, turned).reshape(nt, 2, 2, heads, HD)
        unit_bias = by_core(unit_bias[:, :, 0], unit_bias[:, :, 1])
        unit_bias = jnp.pad(unit_bias, ((0, 0),) * 3 + ((0, LANES - HD),))
        unit_bias = unit_bias.reshape(nt, 2, heads * LANES)
        ff_bias = by_core(smalls[0][vec_size + 2 * block :], smalls[top][vec_size + 2 * block :])
        ff_bias = jnp.pad(ff_bias, (0, wide - ff)).reshape(1, wide)

        inputs_f = tokens.astype(F32)
        first_f, normed_one, spread_one = norm_rows(inputs_f, gain_rows[0], shifts[0])
        first = first_f.astype(BF16)
        first_chip = jnp.concatenate([first, swap_core(first)], axis=0)

        cots = [(g, swap_core(g)) for g in [cotangent, *cot_far]]
        cot_rows = [jnp.concatenate(pair, axis=0) for pair in cots]

        saved = []
        for p in range(nt):
            bias = unit_bias[p]
            if p == nt - 2:
                bias = tie(bias, *cot_rows)
            saved.append(attend(first_chip, attn_w[p], bias))
        mixed = [s[1] for s in saved]
        wides = [s[3] for s in saved]
        fc1_got = swap_top(tie(fc1_own, attn_w[nt - 1]))
        fc2_got = swap_top(fc2_own)
        attn_mine, attn_other = sum_nt(mixed, wides, 3)
        attention = attn_mine.astype(F32) + swap_core(attn_other).astype(F32)
        hidden_one = inputs_f + attention + shifts[1]
        second_f, normed_two, spread_two = norm_rows(hidden_one, gain_rows[1], shifts[2])

        core = c.astype(jnp.int32).reshape(1)
        second = second_f.astype(BF16)
        second_far = [swap_tensor(second, i) for i in far]
        fc1_pair, fc2_pair = (fc1_own, fc1_got), (fc2_own, fc2_got)
        ins = [None] * low
        ins[0] = feed_in(core, (second, swap_core(second)), fc1_pair, ff_bias)
        grad_fc2_t = dot_tn(cot_rows[0], ins[0][1])
        for i, rows_far in zip(far, second_far):
            rows_far = tie(rows_far, grad_fc2_t)
            ins[i] = feed_in(core, (rows_far, swap_core(rows_far)), fc1_pair, ff_bias)
            grad_fc2_t = grad_fc2_t + dot_tn(cot_rows[i], ins[i][1])
        grad_fc2_t = grad_fc2_t.astype(BF16)

        outs, grad_sums, pres, grad_fc1_bias = [None] * low, [None] * low, [None] * low, 0
        after = grad_fc2_t
        for i in reversed(range(low)):
            act, slope = ins[i][1:]
            if i == 0 or i == low - 1:
                slope = tie(slope, after)
            pres[i], out0, out1, grad0, grad1, sums = feed_out(
                core, cots[i], act, slope, fc1_pair + fc2_pair
            )
            outs[i] = (out0, out1)
            grad_fc1_bias = grad_fc1_bias + sums
            value = grad0.astype(F32) + swap_core(grad1).astype(F32)
            grad_sums[i] = value.astype(BF16) if i else value
            after = grad_sums[i]
        grad_fc1 = dot_tn(ins[0][0], pres[0])
        for i in far:
            grad_fc1 = grad_fc1 + dot_tn(ins[i][0], pres[i])
        grad_fc1 = grad_fc1.astype(BF16)

        def scatter_ff(partial):
            own = lax.psum_scatter(partial, "dp", scatter_dimension=0, tiled=True)
            return lax.optimization_barrier(own)[:, :ff].astype(F32)

        grad_fc2_t = by_core(grad_fc2_t, swap_top(grad_fc2_t))
        grad_fc2_own = scatter_ff(grad_fc2_t).T

        grad_second = grad_sums[0]
        for i in far:
            got = tie(swap_tensor(grad_sums[i], i), grad_fc1, grad_fc2_t)
            grad_second = grad_second + got.astype(F32)
        grad_fc1 = by_core(grad_fc1, swap_top(grad_fc1))
        grad_fc1_own = scatter_ff(grad_fc1)

        mlp_out = outs[0][0].astype(F32) + swap_core(outs[0][1]).astype(F32)
        for i in far:
            mine, other = outs[i]
            sent = (mine.astype(F32) + swap_core(other).astype(F32)).astype(BF16)
            mlp_out = mlp_out + swap_tensor(tie(sent, grad_second), i).astype(F32)

        cot_f = cotangent.astype(F32)
        gain_two = jnp.sum(grad_second * normed_two, axis=0)
        shift_two = jnp.sum(grad_second, axis=0)
        grad_hidden = cot_f + norm_back(grad_second, normed_two, spread_two, gain_rows[1])
        shift_out = jnp.sum(grad_hidden, axis=0)
        shift_fc2 = jnp.sum(cot_f, axis=0)
        hidden_in = grad_hidden.astype(BF16)
        hidden_chip = jnp.concatenate([hidden_in, swap_core(hidden_in)], axis=0)
        back, after = {}, None
        grad_w = [None] * nt
        got_w = {}
        for p in reversed(range(nt)):
            qkv, mix, lse = saved[p][:3]
            if after is not None:
                lse = tie(lse, *after)
            back[p] = attend_back(hidden_chip, first_chip, wides[p], qkv, mix, lse, packed)
            value = back[p][1]
            for q in sorted((q for q in got_w if got_w[q][0] == p), reverse=True):
                if p:
                    value = (value.astype(F32) + got_w[q][1].astype(F32)).astype(BF16)
            grad_w[p] = value
            after = [value]
            if p == 0:
                break
            i = p.bit_length() - 1
            got_w[p] = (p - (1 << i), stage(value, i))
            if p == 1:
                after = [value, grad_fc1]
        first_mine, first_other = sum_nt([back[p][0] for p in range(nt)], wides, 0)
        total = grad_w[0].astype(F32)
        for q in sorted((q for q in got_w if got_w[q][0] == 0), reverse=True):
            got = got_w[q][1]
            total = total + (tie(got, first_mine) if q == 1 else got).astype(F32)
        grad_w = [total.astype(BF16)]
        own_half = lax.psum_scatter(
            grad_w[0],
            "dp",
            scatter_dimension=0,
            axis_index_groups=[list(range(0, ndp, 2)), list(range(1, ndp, 2))],
            tiled=True,
        )
        own_half = own_half.reshape(2, part, packed)
        kept = by_core(own_half[0], own_half[1]).astype(F32)
        got = swap_core(by_core(own_half[1], own_half[0])).astype(F32)
        halves = [by_core(kept, got), by_core(got, kept)]
        grad_qkv_own = jnp.stack(
            [
                jnp.concatenate([g[:, k * hh : (k + 1) * hh] for g in halves], axis=1)
                for k in range(3)
            ]
        )
        grad_out_own = jnp.concatenate([g[:, 3 * hh : 4 * hh] for g in halves], axis=1).T

        first_mine = tie(first_mine, grad_w[0])
        grad_first = first_mine.astype(F32) + swap_core(first_other).astype(F32)
        gain_one = jnp.sum(grad_first * normed_one, axis=0)
        shift_one = jnp.sum(grad_first, axis=0)
        grad_tokens = grad_hidden + norm_back(grad_first, normed_one, spread_one, gain_rows[0])

        output = hidden_one + tie(mlp_out, grad_w[0]) + shifts[3]

        spots = [by_core(t ^ p, t ^ reverse_bits(p)) for p in range(nt)]
        where = jnp.stack([c, by_core(t, t ^ top)] + spots).astype(jnp.int32)
        vectors = [gain_one, gain_two, shift_one, shift_out, shift_two, shift_fc2]
        total = pack_small(
            where,
            [v.reshape(1, width) for v in vectors],
            [back[p][2] for p in range(nt)],
            grad_fc1_bias,
            nt,
        )
        total = functools.reduce(jnp.add, [swap_tensor(total, i) for i in range(1, nt)], total)
        total = functools.reduce(jnp.add, [shift_z(total, k) for k in range(1, nz)], total)
        total = total + swap_core(total)
        own = lax.dynamic_slice_in_dim(
            total[0, :vec_count, :width], (d * nt + t) * piece, piece, axis=1
        )
        mine = lax.dynamic_index_in_dim(total, 1 + t, 0, keepdims=False)
        units = mine[1:5, : heads * LANES].reshape(2, 2, heads, LANES)[:, :, :, :HD]
        head_total = units.transpose(1, 0, 2, 3).reshape(2, block)
        bias_total = mine[0, :ff]
        return (
            output,
            grad_tokens,
            own[:gain_count],
            own[gain_count:],
            grad_qkv_own,
            head_total,
            grad_out_own,
            grad_fc1_own,
            bias_total,
            grad_fc2_own,
        )

    return body


def solution(mesh):
    in_specs = (
        P(("dp", "tensor"), None),
        P(None, ("dp", "tensor")),
        P(None, ("dp", "tensor")),
        P(None, "dp", "tensor"),
        P(None, "tensor"),
        P("tensor", "dp"),
        P("dp", "tensor"),
        P("tensor"),
        P("tensor", "dp"),
        P(("dp", "tensor"), None),
    )
    out_specs = (
        P(("dp", "tensor"), None),
        P(("dp", "tensor"), None),
        P(None, ("dp", "tensor")),
        P(None, ("dp", "tensor")),
        P(None, "dp", "tensor"),
        P(None, "tensor"),
        P("tensor", "dp"),
        P("dp", "tensor"),
        P("tensor"),
        P("tensor", "dp"),
    )
    body = make_body(mesh.shape["dp"], mesh.shape["tensor"])

    return jax.shard_map(body, mesh=mesh, in_specs=in_specs, out_specs=out_specs, check_vma=False)
```

```python
import functools

import jax
import jax.numpy as jnp
from jax import lax
from jax.experimental import pallas as pl
from jax.experimental.pallas import tpu as pltpu
from jax.sharding import PartitionSpec as P


HD = 72
SEQ = 256
EPS = 1e-06
F32 = jnp.float32
BF16 = jnp.bfloat16
AXES = ("dp", "tensor")


def norm_rows(values, gain_row, shifts):
    center = values - jnp.mean(values, axis=-1, keepdims=True)
    spread = lax.rsqrt(jnp.mean(center * center, axis=-1, keepdims=True) + EPS)
    normed = center * spread
    return (normed * gain_row + shifts, normed, spread)


def norm_back(grad_rows, normed, spread, gain_row):
    scaled = grad_rows * gain_row
    return spread * (
        scaled
        - jnp.mean(scaled, axis=-1, keepdims=True)
        - normed * jnp.mean(scaled * normed, axis=-1, keepdims=True)
    )


def tie(value, *others):
    return lax.optimization_barrier((value, *others))[0]


def dot_nn(a, b):
    return lax.dot_general(a, b, (((1,), (0,)), ((), ())), preferred_element_type=F32)


def dot_nt(a, b):
    return lax.dot_general(a, b, (((1,), (1,)), ((), ())), preferred_element_type=F32)


def dot_tn(a, b):
    return lax.dot_general(a, b, (((0,), (0,)), ((), ())), preferred_element_type=F32)


LANES = 128
ATTEND_VMEM = 22 << 20
BACK_VMEM = 30 << 20
FEED_VMEM = 18 << 20
FEED_OUT_VMEM = 24 << 20
SUM_VMEM = 20 << 20


def far(x):
    return pltpu.with_memory_space_constraint(x, pltpu.HBM)


def padded(size):
    return -(-size // LANES) * LANES


class Columns:
    def __init__(self, hh):
        self.hh = hh
        self.heads = hh // HD
        self.packed = padded(4 * hh)
        self.three = padded(3 * hh + LANES - HD)
        self.low = 3 * hh // LANES * LANES
        self.window = self.packed - self.low
        self.shift = 3 * hh - self.low


def cut(array, start):
    lane = lax.broadcasted_iota(jnp.int32, (1, LANES), 1)
    piece = array[:, start : start + LANES]
    return jnp.where(lane < HD, piece, jnp.zeros_like(piece))


def place(pieces, before, width):
    rows = pieces[0].shape[0]
    parts = [piece[:, :HD] for piece in pieces]
    if before:
        parts.insert(0, jnp.zeros((rows, before), pieces[0].dtype))
    after = width - before - HD * len(pieces)
    if after:
        parts.append(jnp.zeros((rows, after), pieces[0].dtype))
    return jnp.concatenate(parts, axis=1)


def attend_kernel(cols, images, before, rows_ref, w_ref, scale_ref, bias_ref, *refs):
    lefts, rights, outs = refs[:before], refs[before : 3 * before], refs[3 * before :]
    qkv_ref, mixed_ref, lse_ref = outs[:3]
    heads, hh = cols.heads, cols.hh
    proj = dot_nn(rows_ref[...], w_ref[...])[:, : cols.three]
    qkv = ((proj + bias_ref[...]) * scale_ref[...]).astype(BF16)
    qkv_ref[...] = qkv
    units = [(m, h) for m in range(images) for h in range(heads)]

    def unit(kind, m, h):
        return cut(qkv[m * SEQ : (m + 1) * SEQ], kind * hh + h * HD)

    scores = [dot_nt(unit(0, m, h), unit(1, m, h)) for m, h in units]
    tops = [jnp.max(s, axis=-1, keepdims=True) for s in scores]
    exps = [jnp.exp(s - top) for s, top in zip(scores, tops)]
    sums = [jnp.sum(e, axis=-1, keepdims=True) for e in exps]
    probs = [(e * (1.0 / total)).astype(BF16) for e, total in zip(exps, sums)]
    mixed = [dot_nn(p, unit(2, m, h)).astype(BF16) for (m, h), p in zip(units, probs)]
    for m in range(images):
        rows = slice(m * SEQ, (m + 1) * SEQ)
        group = slice(m * heads, (m + 1) * heads)
        mixed_ref[rows, :] = place(mixed[group], cols.shift, cols.window)
        for h, (top, total) in enumerate(zip(tops[group], sums[group])):
            lse_ref[rows, h : h + 1] = top + jnp.log(total)
    if len(outs) == 3:
        return
    mine_ref, other_ref = outs[3:]
    total = dot_nt(mixed_ref[...], w_ref[:, cols.low :])
    for n, left in enumerate(lefts):
        right = jnp.concatenate([rights[2 * n][...], rights[2 * n + 1][...]], axis=1)
        total += dot_nt(left[...], right)
    value = total.astype(BF16)

    @pl.when(pl.program_id(0) == 0)
    def _():
        other_ref[...] = value

    @pl.when(pl.program_id(0) != 0)
    def _():
        mine_ref[...] = value


def attend(cols, rows, weight, scale, bias, before=None):
    total, width = rows.shape
    last = before is not None
    mixeds, weights = before if last else ((), ())
    tile = total // 2
    images = tile // SEQ
    turn = (lambda i: (lax.rem(i + 1, 2), 0)) if last else (lambda i: (i, 0))
    whole = lambda i: (0, 0)
    block = cols.low // LANES
    assert not last or cols.window == 2 * LANES
    rights = [w for weight in weights for w in (weight, weight)]
    out_specs = [
        pl.BlockSpec((tile, cols.three), turn),
        pl.BlockSpec((tile, cols.window), turn),
        pl.BlockSpec((tile, cols.heads), turn),
    ]
    out_shape = [
        pltpu.HBM((total, cols.three), BF16),
        pltpu.HBM((total, cols.window), BF16),
        pltpu.HBM((total, cols.heads), F32),
    ]
    if last:
        out_specs += [pl.BlockSpec((tile, width), whole)] * 2
        out_shape += [jax.ShapeDtypeStruct((tile, width), BF16), pltpu.HBM((tile, width), BF16)]
    return pl.pallas_call(
        functools.partial(attend_kernel, cols, images, len(mixeds)),
        grid=(2,),
        in_specs=[
            pl.BlockSpec((tile, width), turn),
            pl.BlockSpec(weight.shape, whole),
            pl.BlockSpec(scale.shape, whole),
            pl.BlockSpec(bias.shape, whole),
        ]
        + [pl.BlockSpec((tile, cols.window), turn)] * len(mixeds)
        + [
            pl.BlockSpec((width, LANES), lambda i, j=j: (0, block + j))
            for _ in weights
            for j in range(2)
        ],
        out_specs=out_specs,
        out_shape=out_shape,
        compiler_params=pltpu.CompilerParams(vmem_limit_bytes=ATTEND_VMEM),
        cost_estimate=pl.CostEstimate(
            flops=2 * total * width * cols.packed + 4 * total * SEQ * LANES * cols.heads,
            bytes_accessed=2 * (total * (width + 4 * cols.hh) + weight.size),
            transcendentals=total * SEQ * cols.heads,
        ),
        name="attend",
    )(far(rows), weight, scale, bias, *[far(m) for m in mixeds], *rights)


def attend_back_kernel(
    cols, images, extras, own_ref, other_hbm, rows_ref, w_ref, qkv_ref, mixed_ref, lse_ref, *refs
):
    extra_hbm = refs[:extras]
    proj_ref, gw_ref, sums_ref, acc, grad, other, sems = refs[extras : extras + 7]
    extra = refs[extras + 7 :]
    heads, hh = cols.heads, cols.hh
    step = pl.program_id(0)
    copies = [pltpu.make_async_copy(other_hbm, other, sems.at[0])] + [
        pltpu.make_async_copy(source, target, sems.at[1 + i])
        for i, (source, target) in enumerate(zip(extra_hbm, extra))
    ]

    @pl.when(step == 0)
    def _():
        for copy in copies:
            copy.start()
        grad[...] = own_ref[...]

    @pl.when(step != 0)
    def _():
        copies[0].wait()
        grad[...] = other[...]

    gh = grad[...]
    gmix = dot_nn(gh, w_ref[:, cols.low :]).astype(BF16)
    units = [(m, h) for m in range(images) for h in range(heads)]

    def unit(kind, m, h):
        return cut(qkv_ref[m * SEQ : (m + 1) * SEQ, :], kind * hh + h * HD)

    query = [unit(0, m, h) for m, h in units]
    keys = [unit(1, m, h) for m, h in units]
    vals = [unit(2, m, h) for m, h in units]
    gm = [cut(gmix[m * SEQ : (m + 1) * SEQ], cols.shift + h * HD) for m, h in units]
    lse = [lse_ref[m * SEQ : (m + 1) * SEQ, h : h + 1] for m, h in units]
    probs = [jnp.exp(dot_nt(q, k) - top) for q, k, top in zip(query, keys, lse)]
    dprobs = [dot_nt(g, v) for g, v in zip(gm, vals)]
    dots = [jnp.sum(p * dp, axis=-1, keepdims=True) for p, dp in zip(probs, dprobs)]
    dscores = [(p * (dp - dt)).astype(BF16) for p, dp, dt in zip(probs, dprobs, dots)]
    grads = [
        (
            dot_nn(dscores[n], keys[n]) * HD ** (-0.5),
            dot_tn(dscores[n], query[n]),
            dot_tn(probs[n].astype(BF16), gm[n]),
        )
        for n in range(len(units))
    ]
    sums = [[0.0] * heads for _ in range(2)]
    for n, (m, h) in enumerate(units):
        for row, kind in enumerate((0, 2)):
            sums[row][h] = sums[row][h] + jnp.sum(grads[n][kind], axis=0, keepdims=True)
    sums = jnp.concatenate([jnp.concatenate(s, axis=1) for s in sums], axis=0)
    for m in range(images):
        pieces = [
            grads[m * heads + h][kind].astype(BF16) for kind in range(3) for h in range(heads)
        ]
        proj_ref[m * SEQ : (m + 1) * SEQ, :] = place(pieces, 0, cols.three)
    gw_qkv = dot_tn(rows_ref[...], proj_ref[...])
    gw_out = dot_tn(gh, mixed_ref[...])

    @pl.when(step == 0)
    def _():
        acc[...] = jnp.zeros_like(acc)
        sums_ref[...] = sums

    @pl.when(step > 0)
    def _():
        sums_ref[...] += sums

    acc[:, : cols.three] += gw_qkv
    acc[:, cols.low :] += gw_out

    @pl.when(step != 0)
    def _():
        total = acc[...]
        for i in range(extras):
            copies[1 + i].wait()
            total += extra[i][...].astype(F32)
        gw_ref[...] = total.astype(BF16)


def attend_back(cols, grad_rows, rows, weight, qkv, mixed, lse, extra):
    total, width = rows.shape
    tile = total // 2
    images = tile // SEQ
    step = lambda i: (i, 0)
    whole = lambda i: (0, 0)
    lanes = cols.heads * LANES
    anywhere = pl.BlockSpec(memory_space=pl.ANY)
    own, other = grad_rows
    return pl.pallas_call(
        functools.partial(attend_back_kernel, cols, images, len(extra)),
        grid=(2,),
        in_specs=[
            pl.BlockSpec((tile, width), whole),
            anywhere,
            pl.BlockSpec((tile, width), step),
            pl.BlockSpec(weight.shape, whole),
            pl.BlockSpec((tile, cols.three), step),
            pl.BlockSpec((tile, cols.window), step),
            pl.BlockSpec((tile, cols.heads), step),
        ]
        + [anywhere] * len(extra),
        out_specs=[
            pl.BlockSpec((tile, cols.three), step),
            pl.BlockSpec(weight.shape, whole),
            pl.BlockSpec((2, lanes), whole),
        ],
        out_shape=[
            pltpu.HBM((total, cols.three), BF16),
            jax.ShapeDtypeStruct(weight.shape, BF16),
            jax.ShapeDtypeStruct((2, lanes), F32),
        ],
        scratch_shapes=[
            pltpu.VMEM(weight.shape, F32),
            pltpu.VMEM((tile, width), BF16),
            pltpu.VMEM((tile, width), BF16),
            pltpu.SemaphoreType.DMA((1 + len(extra),)),
        ]
        + [pltpu.VMEM(weight.shape, BF16)] * len(extra),
        compiler_params=pltpu.CompilerParams(vmem_limit_bytes=BACK_VMEM),
        cost_estimate=pl.CostEstimate(
            flops=2 * total * width * (cols.packed + cols.window) + 10 * total * SEQ * lanes,
            bytes_accessed=2 * (2 * total * width + 7 * total * cols.hh + 2 * weight.size),
            transcendentals=total * SEQ * cols.heads,
        ),
        name="attend_back",
    )(own, far(other), far(rows), weight, far(qkv), far(mixed), far(lse), *map(far, extra))


def sum_nt_kernel(count, inner, *refs):
    lefts, rights = refs[:count], refs[count : 2 * count]
    mine_ref, other_ref = refs[2 * count :]
    total = dot_nt(lefts[0][...], rights[0][:, :inner])
    for left, right in zip(lefts[1:], rights[1:]):
        total += dot_nt(left[...], right[:, :inner])
    value = total.astype(BF16)
    half = pl.num_programs(0) // 2

    @pl.when(pl.program_id(0) < half)
    def _():
        other_ref[...] = value

    @pl.when(pl.program_id(0) >= half)
    def _():
        mine_ref[...] = value


def sum_nt(lefts, rights, tile=SEQ):
    count = len(lefts)
    total, inner = lefts[0].shape
    width = rights[0].shape[0]
    half = total // 2 // tile
    return pl.pallas_call(
        functools.partial(sum_nt_kernel, count, inner),
        grid=(2 * half,),
        in_specs=[pl.BlockSpec((tile, inner), lambda i: (lax.rem(i + half, 2 * half), 0))] * count
        + [pl.BlockSpec(right.shape, lambda i: (0, 0), pipeline_mode=pl.Buffered(1)) for right in rights],
        out_specs=[
            pl.BlockSpec((tile, width), lambda i: (jnp.maximum(i - half, 0), 0)),
            pl.BlockSpec((tile, width), lambda i: (jnp.minimum(i, half - 1), 0)),
        ],
        out_shape=[
            jax.ShapeDtypeStruct((total // 2, width), BF16),
            pltpu.HBM((total // 2, width), BF16),
        ],
        compiler_params=pltpu.CompilerParams(vmem_limit_bytes=SUM_VMEM),
        cost_estimate=pl.CostEstimate(
            flops=2 * total * inner * width * count,
            bytes_accessed=2 * (count * (total + width) * inner + total * width),
            transcendentals=0,
        ),
        name="sum_nt",
    )(*map(far, lefts), *rights)


def spread_kernel(count, in_ref, *out_refs):
    blocks = in_ref.shape[0]
    piece = out_refs[0].shape[1] // blocks
    for v in range(count):
        for i in range(blocks):
            out_refs[v][:, i * piece : (i + 1) * piece] = in_ref[
                i : i + 1, v * piece : (v + 1) * piece
            ]


def spread(vecs, count, width):
    return pl.pallas_call(
        functools.partial(spread_kernel, count),
        in_specs=[pl.BlockSpec(memory_space=pltpu.VMEM)],
        out_specs=[pl.BlockSpec(memory_space=pltpu.VMEM)] * count,
        out_shape=[jax.ShapeDtypeStruct((1, width), F32)] * count,
        name="spread",
    )(vecs)


def fetch_weights(core_ref, own, got, kept, sems):
    def fetch(sources):
        copies = [
            pltpu.make_async_copy(source, target, sems.at[i])
            for i, (source, target) in enumerate(zip(sources, kept))
        ]
        for copy in copies:
            copy.start()
        for copy in copies:
            copy.wait()

    @pl.when(core_ref[0] == 0)
    def _():
        fetch(own)

    @pl.when(core_ref[0] != 0)
    def _():
        fetch(got)


def feed_in_kernel(
    half, core_ref, rows0, rows1, w1_own, w1_got, bias_ref, rows_ref, act_ref, slope_ref, w1, sems
):
    step = pl.program_id(0)

    @pl.when(step == 0)
    def _():
        fetch_weights(core_ref, [w1_own], [w1_got], [w1], sems)

    rows = jnp.where(step < half, rows0[...], rows1[...])
    rows_ref[...] = rows
    pre = dot_nn(rows, w1[...]) + bias_ref[...]
    root = (2.0 / jnp.pi) ** 0.5
    square = pre * pre
    tanh = jnp.tanh(root * (pre + 0.044715 * (pre * square)))
    gate = 0.5 * (1.0 + tanh)
    slope = gate + 0.5 * pre * (1.0 - tanh * tanh) * (root * (1.0 + 3 * 0.044715 * square))
    act_ref[...] = (pre * gate).astype(BF16)
    slope_ref[...] = slope.astype(BF16)


def feed_in(core, rows, weights, bias, tile=SEQ):
    count, width = rows[0].shape
    ff = weights[0].shape[1]
    half = count // tile
    step = lambda i: (i, 0)
    anywhere = pl.BlockSpec(memory_space=pl.ANY)
    return pl.pallas_call(
        functools.partial(feed_in_kernel, half),
        grid=(2 * half,),
        in_specs=[
            pl.BlockSpec(memory_space=pltpu.SMEM),
            pl.BlockSpec((tile, width), lambda i: (jnp.minimum(i, half - 1), 0)),
            pl.BlockSpec((tile, width), lambda i: (jnp.maximum(i - half, 0), 0)),
            anywhere,
            anywhere,
            pl.BlockSpec((1, ff), lambda i: (0, 0)),
        ],
        out_specs=[
            pl.BlockSpec((tile, width), step),
            pl.BlockSpec((tile, ff), step),
            pl.BlockSpec((tile, ff), step),
        ],
        out_shape=[
            jax.ShapeDtypeStruct((2 * count, width), BF16),
            jax.ShapeDtypeStruct((2 * count, ff), BF16),
            jax.ShapeDtypeStruct((2 * count, ff), BF16),
        ],
        scratch_shapes=[pltpu.VMEM((width, ff), BF16), pltpu.SemaphoreType.DMA((1,))],
        compiler_params=pltpu.CompilerParams(vmem_limit_bytes=FEED_VMEM),
        cost_estimate=pl.CostEstimate(
            flops=4 * count * width * ff,
            bytes_accessed=2 * (width * ff + 4 * count * (width + ff)),
            transcendentals=2 * count * ff,
        ),
        name="feed_in",
    )(core, *rows, *[far(w) for w in weights], bias)


def feed_out_kernel(
    half, core_ref, cot0, cot1, act_ref, slope_ref, w1_own, w1_got, w2_own, w2_got,
    gpre_ref, out0, out1, grad0, grad1, sums_ref, w1, w2, sems,
):
    step = pl.program_id(0)

    @pl.when(step == 0)
    def _():
        fetch_weights(core_ref, [w1_own, w2_own], [w1_got, w2_got], [w1, w2], sems)

    first = step < half
    cot = jnp.where(first, cot0[...], cot1[...])
    grad_pre = dot_nn(cot, w2[...]) * slope_ref[...].astype(F32)
    sums = jnp.sum(grad_pre, axis=0, keepdims=True)
    grad_in = grad_pre.astype(BF16)
    gpre_ref[...] = grad_in
    grad = dot_nt(grad_in, w1[...]).astype(BF16)
    out = dot_nt(act_ref[...], w2[...]).astype(BF16)

    @pl.when(step == 0)
    def _():
        sums_ref[...] = sums

    @pl.when(step > 0)
    def _():
        sums_ref[...] += sums

    @pl.when(first)
    def _():
        out0[...] = out
        grad0[...] = grad

    @pl.when(jnp.logical_not(first))
    def _():
        out1[...] = out
        grad1[...] = grad


def feed_out(core, cots, act, slope, weights, tile=SEQ):
    count, width = cots[0].shape
    ff = act.shape[1]
    half = count // tile
    low = lambda i: (jnp.minimum(i, half - 1), 0)
    high = lambda i: (jnp.maximum(i - half, 0), 0)
    step = lambda i: (i, 0)
    anywhere = pl.BlockSpec(memory_space=pl.ANY)
    return pl.pallas_call(
        functools.partial(feed_out_kernel, half),
        grid=(2 * half,),
        in_specs=[
            pl.BlockSpec(memory_space=pltpu.SMEM),
            pl.BlockSpec((tile, width), low),
            pl.BlockSpec((tile, width), high),
            pl.BlockSpec((tile, ff), step),
            pl.BlockSpec((tile, ff), step),
        ]
        + [anywhere] * 4,
        out_specs=[
            pl.BlockSpec((tile, ff), step),
            pl.BlockSpec((tile, width), low),
            pl.BlockSpec((tile, width), high),
            pl.BlockSpec((tile, width), low),
            pl.BlockSpec((tile, width), high),
            pl.BlockSpec((1, ff), lambda i: (0, 0)),
        ],
        out_shape=[jax.ShapeDtypeStruct((2 * count, ff), BF16)]
        + [jax.ShapeDtypeStruct((count, width), BF16)] * 4
        + [jax.ShapeDtypeStruct((1, ff), F32)],
        scratch_shapes=[
            pltpu.VMEM((width, ff), BF16),
            pltpu.VMEM((width, ff), BF16),
            pltpu.SemaphoreType.DMA((2,)),
        ],
        compiler_params=pltpu.CompilerParams(vmem_limit_bytes=FEED_OUT_VMEM),
        cost_estimate=pl.CostEstimate(
            flops=12 * count * width * ff,
            bytes_accessed=2 * (2 * width * ff + 2 * count * (3 * width + 3 * ff)),
            transcendentals=0,
        ),
        name="feed_out",
    )(core, *cots, act, slope, *[far(w) for w in weights])


def norm_back_kernel(count, *refs):
    grads, (rows_ref, cot_ref, gain_ref) = refs[:count], refs[count : count + 3]
    out_ref, rounded_ref, sums_ref = refs[count + 3 :]
    grad = grads[0][...].astype(F32)
    for other in grads[1:]:
        grad += other[...].astype(F32)
    rows = rows_ref[...]
    center = rows - jnp.mean(rows, axis=-1, keepdims=True)
    spread = lax.rsqrt(jnp.mean(center * center, axis=-1, keepdims=True) + EPS)
    normed = center * spread
    cot = cot_ref[...].astype(F32)
    out = cot + norm_back(grad, normed, spread, gain_ref[...])
    out_ref[...] = out
    rounded_ref[...] = out.astype(BF16)

    @pl.when(pl.program_id(0) == 0)
    def _():
        sums_ref[...] = jnp.zeros_like(sums_ref)

    for i, value in enumerate((grad * normed, grad, out, cot)):
        sums_ref[i : i + 1, :] += jnp.sum(value, axis=0, keepdims=True)


def norm_back_rows(grads, rows, cot, gain, tile=128):
    count, width = rows.shape
    step = pl.BlockSpec((tile, width), lambda i: (i, 0))
    return pl.pallas_call(
        functools.partial(norm_back_kernel, len(grads)),
        grid=(count // tile,),
        in_specs=[step] * (len(grads) + 2) + [pl.BlockSpec((1, width), lambda i: (0, 0))],
        out_specs=[step, step, pl.BlockSpec((8, width), lambda i: (0, 0))],
        out_shape=[
            jax.ShapeDtypeStruct((count, width), F32),
            jax.ShapeDtypeStruct((count, width), BF16),
            jax.ShapeDtypeStruct((8, width), F32),
        ],
        compiler_params=pltpu.CompilerParams(vmem_limit_bytes=16 << 20),
        cost_estimate=pl.CostEstimate(
            flops=30 * count * width,
            bytes_accessed=count * width * (2 * len(grads) + 12),
            transcendentals=count,
        ),
        name="norm_back",
    )(*grads, rows, cot, gain)


def pack_kernel(where_ref, gain_ref, shift_ref, second_ref, *refs):
    units, bias_ref, out_ref = refs[:-2], refs[-2], refs[-1]
    out_ref[...] = jnp.zeros_like(out_ref)
    width = gain_ref.shape[1]
    out_ref[0, 0:1, :width] = gain_ref[...]
    out_ref[0, 2:3, :width] = shift_ref[...]
    for spot, row in ((1, 0), (3, 2), (4, 1), (5, 3)):
        out_ref[0, spot : spot + 1, :width] = second_ref[row : row + 1, :]
    core = where_ref[0]
    for n, unit in enumerate(units):
        hp = unit.shape[1]
        spot = 1 + where_ref[2 + n]

        @pl.when(core == 0)
        def _():
            out_ref[spot, 1:3, :hp] = unit[...]

        @pl.when(core != 0)
        def _():
            out_ref[spot, 3:5, :hp] = unit[...]

    out_ref[1 + where_ref[1], 0:1, : bias_ref.shape[1]] = bias_ref[...]


def pack_small(where, vectors, units, bias, spots):
    lanes = max(x.shape[1] for x in [*vectors, *units, bias])
    return pl.pallas_call(
        pack_kernel,
        in_specs=[pl.BlockSpec(memory_space=pltpu.SMEM)]
        + [pl.BlockSpec(memory_space=pltpu.VMEM)] * (len(vectors) + len(units) + 1),
        out_specs=pl.BlockSpec(memory_space=pltpu.VMEM),
        out_shape=jax.ShapeDtypeStruct((1 + spots, 8, lanes), F32),
        name="pack_small",
    )(where, *vectors, *units, bias)


def make_body(ndp, nt):
    nz = ndp // 2
    bits = nt.bit_length() - 1
    top = nt // 2
    low = nt // 2

    def perm(move):
        pairs = []
        for d in range(ndp):
            for t in range(nt):
                d2, t2 = move(d, t)
                pairs.append((d * nt + t, d2 * nt + t2))
        return pairs

    def send(value, move):
        return lax.ppermute(value, AXES, perm(move))

    def swap_core(value):
        return send(value, lambda d, t: (d ^ 1, t))

    def swap_tensor(value, i):
        return send(value, lambda d, t: (d, t ^ i))

    def shift_z(value, k):
        return send(value, lambda d, t: ((d + 2 * k) % ndp, t))

    def stage(value, i):
        return send(
            value, lambda d, t: (d, t ^ ((1 << i) if d % 2 == 0 else (1 << (bits - 1 - i))))
        )

    def reverse_bits(p):
        return sum(((p >> i) & 1) << (bits - 1 - i) for i in range(bits))

    def swap_top(value):
        pairs = [(d * nt + t, d * nt + (t ^ top)) for d in range(1, ndp, 2) for t in range(nt)]
        return lax.ppermute(value, AXES, pairs)

    def gather_z(value, z):
        out = jnp.zeros((nz,) + value.shape, value.dtype)
        out = lax.dynamic_update_slice_in_dim(out, value[None], z, 0)
        for k in range(1, nz):
            got = shift_z(value, k)
            out = lax.dynamic_update_slice_in_dim(out, got[None], lax.rem(z - k + nz, nz), 0)
        return out

    def pick(selector, items):
        total = jnp.where(selector == 0, items[0], 0)
        for i in range(1, len(items)):
            total = total + jnp.where(selector == i, items[i], 0)
        return total

    def body(
        tokens, norm_gains, row_biases, w_qkv, head_bias, w_out, w_fc1, fc1_bias, w_fc2, cotangent
    ):
        d = lax.axis_index("dp")
        t = lax.axis_index("tensor")
        z, c = d // 2, d % 2
        core0 = c == 0
        _, width = tokens.shape
        block = w_qkv.shape[2]
        hh = block // 2
        part = w_qkv.shape[1]
        ff = w_fc1.shape[1]

        def by_core(zero, one):
            return jnp.where(core0, zero, one)

        w_out_t = w_out.T

        cols = Columns(hh)
        packed, heads = cols.packed, cols.heads
        wide = padded(ff)

        def half(h):
            sl = slice(h * hh, (h + 1) * hh)
            cols = [w_qkv[0][:, sl], w_qkv[1][:, sl], w_qkv[2][:, sl], w_out_t[:, sl]]
            return jnp.pad(jnp.concatenate(cols, axis=1), ((0, 0), (0, packed - 4 * hh)))

        gathered = lax.all_gather(jnp.stack([half(0), half(1)]), "dp", axis=1, tiled=True)
        others = range(1, low)
        cot_far = [swap_tensor(cotangent, i) for i in others]

        gain_count, shift_count = norm_gains.shape[0], row_biases.shape[0]
        vec_count = gain_count + shift_count
        piece = norm_gains.shape[1]
        small = jnp.concatenate(
            [norm_gains.reshape(-1), row_biases.reshape(-1), head_bias.reshape(-1), fc1_bias]
        )
        smalls = [small] + [swap_tensor(small, i) for i in range(1, nt)]
        vec_size = vec_count * piece
        vecs = jnp.stack([pick(t ^ i, [s[:vec_size] for s in smalls]) for i in range(nt)])
        vecs = gather_z(vecs, z)
        vecs_other = swap_core(vecs)
        vecs = jnp.stack([by_core(vecs, vecs_other), by_core(vecs_other, vecs)], axis=1)
        vecs = spread(vecs.reshape(nz * 2 * nt, vec_size), vec_count, width)
        gain_rows, shifts = vecs[:gain_count], vecs[gain_count:]
        head_biases = jnp.stack([s[vec_size : vec_size + 2 * block] for s in smalls])
        turned = jnp.stack(
            [smalls[reverse_bits(p)][vec_size : vec_size + 2 * block] for p in range(nt)]
        )
        unit_bias = by_core(head_biases, turned).reshape(nt, 2, 2, hh)
        unit_bias = by_core(unit_bias[:, :, 0], unit_bias[:, :, 1])
        unit_bias = jnp.concatenate(
            [
                unit_bias[:, 0],
                jnp.zeros((nt, hh), F32),
                unit_bias[:, 1],
                jnp.zeros((nt, cols.three - 3 * hh), F32),
            ],
            axis=1,
        ).reshape(nt, 1, cols.three)
        scale = jnp.where(jnp.arange(cols.three) < hh, HD ** (-0.5), 1.0).astype(F32)
        scale = scale.reshape(1, cols.three)
        ff_bias = by_core(smalls[0][vec_size + 2 * block :], smalls[top][vec_size + 2 * block :])
        ff_bias = jnp.pad(ff_bias, (0, wide - ff)).reshape(1, wide)

        inputs_f = tokens.astype(F32)
        first_f, normed_one, spread_one = norm_rows(inputs_f, gain_rows[0], shifts[0])
        first = first_f.astype(BF16)
        first_chip = jnp.concatenate([first, swap_core(first)], axis=0)

        cots = [(g, swap_core(g)) for g in [cotangent, *cot_far]]
        cot_rows = [jnp.concatenate(pair, axis=0) for pair in cots]
        early = (first_chip, unit_bias, ff_bias)
        attn_w = [lax.dynamic_index_in_dim(tie(gathered, *early), c, 0, keepdims=False)]
        for i in range(bits):
            sent = list(attn_w)
            if i:
                sent[-1] = tie(sent[-1], *cot_rows)
            attn_w = attn_w + [stage(b, i) for b in sent]

        def gather_ff(own):
            return lax.all_gather(
                jnp.pad(own, ((0, 0), (0, wide - ff))), "dp", axis=0, tiled=True
            )

        fc1_own, fc2_own = gather_ff(w_fc1), gather_ff(tie(w_fc2.T, *vecs))

        saved = []
        for p in range(nt):
            before = None
            if p == nt - 1:
                before = ([s[1] for s in saved], attn_w[:p])
            saved.append(attend(cols, first_chip, attn_w[p], scale, unit_bias[p], before))
        attn_mine, attn_other = saved[-1][3:]
        fc1_got = swap_top(tie(fc1_own, attn_w[nt - 1], attn_w[nt - 2]))
        fc2_got = swap_top(fc2_own)
        attention = attn_mine.astype(F32) + swap_core(attn_other).astype(F32)
        hidden_one = inputs_f + attention + shifts[1]
        second_f = norm_rows(hidden_one, gain_rows[1], shifts[2])[0]

        core = c.astype(jnp.int32).reshape(1)
        second = second_f.astype(BF16)
        second_far = [swap_tensor(second, i) for i in others]
        fc1_pair, fc2_pair = (fc1_own, fc1_got), (fc2_own, fc2_got)
        ins = [None] * low
        ins[0] = feed_in(core, (second, swap_core(second)), fc1_pair, ff_bias)
        grad_fc2_t = dot_tn(cot_rows[0], ins[0][1])
        for i, rows_far in zip(others, second_far):
            rows_far = tie(rows_far, grad_fc2_t)
            ins[i] = feed_in(core, (rows_far, swap_core(rows_far)), fc1_pair, ff_bias)

        outs, grad_sums, pres, grad_fc1_bias = [None] * low, [None] * low, [None] * low, 0
        after = []
        for i in reversed(range(low)):
            act, slope = ins[i][1:]
            if i == 0 or i == low - 1:
                slope = tie(slope, *after)
            pres[i], out0, out1, grad0, grad1, sums = feed_out(
                core, cots[i], act, slope, fc1_pair + fc2_pair
            )
            grad_fc1_bias = grad_fc1_bias + sums
            got = swap_core(grad1)
            got_out = swap_core(out1).astype(F32)
            if i:
                grad_fc2_t = grad_fc2_t + dot_tn(cot_rows[i], tie(ins[i][1], pres[i]))
                got = tie(got, grad_fc2_t)
            if i:
                got = (grad0.astype(F32) + got.astype(F32)).astype(BF16)
            grad_sums[i] = got
            grad_near = grad0
            if i == 1:
                grad_fc2_t = tie(grad_fc2_t, grad_sums[i]).astype(BF16)
            outs[i] = out0.astype(F32) + got_out
            if i:
                outs[i] = tie(outs[i].astype(BF16), grad_sums[i])
            after = [grad_sums[i], grad_fc2_t, outs[i]]
        got_fc2 = swap_top(grad_fc2_t)
        grad_fc1 = 0
        for i in reversed(range(low)):
            grad_fc1 = grad_fc1 + dot_tn(ins[i][0], tie(pres[i], grad_sums[0]))
        grad_fc1 = grad_fc1.astype(BF16)
        got_fc1 = swap_top(grad_fc1)

        def scatter_ff(partial):
            own = lax.psum_scatter(partial, "dp", scatter_dimension=0, tiled=True)
            return lax.optimization_barrier(own)[:, :ff].astype(F32)

        grad_fc2_t = by_core(grad_fc2_t, tie(got_fc2, grad_fc1))
        grad_fc2_own = scatter_ff(grad_fc2_t).T

        grad_second = [grad_near, grad_sums[0]]
        for i in others:
            got = swap_tensor(grad_sums[i], i)
            grad_second.append(tie(got, grad_fc1, grad_fc2_t))
        mlp_out = outs[0]
        for i in others:
            mlp_out = mlp_out + swap_tensor(outs[i], i).astype(F32)

        grad_hidden, hidden_in, second_sums = norm_back_rows(
            grad_second, hidden_one, cotangent, gain_rows[1]
        )
        hidden_pair = (hidden_in, swap_core(hidden_in))
        back, after = {}, None
        grad_w = [None] * nt
        got_w = {}
        for p in reversed(range(nt)):
            qkv, mix, lse = saved[p][:3]
            if after is not None:
                lse = tie(lse, *after)
            come = sorted((q for q in got_w if got_w[q][0] == p and (p or q > 1)), reverse=True)
            extra = [got_w[q][1] for q in come]
            back[p] = attend_back(cols, hidden_pair, first_chip, attn_w[p], qkv, mix, lse, extra)
            value = back[p][1]
            grad_w[p] = value
            after = [value]
            if p == nt - 2:
                grad_fc1 = by_core(grad_fc1, tie(got_fc1, value))
                grad_fc1_own = scatter_ff(grad_fc1)
                after = [value, grad_fc1]
            if p == 0:
                break
            i = p.bit_length() - 1
            got_w[p] = (p - (1 << i), stage(value, i))
        grad_w = [(grad_w[0].astype(F32) + got_w[1][1].astype(F32)).astype(BF16)]
        own_half = lax.psum_scatter(
            grad_w[0],
            "dp",
            scatter_dimension=0,
            axis_index_groups=[list(range(0, ndp, 2)), list(range(1, ndp, 2))],
            tiled=True,
        )
        own_half = own_half.reshape(2, part, packed)
        kept = by_core(own_half[0], own_half[1]).astype(F32)
        got = swap_core(by_core(own_half[1], own_half[0])).astype(F32)
        halves = [by_core(kept, got), by_core(got, kept)]
        grad_qkv_own = jnp.stack(
            [
                jnp.concatenate([g[:, k * hh : (k + 1) * hh] for g in halves], axis=1)
                for k in range(3)
            ]
        )
        grad_out_own = jnp.concatenate([g[:, 3 * hh : 4 * hh] for g in halves], axis=1).T

        projs = [back[p][0] for p in range(nt)]
        projs[0] = tie(projs[0], grad_w[0])
        first_mine, first_other = sum_nt(projs, attn_w)
        grad_first = first_mine.astype(F32) + swap_core(first_other).astype(F32)
        gain_one = jnp.sum(grad_first * normed_one, axis=0, keepdims=True)
        shift_one = jnp.sum(grad_first, axis=0, keepdims=True)
        grad_tokens = grad_hidden + norm_back(grad_first, normed_one, spread_one, gain_rows[0])

        output = hidden_one + tie(mlp_out, grad_w[0]) + shifts[3]

        spots = [by_core(t ^ p, t ^ reverse_bits(p)) for p in range(nt)]
        where = jnp.stack([c, by_core(t, t ^ top)] + spots).astype(jnp.int32)
        total = pack_small(
            where,
            [gain_one, shift_one, second_sums],
            [back[p][2] for p in range(nt)],
            grad_fc1_bias,
            nt,
        )
        total = functools.reduce(jnp.add, [swap_tensor(total, i) for i in range(1, nt)], total)
        total = tie(total, grad_tokens)
        total = functools.reduce(jnp.add, [shift_z(total, k) for k in range(1, nz)], total)
        total = tie(total, output, grad_fc1_own, grad_fc2_own)
        total = total + swap_core(total)
        own = lax.dynamic_slice_in_dim(
            total[0, :vec_count, :width], (d * nt + t) * piece, piece, axis=1
        )
        mine = lax.dynamic_index_in_dim(total, 1 + t, 0, keepdims=False)
        units = mine[1:5, : heads * LANES].reshape(2, 2, heads, LANES)[:, :, :, :HD]
        head_total = units.transpose(1, 0, 2, 3).reshape(2, block)
        bias_total = mine[0, :ff]
        return (
            output,
            grad_tokens,
            own[:gain_count],
            own[gain_count:],
            grad_qkv_own,
            head_total,
            grad_out_own,
            grad_fc1_own,
            bias_total,
            grad_fc2_own,
        )

    return body


def solution(mesh):
    in_specs = (
        P(("dp", "tensor"), None),
        P(None, ("dp", "tensor")),
        P(None, ("dp", "tensor")),
        P(None, "dp", "tensor"),
        P(None, "tensor"),
        P("tensor", "dp"),
        P("dp", "tensor"),
        P("tensor"),
        P("tensor", "dp"),
        P(("dp", "tensor"), None),
    )
    out_specs = (
        P(("dp", "tensor"), None),
        P(("dp", "tensor"), None),
        P(None, ("dp", "tensor")),
        P(None, ("dp", "tensor")),
        P(None, "dp", "tensor"),
        P(None, "tensor"),
        P("tensor", "dp"),
        P("dp", "tensor"),
        P("tensor"),
        P("tensor", "dp"),
    )
    body = make_body(mesh.shape["dp"], mesh.shape["tensor"])

    return jax.shard_map(body, mesh=mesh, in_specs=in_specs, out_specs=out_specs, check_vma=False)
```

```python
import functools

import jax
import jax.numpy as jnp
from jax import lax
from jax.experimental import pallas as pl
from jax.experimental.pallas import tpu as pltpu
from jax.sharding import PartitionSpec as P


HD = 72
SEQ = 256
EPS = 1e-06
F32 = jnp.float32
BF16 = jnp.bfloat16
AXES = ("dp", "tensor")


def norm_rows(values, gain_row, shifts):
    center = values - jnp.mean(values, axis=-1, keepdims=True)
    spread = lax.rsqrt(jnp.mean(center * center, axis=-1, keepdims=True) + EPS)
    normed = center * spread
    return (normed * gain_row + shifts, normed, spread)


def norm_back(grad_rows, normed, spread, gain_row):
    scaled = grad_rows * gain_row
    return spread * (
        scaled
        - jnp.mean(scaled, axis=-1, keepdims=True)
        - normed * jnp.mean(scaled * normed, axis=-1, keepdims=True)
    )


def tie(value, *others):
    return lax.optimization_barrier((value, *others))[0]


def dot_nn(a, b):
    return lax.dot_general(a, b, (((1,), (0,)), ((), ())), preferred_element_type=F32)


def dot_nt(a, b):
    return lax.dot_general(a, b, (((1,), (1,)), ((), ())), preferred_element_type=F32)


def dot_tn(a, b):
    return lax.dot_general(a, b, (((0,), (0,)), ((), ())), preferred_element_type=F32)


LANES = 128
ATTEND_VMEM = 22 << 20
BACK_VMEM = 30 << 20
FEED_VMEM = 18 << 20
FEED_OUT_VMEM = 24 << 20
SUM_VMEM = 20 << 20


def far(x):
    return pltpu.with_memory_space_constraint(x, pltpu.HBM)


def near(x):
    return pltpu.with_memory_space_constraint(x, pltpu.VMEM)


def padded(size):
    return -(-size // LANES) * LANES


class Columns:
    def __init__(self, hh):
        self.hh = hh
        self.heads = hh // HD
        self.packed = padded(4 * hh)
        self.three = padded(3 * hh + LANES - HD)
        self.low = 3 * hh // LANES * LANES
        self.window = self.packed - self.low
        self.shift = 3 * hh - self.low


def cut(array, start):
    lane = lax.broadcasted_iota(jnp.int32, (1, LANES), 1)
    piece = array[:, start : start + LANES]
    return jnp.where(lane < HD, piece, jnp.zeros_like(piece))


def place(pieces, before, width):
    rows = pieces[0].shape[0]
    parts = [piece[:, :HD] for piece in pieces]
    if before:
        parts.insert(0, jnp.zeros((rows, before), pieces[0].dtype))
    after = width - before - HD * len(pieces)
    if after:
        parts.append(jnp.zeros((rows, after), pieces[0].dtype))
    return jnp.concatenate(parts, axis=1)


def attend_kernel(cols, images, before, rows_ref, w_ref, scale_ref, bias_ref, *refs):
    lefts, rights, outs = refs[:before], refs[before : 3 * before], refs[3 * before :]
    qkv_ref, mixed_ref, lse_ref = outs[:3]
    heads, hh = cols.heads, cols.hh
    proj = dot_nn(rows_ref[...], w_ref[...])[:, : cols.three]
    qkv = ((proj + bias_ref[...]) * scale_ref[...]).astype(BF16)
    qkv_ref[...] = qkv
    units = [(m, h) for m in range(images) for h in range(heads)]

    def unit(kind, m, h):
        return cut(qkv[m * SEQ : (m + 1) * SEQ], kind * hh + h * HD)

    scores = [dot_nt(unit(0, m, h), unit(1, m, h)) for m, h in units]
    tops = [jnp.max(s, axis=-1, keepdims=True) for s in scores]
    exps = [jnp.exp(s - top) for s, top in zip(scores, tops)]
    sums = [jnp.sum(e, axis=-1, keepdims=True) for e in exps]
    probs = [(e * (1.0 / total)).astype(BF16) for e, total in zip(exps, sums)]
    mixed = [dot_nn(p, unit(2, m, h)).astype(BF16) for (m, h), p in zip(units, probs)]
    for m in range(images):
        rows = slice(m * SEQ, (m + 1) * SEQ)
        group = slice(m * heads, (m + 1) * heads)
        mixed_ref[rows, :] = place(mixed[group], cols.shift, cols.window)
        lse = [top + jnp.log(total) for top, total in zip(tops[group], sums[group])]
        lane = lax.broadcasted_iota(jnp.int32, (1, LANES), 1)
        wide = jnp.broadcast_to(lse[0], (SEQ, LANES))
        for h in range(1, heads):
            wide = jnp.where(lane == h, lse[h], wide)
        lse_ref[rows, :] = wide
    if len(outs) == 3:
        return
    mine_ref, other_ref = outs[3:]
    total = dot_nt(mixed_ref[...], w_ref[:, cols.low :])
    for n, left in enumerate(lefts):
        right = jnp.concatenate([rights[2 * n][...], rights[2 * n + 1][...]], axis=1)
        total += dot_nt(left[...], right)
    value = total.astype(BF16)

    @pl.when(pl.program_id(0) == 0)
    def _():
        other_ref[...] = value

    @pl.when(pl.program_id(0) != 0)
    def _():
        mine_ref[...] = value


def attend(cols, rows, weight, scale, bias, before=None):
    total, width = rows.shape
    last = before is not None
    mixeds, weights = before if last else ((), ())
    tile = total // 2
    images = tile // SEQ
    turn = (lambda i: (lax.rem(i + 1, 2), 0)) if last else (lambda i: (i, 0))
    whole = lambda i: (0, 0)
    block = cols.low // LANES
    assert not last or cols.window == 2 * LANES
    rights = [w for weight in weights for w in (weight, weight)]
    out_specs = [
        pl.BlockSpec((tile, cols.three), turn),
        pl.BlockSpec((tile, cols.window), turn),
        pl.BlockSpec((tile, LANES), turn),
    ]
    out_shape = [
        pltpu.HBM((total, cols.three), BF16),
        pltpu.HBM((total, cols.window), BF16),
        pltpu.HBM((total, LANES), F32),
    ]
    if last:
        out_specs += [pl.BlockSpec((tile, width), whole)] * 2
        out_shape += [jax.ShapeDtypeStruct((tile, width), BF16), pltpu.HBM((tile, width), BF16)]
    return pl.pallas_call(
        functools.partial(attend_kernel, cols, images, len(mixeds)),
        grid=(2,),
        in_specs=[
            pl.BlockSpec((tile, width), turn),
            pl.BlockSpec(weight.shape, whole),
            pl.BlockSpec(scale.shape, whole),
            pl.BlockSpec(bias.shape, whole),
        ]
        + [pl.BlockSpec((tile, cols.window), turn)] * len(mixeds)
        + [
            pl.BlockSpec((width, LANES), lambda i, j=j: (0, block + j))
            for _ in weights
            for j in range(2)
        ],
        out_specs=out_specs,
        out_shape=out_shape,
        compiler_params=pltpu.CompilerParams(vmem_limit_bytes=ATTEND_VMEM),
        cost_estimate=pl.CostEstimate(
            flops=2 * total * width * cols.packed + 4 * total * SEQ * LANES * cols.heads,
            bytes_accessed=2 * (total * (width + 4 * cols.hh) + weight.size),
            transcendentals=total * SEQ * cols.heads,
        ),
        name="attend",
    )(far(rows), weight, scale, bias, *[far(m) for m in mixeds], *rights)


def attend_back_kernel(
    cols, images, extras, own_ref, other_hbm, rows_ref, w_ref, qkv_ref, mixed_ref, lse_ref, *refs
):
    extra_hbm = refs[:extras]
    proj_ref, gw_ref, sums_ref, acc, grad, other, sems = refs[extras : extras + 7]
    extra = refs[extras + 7 :]
    heads, hh = cols.heads, cols.hh
    step = pl.program_id(0)
    copies = [pltpu.make_async_copy(other_hbm, other, sems.at[0])] + [
        pltpu.make_async_copy(source, target, sems.at[1 + i])
        for i, (source, target) in enumerate(zip(extra_hbm, extra))
    ]

    @pl.when(step == 0)
    def _():
        for copy in copies:
            copy.start()
        grad[...] = own_ref[...]

    @pl.when(step != 0)
    def _():
        copies[0].wait()
        grad[...] = other[...]

    gh = grad[...]
    gmix = dot_nn(gh, w_ref[:, cols.low :]).astype(BF16)
    units = [(m, h) for m in range(images) for h in range(heads)]

    def unit(kind, m, h):
        return cut(qkv_ref[m * SEQ : (m + 1) * SEQ, :], kind * hh + h * HD)

    query = [unit(0, m, h) for m, h in units]
    keys = [unit(1, m, h) for m, h in units]
    vals = [unit(2, m, h) for m, h in units]
    gm = [cut(gmix[m * SEQ : (m + 1) * SEQ], cols.shift + h * HD) for m, h in units]
    lse = [lse_ref[m * SEQ : (m + 1) * SEQ, h : h + 1] for m, h in units]
    probs = [jnp.exp(dot_nt(q, k) - top) for q, k, top in zip(query, keys, lse)]
    dprobs = [dot_nt(g, v) for g, v in zip(gm, vals)]
    dots = [jnp.sum(p * dp, axis=-1, keepdims=True) for p, dp in zip(probs, dprobs)]
    dscores = [(p * (dp - dt)).astype(BF16) for p, dp, dt in zip(probs, dprobs, dots)]
    grads = [
        (
            dot_nn(dscores[n], keys[n]) * HD ** (-0.5),
            dot_tn(dscores[n], query[n]),
            dot_tn(probs[n].astype(BF16), gm[n]),
        )
        for n in range(len(units))
    ]
    sums = [[0.0] * heads for _ in range(2)]
    for n, (m, h) in enumerate(units):
        for row, kind in enumerate((0, 2)):
            sums[row][h] = sums[row][h] + jnp.sum(grads[n][kind], axis=0, keepdims=True)
    sums = jnp.concatenate([jnp.concatenate(s, axis=1) for s in sums], axis=0)
    for m in range(images):
        pieces = [
            grads[m * heads + h][kind].astype(BF16) for kind in range(3) for h in range(heads)
        ]
        proj_ref[m * SEQ : (m + 1) * SEQ, :] = place(pieces, 0, cols.three)
    gw_qkv = dot_tn(rows_ref[...], proj_ref[...])
    gw_out = dot_tn(gh, mixed_ref[...])

    @pl.when(step == 0)
    def _():
        acc[...] = jnp.zeros_like(acc)
        sums_ref[...] = sums

    @pl.when(step > 0)
    def _():
        sums_ref[...] += sums

    acc[:, : cols.three] += gw_qkv
    acc[:, cols.low :] += gw_out

    @pl.when(step != 0)
    def _():
        total = acc[...]
        for i in range(extras):
            copies[1 + i].wait()
            total += extra[i][...].astype(F32)
        gw_ref[...] = total.astype(BF16)


def attend_back(cols, grad_rows, rows, weight, qkv, mixed, lse, extra):
    total, width = rows.shape
    tile = total // 2
    images = tile // SEQ
    step = lambda i: (i, 0)
    whole = lambda i: (0, 0)
    lanes = cols.heads * LANES
    anywhere = pl.BlockSpec(memory_space=pl.ANY)
    own, other = grad_rows
    return pl.pallas_call(
        functools.partial(attend_back_kernel, cols, images, len(extra)),
        grid=(2,),
        in_specs=[
            pl.BlockSpec((tile, width), whole),
            anywhere,
            pl.BlockSpec((tile, width), step),
            pl.BlockSpec(weight.shape, whole),
            pl.BlockSpec((tile, cols.three), step),
            pl.BlockSpec((tile, cols.window), step),
            pl.BlockSpec((tile, LANES), step),
        ]
        + [anywhere] * len(extra),
        out_specs=[
            pl.BlockSpec((tile, cols.three), step),
            pl.BlockSpec(weight.shape, whole),
            pl.BlockSpec((2, lanes), whole),
        ],
        out_shape=[
            pltpu.HBM((total, cols.three), BF16),
            jax.ShapeDtypeStruct(weight.shape, BF16),
            jax.ShapeDtypeStruct((2, lanes), F32),
        ],
        scratch_shapes=[
            pltpu.VMEM(weight.shape, F32),
            pltpu.VMEM((tile, width), BF16),
            pltpu.VMEM((tile, width), BF16),
            pltpu.SemaphoreType.DMA((1 + len(extra),)),
        ]
        + [pltpu.VMEM(weight.shape, BF16)] * len(extra),
        compiler_params=pltpu.CompilerParams(vmem_limit_bytes=BACK_VMEM),
        cost_estimate=pl.CostEstimate(
            flops=2 * total * width * (cols.packed + cols.window) + 10 * total * SEQ * lanes,
            bytes_accessed=2 * (2 * total * width + 7 * total * cols.hh + 2 * weight.size),
            transcendentals=total * SEQ * cols.heads,
        ),
        name="attend_back",
    )(far(own), far(other), far(rows), far(weight), far(qkv), far(mixed), far(lse), *extra)


def sum_nt_kernel(count, inner, *refs):
    lefts, rights = refs[:count], refs[count : 2 * count]
    before, (mine_ref, other_ref) = refs[2 * count : -2], refs[-2:]
    total = dot_nt(lefts[0][...], rights[0][:, :inner])
    for left, right in zip(lefts[1:], rights[1:]):
        total += dot_nt(left[...], right[:, :inner])
    half = pl.num_programs(0) // 2

    def store(target, source):
        value = total + source[0][...].astype(F32) if source else total
        target[...] = value.astype(BF16)

    @pl.when(pl.program_id(0) < half)
    def _():
        store(other_ref, before[1:])

    @pl.when(pl.program_id(0) >= half)
    def _():
        store(mine_ref, before[:1])


def sum_nt(lefts, rights, before=(), tile=SEQ):
    count = len(lefts)
    total, inner = lefts[0].shape
    width = rights[0].shape[0]
    half = total // 2 // tile
    rows_specs = [
        pl.BlockSpec((tile, width), lambda i: (jnp.maximum(i - half, 0), 0)),
        pl.BlockSpec((tile, width), lambda i: (jnp.minimum(i, half - 1), 0)),
    ]
    return pl.pallas_call(
        functools.partial(sum_nt_kernel, count, inner),
        grid=(2 * half,),
        in_specs=[pl.BlockSpec((tile, inner), lambda i: (lax.rem(i + half, 2 * half), 0))] * count
        + [pl.BlockSpec(r.shape, lambda i: (0, 0), pipeline_mode=pl.Buffered(1)) for r in rights]
        + rows_specs[: len(before)],
        out_specs=rows_specs,
        out_shape=[
            jax.ShapeDtypeStruct((total // 2, width), BF16),
            pltpu.HBM((total // 2, width), BF16),
        ],
        compiler_params=pltpu.CompilerParams(vmem_limit_bytes=SUM_VMEM),
        cost_estimate=pl.CostEstimate(
            flops=2 * total * inner * width * count,
            bytes_accessed=2 * (count * (total + width) * inner + total * width),
            transcendentals=0,
        ),
        name="sum_nt",
    )(*map(far, lefts), *map(far, rights), *before)


def spread_kernel(count, in_ref, *out_refs):
    blocks = in_ref.shape[0]
    piece = out_refs[0].shape[1] // blocks
    for v in range(count):
        for i in range(blocks):
            out_refs[v][:, i * piece : (i + 1) * piece] = in_ref[
                i : i + 1, v * piece : (v + 1) * piece
            ]


def spread(vecs, count, width):
    return pl.pallas_call(
        functools.partial(spread_kernel, count),
        in_specs=[pl.BlockSpec(memory_space=pltpu.VMEM)],
        out_specs=[pl.BlockSpec(memory_space=pltpu.VMEM)] * count,
        out_shape=[jax.ShapeDtypeStruct((1, width), F32)] * count,
        name="spread",
    )(vecs)


def fetch_weights(core_ref, own, got, kept, sems):
    def fetch(sources):
        copies = [
            pltpu.make_async_copy(source, target, sems.at[i])
            for i, (source, target) in enumerate(zip(sources, kept))
        ]
        for copy in copies:
            copy.start()
        for copy in copies:
            copy.wait()

    @pl.when(core_ref[0] == 0)
    def _():
        fetch(own)

    @pl.when(core_ref[0] != 0)
    def _():
        fetch(got)


def feed_in_kernel(half, rows0, rows1, w1, bias_ref, rows_ref, act_ref, slope_ref):
    step = pl.program_id(0)
    rows = jnp.where(step < half, rows0[...], rows1[...])
    rows_ref[...] = rows
    pre = dot_nn(rows, w1[...]) + bias_ref[...]
    root = (2.0 / jnp.pi) ** 0.5
    square = pre * pre
    tanh = jnp.tanh(root * (pre + 0.044715 * (pre * square)))
    gate = 0.5 * (1.0 + tanh)
    slope = gate + 0.5 * pre * (1.0 - tanh * tanh) * (root * (1.0 + 3 * 0.044715 * square))
    act_ref[...] = (pre * gate).astype(BF16)
    slope_ref[...] = slope.astype(BF16)


def feed_in(rows, weight, bias, tile=SEQ):
    count, width = rows[0].shape
    ff = weight.shape[1]
    half = count // tile
    step = lambda i: (i, 0)
    whole = lambda i: (0, 0)
    return pl.pallas_call(
        functools.partial(feed_in_kernel, half),
        grid=(2 * half,),
        in_specs=[
            pl.BlockSpec((tile, width), lambda i: (jnp.minimum(i, half - 1), 0)),
            pl.BlockSpec((tile, width), lambda i: (jnp.maximum(i - half, 0), 0)),
            pl.BlockSpec((width, ff), whole, pipeline_mode=pl.Buffered(1)),
            pl.BlockSpec((1, ff), whole),
        ],
        out_specs=[
            pl.BlockSpec((tile, width), step),
            pl.BlockSpec((tile, ff), step),
            pl.BlockSpec((tile, ff), step),
        ],
        out_shape=[
            jax.ShapeDtypeStruct((2 * count, width), BF16),
            jax.ShapeDtypeStruct((2 * count, ff), BF16),
            jax.ShapeDtypeStruct((2 * count, ff), BF16),
        ],
        compiler_params=pltpu.CompilerParams(vmem_limit_bytes=FEED_VMEM),
        cost_estimate=pl.CostEstimate(
            flops=4 * count * width * ff,
            bytes_accessed=2 * (width * ff + 4 * count * (width + ff)),
            transcendentals=2 * count * ff,
        ),
        name="feed_in",
    )(*rows, near(weight), bias)


def feed_out_kernel(
    half, core_ref, cot0, cot1, act_ref, slope_ref, w1, w2_own, w2_got,
    gpre_ref, out0, out1, grad0, grad1, sums_ref, w2, sems,
):
    step = pl.program_id(0)

    @pl.when(step == 0)
    def _():
        fetch_weights(core_ref, [w2_own], [w2_got], [w2], sems)

    first = step < half
    cot = jnp.where(first, cot0[...], cot1[...])
    grad_pre = dot_nn(cot, w2[...]) * slope_ref[...].astype(F32)
    sums = jnp.sum(grad_pre, axis=0, keepdims=True)
    grad_in = grad_pre.astype(BF16)
    gpre_ref[...] = grad_in
    grad = dot_nt(grad_in, w1[...]).astype(BF16)
    out = dot_nt(act_ref[...], w2[...]).astype(BF16)

    @pl.when(step == 0)
    def _():
        sums_ref[...] = sums

    @pl.when(step > 0)
    def _():
        sums_ref[...] += sums

    @pl.when(first)
    def _():
        out0[...] = out
        grad0[...] = grad

    @pl.when(jnp.logical_not(first))
    def _():
        out1[...] = out
        grad1[...] = grad


def feed_out(core, cots, act, slope, weights, tile=SEQ):
    count, width = cots[0].shape
    ff = act.shape[1]
    half = count // tile
    low = lambda i: (jnp.minimum(i, half - 1), 0)
    high = lambda i: (jnp.maximum(i - half, 0), 0)
    step = lambda i: (i, 0)
    anywhere = pl.BlockSpec(memory_space=pl.ANY)
    return pl.pallas_call(
        functools.partial(feed_out_kernel, half),
        grid=(2 * half,),
        in_specs=[
            pl.BlockSpec(memory_space=pltpu.SMEM),
            pl.BlockSpec((tile, width), low),
            pl.BlockSpec((tile, width), high),
            pl.BlockSpec((tile, ff), step),
            pl.BlockSpec((tile, ff), step),
        ]
        + [pl.BlockSpec((width, ff), lambda i: (0, 0), pipeline_mode=pl.Buffered(1))]
        + [anywhere] * 2,
        out_specs=[
            pl.BlockSpec((tile, ff), step),
            pl.BlockSpec((tile, width), low),
            pl.BlockSpec((tile, width), high),
            pl.BlockSpec((tile, width), low),
            pl.BlockSpec((tile, width), high),
            pl.BlockSpec((1, ff), lambda i: (0, 0)),
        ],
        out_shape=[jax.ShapeDtypeStruct((2 * count, ff), BF16)]
        + [pltpu.HBM((count, width), BF16)] * 4
        + [jax.ShapeDtypeStruct((1, ff), F32)],
        scratch_shapes=[pltpu.VMEM((width, ff), BF16), pltpu.SemaphoreType.DMA((1,))],
        compiler_params=pltpu.CompilerParams(vmem_limit_bytes=FEED_OUT_VMEM),
        cost_estimate=pl.CostEstimate(
            flops=12 * count * width * ff,
            bytes_accessed=2 * (2 * width * ff + 2 * count * (3 * width + 3 * ff)),
            transcendentals=0,
        ),
        name="feed_out",
    )(core, *cots, act, slope, near(weights[0]), far(weights[1]), weights[2])


def norm_back_kernel(count, *refs):
    grads, (rows_ref, cot_ref, gain_ref) = refs[:count], refs[count : count + 3]
    out_ref, *rounded_ref, sums_ref = refs[count + 3 :]
    grad = grads[0][...].astype(F32)
    for other in grads[1:]:
        grad += other[...].astype(F32)
    rows = rows_ref[...].astype(F32)
    center = rows - jnp.mean(rows, axis=-1, keepdims=True)
    spread = lax.rsqrt(jnp.mean(center * center, axis=-1, keepdims=True) + EPS)
    normed = center * spread
    cot = cot_ref[...].astype(F32)
    out = cot + norm_back(grad, normed, spread, gain_ref[...])
    out_ref[...] = out
    for ref in rounded_ref:
        ref[...] = out.astype(BF16)

    @pl.when(pl.program_id(0) == 0)
    def _():
        sums_ref[...] = jnp.zeros_like(sums_ref)

    for i, value in enumerate((grad * normed, grad, out, cot)):
        sums_ref[i : i + 1, :] += jnp.sum(value, axis=0, keepdims=True)


def norm_back_rows(grads, rows, cot, gain, rounded, tile=128):
    count, width = rows.shape
    step = pl.BlockSpec((tile, width), lambda i: (i, 0))
    extra = [pltpu.HBM((count, width), BF16)] if rounded else []
    return pl.pallas_call(
        functools.partial(norm_back_kernel, len(grads)),
        grid=(count // tile,),
        in_specs=[step] * (len(grads) + 2) + [pl.BlockSpec((1, width), lambda i: (0, 0))],
        out_specs=[step] * (1 + len(extra)) + [pl.BlockSpec((8, width), lambda i: (0, 0))],
        out_shape=[
            pltpu.HBM((count, width), F32),
            *extra,
            jax.ShapeDtypeStruct((8, width), F32),
        ],
        compiler_params=pltpu.CompilerParams(vmem_limit_bytes=16 << 20),
        cost_estimate=pl.CostEstimate(
            flops=30 * count * width,
            bytes_accessed=count * width * (2 * len(grads) + 12),
            transcendentals=count,
        ),
        name="norm_back",
    )(*map(far, grads), far(rows), far(cot), gain)


def norm_kernel(count, *refs):
    parts, (shift_ref, gain_ref, bias_ref) = refs[:count], refs[count : count + 3]
    rows_ref, out_ref = refs[count + 3 :]
    rows = parts[0][...].astype(F32) + shift_ref[...]
    for part in parts[1:]:
        rows += part[...].astype(F32)
    rows_ref[...] = rows
    out_ref[...] = norm_rows(rows, gain_ref[...], bias_ref[...])[0].astype(BF16)


def norm_sum(parts, shift, gain, bias, tile=128):
    count, width = parts[0].shape
    step = pl.BlockSpec((tile, width), lambda i: (i, 0))
    row = pl.BlockSpec((1, width), lambda i: (0, 0))
    return pl.pallas_call(
        functools.partial(norm_kernel, len(parts)),
        grid=(count // tile,),
        in_specs=[step] * len(parts) + [row] * 3,
        out_specs=[step, step],
        out_shape=[pltpu.HBM((count, width), F32), jax.ShapeDtypeStruct((count, width), BF16)],
        compiler_params=pltpu.CompilerParams(vmem_limit_bytes=16 << 20),
        cost_estimate=pl.CostEstimate(
            flops=12 * count * width,
            bytes_accessed=count * width * (2 * len(parts) + 6),
            transcendentals=count,
        ),
        name="norm_sum",
    )(*parts, shift, gain, bias)


def pack_kernel(where_ref, first_ref, second_ref, *refs):
    units, bias_ref, out_ref = refs[:-2], refs[-2], refs[-1]
    out_ref[...] = jnp.zeros_like(out_ref)
    width = first_ref.shape[1]
    for spot, ref, row in (
        (0, first_ref, 0), (1, second_ref, 0), (2, first_ref, 1),
        (3, second_ref, 2), (4, second_ref, 1), (5, second_ref, 3),
    ):
        out_ref[spot : spot + 1, :width] = ref[row : row + 1, :]
    core = where_ref[0]
    for n, unit in enumerate(units):
        lanes = unit.shape[1]
        spot = 7 + 2 * where_ref[2 + n]
        sums = jnp.concatenate([unit[0:1, :], unit[1:2, :]], axis=1)

        @pl.when(core == 0)
        def _():
            out_ref[pl.ds(spot, 1), : 2 * lanes] = sums

        @pl.when(core != 0)
        def _():
            out_ref[pl.ds(spot, 1), 2 * lanes : 4 * lanes] = sums

    out_ref[pl.ds(6 + 2 * where_ref[1], 1), : bias_ref.shape[1]] = bias_ref[...]


def pack_small(where, vectors, units, bias, spots):
    lanes = max(x.shape[1] for x in [*vectors, bias])
    rows = -(-(6 + 2 * spots) // 8) * 8
    return pl.pallas_call(
        pack_kernel,
        in_specs=[pl.BlockSpec(memory_space=pltpu.SMEM)]
        + [pl.BlockSpec(memory_space=pltpu.VMEM)] * (len(vectors) + len(units) + 1),
        out_specs=pl.BlockSpec(memory_space=pltpu.VMEM),
        out_shape=jax.ShapeDtypeStruct((rows, lanes), F32),
        name="pack_small",
    )(where, *vectors, *units, bias)


def make_body(ndp, nt):
    nz = ndp // 2
    bits = nt.bit_length() - 1
    top = nt // 2
    low = nt // 2

    def perm(move):
        pairs = []
        for d in range(ndp):
            for t in range(nt):
                d2, t2 = move(d, t)
                pairs.append((d * nt + t, d2 * nt + t2))
        return pairs

    def send(value, move):
        return lax.ppermute(value, AXES, perm(move))

    def swap_core(value):
        return send(value, lambda d, t: (d ^ 1, t))

    def swap_tensor(value, i):
        return send(value, lambda d, t: (d, t ^ i))

    def shift_z(value, k):
        return send(value, lambda d, t: ((d + 2 * k) % ndp, t))

    def stage(value, i):
        return send(
            value, lambda d, t: (d, t ^ ((1 << i) if d % 2 == 0 else (1 << (bits - 1 - i))))
        )

    def reverse_bits(p):
        return sum(((p >> i) & 1) << (bits - 1 - i) for i in range(bits))

    def swap_top(value):
        pairs = [(d * nt + t, d * nt + (t ^ top)) for d in range(1, ndp, 2) for t in range(nt)]
        return lax.ppermute(value, AXES, pairs)

    def gather_z(value, z):
        out = jnp.zeros((nz,) + value.shape, value.dtype)
        out = lax.dynamic_update_slice_in_dim(out, value[None], z, 0)
        for k in range(1, nz):
            got = shift_z(value, k)
            out = lax.dynamic_update_slice_in_dim(out, got[None], lax.rem(z - k + nz, nz), 0)
        return out

    def pick(selector, items):
        total = jnp.where(selector == 0, items[0], 0)
        for i in range(1, len(items)):
            total = total + jnp.where(selector == i, items[i], 0)
        return total

    def body(
        tokens, norm_gains, row_biases, w_qkv, head_bias, w_out, w_fc1, fc1_bias, w_fc2, cotangent
    ):
        d = lax.axis_index("dp")
        t = lax.axis_index("tensor")
        z, c = d // 2, d % 2
        core0 = c == 0
        _, width = tokens.shape
        block = w_qkv.shape[2]
        hh = block // 2
        part = w_qkv.shape[1]
        ff = w_fc1.shape[1]

        def by_core(zero, one):
            return jnp.where(core0, zero, one)

        w_out_t = w_out.T

        cols = Columns(hh)
        packed, heads = cols.packed, cols.heads
        wide = padded(ff)

        def half(h):
            sl = slice(h * hh, (h + 1) * hh)
            cols = [w_qkv[0][:, sl], w_qkv[1][:, sl], w_qkv[2][:, sl], w_out_t[:, sl]]
            return jnp.pad(jnp.concatenate(cols, axis=1), ((0, 0), (0, packed - 4 * hh)))

        gathered = lax.all_gather(jnp.stack([half(0), half(1)]), "dp", axis=1, tiled=True)
        others = range(1, low)
        cot_far = [swap_tensor(cotangent, i) for i in others]

        gain_count, shift_count = norm_gains.shape[0], row_biases.shape[0]
        vec_count = gain_count + shift_count
        piece = norm_gains.shape[1]
        small = jnp.concatenate(
            [norm_gains.reshape(-1), row_biases.reshape(-1), head_bias.reshape(-1), fc1_bias]
        )
        smalls = [small] + [swap_tensor(small, i) for i in range(1, nt)]
        vec_size = vec_count * piece
        vecs = jnp.stack([pick(t ^ i, [s[:vec_size] for s in smalls]) for i in range(nt)])
        vecs = gather_z(vecs, z)
        vecs_other = swap_core(vecs)
        vecs = jnp.stack([by_core(vecs, vecs_other), by_core(vecs_other, vecs)], axis=1)
        vecs = spread(vecs.reshape(nz * 2 * nt, vec_size), vec_count, width)
        gain_rows, shifts = vecs[:gain_count], vecs[gain_count:]
        head_biases = jnp.stack([s[vec_size : vec_size + 2 * block] for s in smalls])
        turned = jnp.stack(
            [smalls[reverse_bits(p)][vec_size : vec_size + 2 * block] for p in range(nt)]
        )
        unit_bias = by_core(head_biases, turned).reshape(nt, 2, 2, hh)
        unit_bias = by_core(unit_bias[:, :, 0], unit_bias[:, :, 1])
        unit_bias = jnp.concatenate(
            [
                unit_bias[:, 0],
                jnp.zeros((nt, hh), F32),
                unit_bias[:, 1],
                jnp.zeros((nt, cols.three - 3 * hh), F32),
            ],
            axis=1,
        ).reshape(nt, 1, cols.three)
        scale = jnp.where(jnp.arange(cols.three) < hh, HD ** (-0.5), 1.0).astype(F32)
        scale = scale.reshape(1, cols.three)
        ff_bias = by_core(smalls[0][vec_size + 2 * block :], smalls[top][vec_size + 2 * block :])
        ff_bias = jnp.pad(ff_bias, (0, wide - ff)).reshape(1, wide)

        inputs_f = tokens.astype(F32)
        first = norm_rows(inputs_f, gain_rows[0], shifts[0])[0].astype(BF16)
        first_chip = jnp.concatenate([first, swap_core(first)], axis=0)

        cots = [(g, swap_core(g)) for g in [cotangent, *cot_far]]
        early = (first_chip, unit_bias, ff_bias)
        attn_w = [lax.dynamic_index_in_dim(tie(gathered, *early), c, 0, keepdims=False)]
        saved = [attend(cols, first_chip, attn_w[0], scale, unit_bias[0])]
        cot_rows = [jnp.concatenate([tie(g, saved[0][1]), o], axis=0) for g, o in cots]
        for i in range(bits):
            sent = list(attn_w)
            if i:
                sent[-1] = tie(sent[-1], *cot_rows)
            attn_w = attn_w + [stage(b, i) for b in sent]

        def gather_ff(own):
            return lax.all_gather(
                jnp.pad(own, ((0, 0), (0, wide - ff))), "dp", axis=0, tiled=True
            )

        fc1_own, fc2_own = gather_ff(w_fc1), gather_ff(tie(w_fc2.T, *vecs))

        for p in range(1, nt):
            before = None
            if p == nt - 1:
                before = ([s[1] for s in saved], attn_w[:p])
            saved.append(attend(cols, first_chip, attn_w[p], scale, unit_bias[p], before))
        attn_mine, attn_other = saved[-1][3:]
        fc1_got = swap_top(tie(fc1_own, attn_w[nt - 1], attn_w[nt - 2]))
        fc2_got = swap_top(fc2_own)
        hidden_one, second = norm_sum(
            [tokens, attn_mine, swap_core(attn_other)], shifts[1], gain_rows[1], shifts[2]
        )

        core = c.astype(jnp.int32).reshape(1)
        second_far = [swap_tensor(second, i) for i in others]
        fc1 = by_core(fc1_own, fc1_got)
        ins = [None] * low
        ins[0] = feed_in((second, swap_core(second)), fc1, ff_bias)
        grad_fc2_t = dot_tn(cot_rows[0], ins[0][1])
        for i, rows_far in zip(others, second_far):
            rows_far = tie(rows_far, grad_fc2_t)
            ins[i] = feed_in((rows_far, swap_core(rows_far)), fc1, ff_bias)

        outs, grad_sums, pres, grad_fc1_bias = [None] * low, [None] * low, [None] * low, 0
        after = []
        for i in reversed(range(low)):
            act, slope = ins[i][1:]
            if i == 0 or i == low - 1:
                slope = tie(slope, *after)
            pres[i], out0, out1, grad0, grad1, sums = feed_out(
                core, cots[i], act, slope, (fc1, fc2_own, fc2_got)
            )
            grad_fc1_bias = grad_fc1_bias + sums
            got = swap_core(grad1)
            got_out = swap_core(out1).astype(F32)
            if i:
                grad_fc2_t = grad_fc2_t + dot_tn(cot_rows[i], tie(ins[i][1], pres[i]))
                got = tie(got, grad_fc2_t)
            if i:
                got = (grad0.astype(F32) + got.astype(F32)).astype(BF16)
            grad_sums[i] = got
            grad_near = grad0
            if i == 1:
                grad_fc2_t = tie(grad_fc2_t, grad_sums[i]).astype(BF16)
            outs[i] = out0.astype(F32) + got_out
            if i:
                outs[i] = tie(outs[i].astype(BF16), grad_sums[i])
            after = [grad_sums[i], grad_fc2_t, outs[i]]
        got_fc2 = swap_top(grad_fc2_t)
        grad_fc1 = 0
        for i in reversed(range(low)):
            grad_fc1 = grad_fc1 + dot_tn(ins[i][0], tie(pres[i], grad_sums[0]))
        grad_fc1 = grad_fc1.astype(BF16)
        got_fc1 = swap_top(grad_fc1)

        def scatter_ff(partial):
            own = lax.psum_scatter(partial, "dp", scatter_dimension=0, tiled=True)
            return lax.optimization_barrier(own)[:, :ff].astype(F32)

        grad_fc2_t = by_core(grad_fc2_t, tie(got_fc2, grad_fc1))
        grad_fc2_own = scatter_ff(grad_fc2_t).T

        grad_second = [grad_near, grad_sums[0]]
        for i in others:
            got = swap_tensor(grad_sums[i], i)
            grad_second.append(tie(got, grad_fc1, grad_fc2_t))
        mlp_out = outs[0]
        for i in others:
            mlp_out = mlp_out + swap_tensor(outs[i], i).astype(F32)

        grad_hidden, hidden_in, second_sums = norm_back_rows(
            grad_second, hidden_one, cotangent, gain_rows[1], True
        )
        hidden_pair = (hidden_in, swap_core(hidden_in))
        back, after = {}, None
        grad_w = [None] * nt
        got_w = {}
        for p in reversed(range(nt)):
            qkv, mix, lse = saved[p][:3]
            if after is not None:
                lse = tie(lse, *after)
            come = sorted((q for q in got_w if got_w[q][0] == p and (p or q > 1)), reverse=True)
            extra = [got_w[q][1] for q in come]
            back[p] = attend_back(cols, hidden_pair, first_chip, attn_w[p], qkv, mix, lse, extra)
            value = back[p][1]
            grad_w[p] = value
            after = [value]
            if p == 1:
                parts = [q for q in range(nt) if q > 1]
                first_part = sum_nt(
                    [tie(back[q][0], value) for q in parts], [attn_w[q] for q in parts]
                )
                after = [value, first_part[0]]
            if p == nt - 2:
                grad_fc1 = by_core(grad_fc1, tie(got_fc1, value))
                grad_fc1_own = scatter_ff(grad_fc1)
                after = [value, grad_fc1]
            if p == 0:
                break
            i = p.bit_length() - 1
            got_w[p] = (p - (1 << i), stage(value, i))
        grad_w = [(grad_w[0].astype(F32) + got_w[1][1].astype(F32)).astype(BF16)]
        first_mine, first_other = sum_nt(
            [tie(back[q][0], grad_w[0]) for q in (1, 0)], attn_w[1::-1], first_part
        )
        own_half = lax.psum_scatter(
            grad_w[0],
            "dp",
            scatter_dimension=0,
            axis_index_groups=[list(range(0, ndp, 2)), list(range(1, ndp, 2))],
            tiled=True,
        )
        own_half = tie(own_half, grad_fc1_own, grad_fc2_own).reshape(2, part, packed)
        kept = by_core(own_half[0], own_half[1]).astype(F32)
        got = swap_core(by_core(own_half[1], own_half[0])).astype(F32)
        halves = [by_core(kept, got), by_core(got, kept)]
        grad_qkv_own = jnp.stack(
            [
                jnp.concatenate([g[:, k * hh : (k + 1) * hh] for g in halves], axis=1)
                for k in range(3)
            ]
        )
        grad_out_own = jnp.concatenate([g[:, 3 * hh : 4 * hh] for g in halves], axis=1).T

        grad_tokens, first_sums = norm_back_rows(
            [first_mine, swap_core(first_other)], tokens, grad_hidden, gain_rows[0], False
        )
        output = hidden_one + tie(mlp_out, grad_w[0]) + shifts[3]

        spots = [by_core(t ^ p, t ^ reverse_bits(p)) for p in range(nt)]
        where = jnp.stack([c, by_core(t, t ^ top)] + spots).astype(jnp.int32)
        total = pack_small(
            where,
            [first_sums, second_sums],
            [back[p][2] for p in range(nt)],
            grad_fc1_bias,
            nt,
        )
        total = functools.reduce(jnp.add, [swap_tensor(total, i) for i in range(1, nt)], total)
        total = tie(total, grad_tokens)
        total = functools.reduce(jnp.add, [shift_z(total, k) for k in range(1, nz)], total)
        total = tie(total, output, grad_fc1_own, grad_fc2_own, grad_qkv_own, grad_out_own)
        total = total + swap_core(total)
        own = lax.dynamic_slice_in_dim(
            total[:vec_count, :width], (d * nt + t) * piece, piece, axis=1
        )
        mine = lax.dynamic_slice_in_dim(total, 6 + 2 * t, 2, axis=0)
        bias_total = mine[0, :ff]
        units = mine[1, : 4 * heads * LANES].reshape(2, 2, heads, LANES)[:, :, :, :HD]
        head_total = units.transpose(1, 0, 2, 3).reshape(2, block)
        return (
            output,
            grad_tokens,
            own[:gain_count],
            own[gain_count:],
            grad_qkv_own,
            head_total,
            grad_out_own,
            grad_fc1_own,
            bias_total,
            grad_fc2_own,
        )

    return body


def solution(mesh):
    in_specs = (
        P(("dp", "tensor"), None),
        P(None, ("dp", "tensor")),
        P(None, ("dp", "tensor")),
        P(None, "dp", "tensor"),
        P(None, "tensor"),
        P("tensor", "dp"),
        P("dp", "tensor"),
        P("tensor"),
        P("tensor", "dp"),
        P(("dp", "tensor"), None),
    )
    out_specs = (
        P(("dp", "tensor"), None),
        P(("dp", "tensor"), None),
        P(None, ("dp", "tensor")),
        P(None, ("dp", "tensor")),
        P(None, "dp", "tensor"),
        P(None, "tensor"),
        P("tensor", "dp"),
        P("dp", "tensor"),
        P("tensor"),
        P("tensor", "dp"),
    )
    body = make_body(mesh.shape["dp"], mesh.shape["tensor"])

    return jax.shard_map(body, mesh=mesh, in_specs=in_specs, out_specs=out_specs, check_vma=False)
```

```python
import functools

import jax
import jax.numpy as jnp
from jax import lax
from jax.experimental import pallas as pl
from jax.experimental.pallas import tpu as pltpu
from jax.sharding import PartitionSpec as P


HD = 72
SEQ = 256
EPS = 1e-06
F32 = jnp.float32
BF16 = jnp.bfloat16
AXES = ("dp", "tensor")


def norm_rows(values, gain_row, shifts):
    center = values - jnp.mean(values, axis=-1, keepdims=True)
    spread = lax.rsqrt(jnp.mean(center * center, axis=-1, keepdims=True) + EPS)
    normed = center * spread
    return (normed * gain_row + shifts, normed, spread)


def norm_back(grad_rows, normed, spread, gain_row):
    scaled = grad_rows * gain_row
    return spread * (
        scaled
        - jnp.mean(scaled, axis=-1, keepdims=True)
        - normed * jnp.mean(scaled * normed, axis=-1, keepdims=True)
    )


def tie(value, *others):
    return lax.optimization_barrier((value, *others))[0]


def dot_nn(a, b):
    return lax.dot_general(a, b, (((1,), (0,)), ((), ())), preferred_element_type=F32)


def dot_nt(a, b):
    return lax.dot_general(a, b, (((1,), (1,)), ((), ())), preferred_element_type=F32)


def dot_tn(a, b):
    return lax.dot_general(a, b, (((0,), (0,)), ((), ())), preferred_element_type=F32)


LANES = 128
ATTEND_VMEM = 22 << 20
BACK_VMEM = 30 << 20
FEED_VMEM = 18 << 20
FEED_OUT_VMEM = 24 << 20
SUM_VMEM = 20 << 20


def far(x):
    return pltpu.with_memory_space_constraint(x, pltpu.HBM)


def near(x):
    return pltpu.with_memory_space_constraint(x, pltpu.VMEM)


def padded(size):
    return -(-size // LANES) * LANES


class Columns:
    def __init__(self, hh):
        self.hh = hh
        self.heads = hh // HD
        self.packed = padded(4 * hh)
        self.three = padded(3 * hh + LANES - HD)
        self.low = 3 * hh // LANES * LANES
        self.window = self.packed - self.low
        self.shift = 3 * hh - self.low


def cut(array, start):
    lane = lax.broadcasted_iota(jnp.int32, (1, LANES), 1)
    piece = array[:, start : start + LANES]
    return jnp.where(lane < HD, piece, jnp.zeros_like(piece))


def place(pieces, before, width):
    rows = pieces[0].shape[0]
    parts = [piece[:, :HD] for piece in pieces]
    if before:
        parts.insert(0, jnp.zeros((rows, before), pieces[0].dtype))
    after = width - before - HD * len(pieces)
    if after:
        parts.append(jnp.zeros((rows, after), pieces[0].dtype))
    return jnp.concatenate(parts, axis=1)


def attend_kernel(cols, images, before, rows_ref, w_ref, scale_ref, bias_ref, *refs):
    lefts, rights = refs[:before], refs[before : 3 * before + 2]
    outs = refs[3 * before + 2 :] if before else refs
    qkv_ref, mixed_ref, lse_ref = outs[:3]
    heads, hh = cols.heads, cols.hh
    proj = dot_nn(rows_ref[...], w_ref[...])
    qkv = ((proj + bias_ref[...]) * scale_ref[...]).astype(BF16)
    qkv_ref[...] = qkv
    units = [(m, h) for m in range(images) for h in range(heads)]

    def unit(kind, m, h):
        return cut(qkv[m * SEQ : (m + 1) * SEQ], kind * hh + h * HD)

    scores = [dot_nt(unit(0, m, h), unit(1, m, h)) for m, h in units]
    tops = [jnp.max(s, axis=-1, keepdims=True) for s in scores]
    exps = [jnp.exp(s - top) for s, top in zip(scores, tops)]
    sums = [jnp.sum(e, axis=-1, keepdims=True) for e in exps]
    probs = [(e * (1.0 / total)).astype(BF16) for e, total in zip(exps, sums)]
    mixed = [dot_nn(p, unit(2, m, h)).astype(BF16) for (m, h), p in zip(units, probs)]
    for m in range(images):
        rows = slice(m * SEQ, (m + 1) * SEQ)
        group = slice(m * heads, (m + 1) * heads)
        mixed_ref[rows, :] = place(mixed[group], cols.shift, cols.window)
        lse = [top + jnp.log(total) for top, total in zip(tops[group], sums[group])]
        lane = lax.broadcasted_iota(jnp.int32, (1, LANES), 1)
        wide = jnp.broadcast_to(lse[0], (SEQ, LANES))
        for h in range(1, heads):
            wide = jnp.where(lane == h, lse[h], wide)
        lse_ref[rows, :] = wide
    if len(outs) == 3:
        return
    mine_ref, other_ref = outs[3:]
    total = 0.0
    for n, left in enumerate([*lefts, mixed_ref]):
        right = jnp.concatenate([rights[2 * n][...], rights[2 * n + 1][...]], axis=1)
        total += dot_nt(left[...], right)
    value = total.astype(BF16)

    @pl.when(pl.program_id(0) == 0)
    def _():
        other_ref[...] = value

    @pl.when(pl.program_id(0) != 0)
    def _():
        mine_ref[...] = value


def attend(cols, rows, weight, scale, bias, before=None):
    total, width = rows.shape
    last = before is not None
    mixeds, weights = before if last else ((), ())
    tile = total // 2
    images = tile // SEQ
    turn = (lambda i: (lax.rem(i + 1, 2), 0)) if last else (lambda i: (i, 0))
    whole = lambda i: (0, 0)
    block = cols.low // LANES
    assert not last or cols.window == 2 * LANES
    rights = [w for w in [*weights, weight] for _ in range(2)] if last else []
    out_specs = [
        pl.BlockSpec((tile, cols.three), turn),
        pl.BlockSpec((tile, cols.window), turn),
        pl.BlockSpec((tile, LANES), turn),
    ]
    out_shape = [
        pltpu.HBM((total, cols.three), BF16),
        pltpu.HBM((total, cols.window), BF16),
        pltpu.HBM((total, LANES), F32),
    ]
    if last:
        out_specs += [pl.BlockSpec((tile, width), whole)] * 2
        out_shape += [jax.ShapeDtypeStruct((tile, width), BF16), pltpu.HBM((tile, width), BF16)]
    return pl.pallas_call(
        functools.partial(attend_kernel, cols, images, len(mixeds)),
        grid=(2,),
        in_specs=[
            pl.BlockSpec((tile, width), turn),
            pl.BlockSpec((width, cols.three), whole),
            pl.BlockSpec(scale.shape, whole),
            pl.BlockSpec(bias.shape, whole),
        ]
        + [pl.BlockSpec((tile, cols.window), turn)] * len(mixeds)
        + [
            pl.BlockSpec((width, LANES), lambda i, j=n % 2: (0, block + j))
            for n in range(len(rights))
        ],
        out_specs=out_specs,
        out_shape=out_shape,
        compiler_params=pltpu.CompilerParams(vmem_limit_bytes=ATTEND_VMEM),
        cost_estimate=pl.CostEstimate(
            flops=2 * total * width * cols.packed + 4 * total * SEQ * LANES * cols.heads,
            bytes_accessed=2 * (total * (width + 4 * cols.hh) + weight.size),
            transcendentals=total * SEQ * cols.heads,
        ),
        name="attend",
    )(far(rows), weight, scale, bias, *[far(m) for m in mixeds], *rights)


def attend_back_kernel(
    cols, images, extras, own_ref, other_hbm, rows_ref, w0_ref, w1_ref, qkv_ref, mixed_ref,
    lse_ref, *refs
):
    extra_hbm = refs[:extras]
    proj_ref, gw_ref, sums_ref, acc, grad, other, sems = refs[extras : extras + 7]
    extra = refs[extras + 7 :]
    heads, hh = cols.heads, cols.hh
    step = pl.program_id(0)
    copies = [pltpu.make_async_copy(other_hbm, other, sems.at[0])] + [
        pltpu.make_async_copy(source, target, sems.at[1 + i])
        for i, (source, target) in enumerate(zip(extra_hbm, extra))
    ]

    @pl.when(step == 0)
    def _():
        for copy in copies:
            copy.start()
        grad[...] = own_ref[...]

    @pl.when(step != 0)
    def _():
        copies[0].wait()
        grad[...] = other[...]

    gh = grad[...]
    gmix = dot_nn(gh, jnp.concatenate([w0_ref[...], w1_ref[...]], axis=1)).astype(BF16)
    units = [(m, h) for m in range(images) for h in range(heads)]

    def unit(kind, m, h):
        return cut(qkv_ref[m * SEQ : (m + 1) * SEQ, :], kind * hh + h * HD)

    query = [unit(0, m, h) for m, h in units]
    keys = [unit(1, m, h) for m, h in units]
    vals = [unit(2, m, h) for m, h in units]
    gm = [cut(gmix[m * SEQ : (m + 1) * SEQ], cols.shift + h * HD) for m, h in units]
    lse = [lse_ref[m * SEQ : (m + 1) * SEQ, h : h + 1] for m, h in units]
    probs = [jnp.exp(dot_nt(q, k) - top) for q, k, top in zip(query, keys, lse)]
    dprobs = [dot_nt(g, v) for g, v in zip(gm, vals)]
    dots = [jnp.sum(p * dp, axis=-1, keepdims=True) for p, dp in zip(probs, dprobs)]
    dscores = [(p * (dp - dt)).astype(BF16) for p, dp, dt in zip(probs, dprobs, dots)]
    grads = [
        (
            dot_nn(dscores[n], keys[n]) * HD ** (-0.5),
            dot_tn(dscores[n], query[n]),
            dot_tn(probs[n].astype(BF16), gm[n]),
        )
        for n in range(len(units))
    ]
    sums = [[0.0] * heads for _ in range(2)]
    for n, (m, h) in enumerate(units):
        for row, kind in enumerate((0, 2)):
            sums[row][h] = sums[row][h] + jnp.sum(grads[n][kind], axis=0, keepdims=True)
    sums = jnp.concatenate([jnp.concatenate(s, axis=1) for s in sums], axis=0)
    for m in range(images):
        pieces = [
            grads[m * heads + h][kind].astype(BF16) for kind in range(3) for h in range(heads)
        ]
        proj_ref[m * SEQ : (m + 1) * SEQ, :] = place(pieces, 0, cols.three)
    gw_qkv = dot_tn(rows_ref[...], proj_ref[...])
    gw_out = dot_tn(gh, mixed_ref[...])

    @pl.when(step == 0)
    def _():
        acc[...] = jnp.zeros_like(acc)
        sums_ref[...] = sums

    @pl.when(step > 0)
    def _():
        sums_ref[...] += sums

    acc[:, : cols.three] += gw_qkv
    acc[:, cols.low :] += gw_out

    @pl.when(step != 0)
    def _():
        total = acc[...]
        for i in range(extras):
            copies[1 + i].wait()
            total += extra[i][...].astype(F32)
        gw_ref[...] = total.astype(BF16)


def attend_back(cols, grad_rows, rows, weight, qkv, mixed, lse, extra):
    total, width = rows.shape
    tile = total // 2
    images = tile // SEQ
    step = lambda i: (i, 0)
    whole = lambda i: (0, 0)
    lanes = cols.heads * LANES
    block = cols.low // LANES
    assert cols.window == 2 * LANES
    anywhere = pl.BlockSpec(memory_space=pl.ANY)
    own, other = grad_rows
    return pl.pallas_call(
        functools.partial(attend_back_kernel, cols, images, len(extra)),
        grid=(2,),
        in_specs=[
            pl.BlockSpec((tile, width), whole),
            anywhere,
            pl.BlockSpec((tile, width), step),
            pl.BlockSpec((width, LANES), lambda i: (0, block)),
            pl.BlockSpec((width, LANES), lambda i: (0, block + 1)),
            pl.BlockSpec((tile, cols.three), step),
            pl.BlockSpec((tile, cols.window), step),
            pl.BlockSpec((tile, LANES), step),
        ]
        + [anywhere] * len(extra),
        out_specs=[
            pl.BlockSpec((tile, cols.three), step),
            pl.BlockSpec(weight.shape, whole),
            pl.BlockSpec((2, lanes), whole),
        ],
        out_shape=[
            pltpu.HBM((total, cols.three), BF16),
            pltpu.HBM(weight.shape, BF16),
            jax.ShapeDtypeStruct((2, lanes), F32),
        ],
        scratch_shapes=[
            pltpu.VMEM(weight.shape, F32),
            pltpu.VMEM((tile, width), BF16),
            pltpu.VMEM((tile, width), BF16),
            pltpu.SemaphoreType.DMA((1 + len(extra),)),
        ]
        + [pltpu.VMEM(weight.shape, BF16)] * len(extra),
        compiler_params=pltpu.CompilerParams(vmem_limit_bytes=BACK_VMEM),
        cost_estimate=pl.CostEstimate(
            flops=2 * total * width * (cols.packed + cols.window) + 10 * total * SEQ * lanes,
            bytes_accessed=2 * (2 * total * width + 7 * total * cols.hh + 2 * weight.size),
            transcendentals=total * SEQ * cols.heads,
        ),
        name="attend_back",
    )(
        far(own), far(other), far(rows), far(weight), far(weight), far(qkv), far(mixed), far(lse),
        *map(far, extra),
    )


def sum_nt_kernel(count, *refs):
    lefts, rights = refs[:count], refs[count : 2 * count]
    before, (mine_ref, other_ref) = refs[2 * count : -2], refs[-2:]
    total = dot_nt(lefts[0][...], rights[0][...])
    for left, right in zip(lefts[1:], rights[1:]):
        total += dot_nt(left[...], right[...])
    half = pl.num_programs(0) // 2

    def store(target, source):
        value = total + source[0][...].astype(F32) if source else total
        target[...] = value.astype(BF16)

    @pl.when(pl.program_id(0) < half)
    def _():
        store(other_ref, before[1:])

    @pl.when(pl.program_id(0) >= half)
    def _():
        store(mine_ref, before[:1])


def sum_nt(lefts, rights, before=(), tile=SEQ):
    count = len(lefts)
    total, inner = lefts[0].shape
    width = rights[0].shape[0]
    half = total // 2 // tile
    rows_specs = [
        pl.BlockSpec((tile, width), lambda i: (jnp.maximum(i - half, 0), 0)),
        pl.BlockSpec((tile, width), lambda i: (jnp.minimum(i, half - 1), 0)),
    ]
    return pl.pallas_call(
        functools.partial(sum_nt_kernel, count),
        grid=(2 * half,),
        in_specs=[pl.BlockSpec((tile, inner), lambda i: (lax.rem(i + half, 2 * half), 0))] * count
        + [
            pl.BlockSpec((width, inner), lambda i: (0, 0), pipeline_mode=pl.Buffered(1))
        ]
        * count
        + rows_specs[: len(before)],
        out_specs=rows_specs,
        out_shape=[
            jax.ShapeDtypeStruct((total // 2, width), BF16),
            pltpu.HBM((total // 2, width), BF16),
        ],
        compiler_params=pltpu.CompilerParams(vmem_limit_bytes=SUM_VMEM),
        cost_estimate=pl.CostEstimate(
            flops=2 * total * inner * width * count,
            bytes_accessed=2 * (count * (total + width) * inner + total * width),
            transcendentals=0,
        ),
        name="sum_nt",
    )(*map(far, lefts), *map(far, rights), *before)


def spread_kernel(count, in_ref, *out_refs):
    blocks = in_ref.shape[0]
    piece = out_refs[0].shape[1] // blocks
    for v in range(count):
        for i in range(blocks):
            out_refs[v][:, i * piece : (i + 1) * piece] = in_ref[
                i : i + 1, v * piece : (v + 1) * piece
            ]


def spread(vecs, count, width):
    return pl.pallas_call(
        functools.partial(spread_kernel, count),
        in_specs=[pl.BlockSpec(memory_space=pltpu.VMEM)],
        out_specs=[pl.BlockSpec(memory_space=pltpu.VMEM)] * count,
        out_shape=[jax.ShapeDtypeStruct((1, width), F32)] * count,
        name="spread",
    )(vecs)


def fetch_weights(core_ref, own, got, kept, sems):
    def fetch(sources):
        copies = [
            pltpu.make_async_copy(source, target, sems.at[i])
            for i, (source, target) in enumerate(zip(sources, kept))
        ]
        for copy in copies:
            copy.start()
        for copy in copies:
            copy.wait()

    @pl.when(core_ref[0] == 0)
    def _():
        fetch(own)

    @pl.when(core_ref[0] != 0)
    def _():
        fetch(got)


def feed_in_kernel(half, rows0, rows1, w1, bias_ref, rows_ref, act_ref, slope_ref):
    step = pl.program_id(0)
    rows = jnp.where(step < half, rows0[...], rows1[...])
    rows_ref[...] = rows
    pre = dot_nn(rows, w1[...]) + bias_ref[...]
    root = (2.0 / jnp.pi) ** 0.5
    square = pre * pre
    tanh = jnp.tanh(root * (pre + 0.044715 * (pre * square)))
    gate = 0.5 * (1.0 + tanh)
    slope = gate + 0.5 * pre * (1.0 - tanh * tanh) * (root * (1.0 + 3 * 0.044715 * square))
    act_ref[...] = (pre * gate).astype(BF16)
    slope_ref[...] = slope.astype(BF16)


def feed_in(rows, weight, bias, tile=SEQ):
    count, width = rows[0].shape
    ff = weight.shape[1]
    half = count // tile
    step = lambda i: (i, 0)
    whole = lambda i: (0, 0)
    return pl.pallas_call(
        functools.partial(feed_in_kernel, half),
        grid=(2 * half,),
        in_specs=[
            pl.BlockSpec((tile, width), lambda i: (jnp.minimum(i, half - 1), 0)),
            pl.BlockSpec((tile, width), lambda i: (jnp.maximum(i - half, 0), 0)),
            pl.BlockSpec((width, ff), whole, pipeline_mode=pl.Buffered(1)),
            pl.BlockSpec((1, ff), whole),
        ],
        out_specs=[
            pl.BlockSpec((tile, width), step),
            pl.BlockSpec((tile, ff), step),
            pl.BlockSpec((tile, ff), step),
        ],
        out_shape=[
            jax.ShapeDtypeStruct((2 * count, width), BF16),
            jax.ShapeDtypeStruct((2 * count, ff), BF16),
            jax.ShapeDtypeStruct((2 * count, ff), BF16),
        ],
        compiler_params=pltpu.CompilerParams(vmem_limit_bytes=FEED_VMEM),
        cost_estimate=pl.CostEstimate(
            flops=4 * count * width * ff,
            bytes_accessed=2 * (width * ff + 4 * count * (width + ff)),
            transcendentals=2 * count * ff,
        ),
        name="feed_in",
    )(*rows, near(weight), bias)


def feed_out_kernel(
    half, core_ref, cot0, cot1, act_ref, slope_ref, w1, w2_own, w2_got,
    gpre_ref, out0, out1, grad0, grad1, sums_ref, w2, sems,
):
    step = pl.program_id(0)

    @pl.when(step == 0)
    def _():
        fetch_weights(core_ref, [w2_own], [w2_got], [w2], sems)

    first = step < half
    cot = jnp.where(first, cot0[...], cot1[...])
    grad_pre = dot_nn(cot, w2[...]) * slope_ref[...].astype(F32)
    sums = jnp.sum(grad_pre, axis=0, keepdims=True)
    grad_in = grad_pre.astype(BF16)
    gpre_ref[...] = grad_in
    grad = dot_nt(grad_in, w1[...]).astype(BF16)
    out = dot_nt(act_ref[...], w2[...]).astype(BF16)

    @pl.when(step == 0)
    def _():
        sums_ref[...] = sums

    @pl.when(step > 0)
    def _():
        sums_ref[...] += sums

    @pl.when(first)
    def _():
        out0[...] = out
        grad0[...] = grad

    @pl.when(jnp.logical_not(first))
    def _():
        out1[...] = out
        grad1[...] = grad


def feed_out(core, cots, act, slope, weights, tile=SEQ):
    count, width = cots[0].shape
    ff = act.shape[1]
    half = count // tile
    low = lambda i: (jnp.minimum(i, half - 1), 0)
    high = lambda i: (jnp.maximum(i - half, 0), 0)
    step = lambda i: (i, 0)
    anywhere = pl.BlockSpec(memory_space=pl.ANY)
    return pl.pallas_call(
        functools.partial(feed_out_kernel, half),
        grid=(2 * half,),
        in_specs=[
            pl.BlockSpec(memory_space=pltpu.SMEM),
            pl.BlockSpec((tile, width), low),
            pl.BlockSpec((tile, width), high),
            pl.BlockSpec((tile, ff), step),
            pl.BlockSpec((tile, ff), step),
        ]
        + [pl.BlockSpec((width, ff), lambda i: (0, 0), pipeline_mode=pl.Buffered(1))]
        + [anywhere] * 2,
        out_specs=[
            pl.BlockSpec((tile, ff), step),
            pl.BlockSpec((tile, width), low),
            pl.BlockSpec((tile, width), high),
            pl.BlockSpec((tile, width), low),
            pl.BlockSpec((tile, width), high),
            pl.BlockSpec((1, ff), lambda i: (0, 0)),
        ],
        out_shape=[jax.ShapeDtypeStruct((2 * count, ff), BF16)]
        + [jax.ShapeDtypeStruct((count, width), BF16)] * 4
        + [jax.ShapeDtypeStruct((1, ff), F32)],
        scratch_shapes=[pltpu.VMEM((width, ff), BF16), pltpu.SemaphoreType.DMA((1,))],
        compiler_params=pltpu.CompilerParams(vmem_limit_bytes=FEED_OUT_VMEM),
        cost_estimate=pl.CostEstimate(
            flops=12 * count * width * ff,
            bytes_accessed=2 * (2 * width * ff + 2 * count * (3 * width + 3 * ff)),
            transcendentals=0,
        ),
        name="feed_out",
    )(core, *cots, act, slope, near(weights[0]), far(weights[1]), weights[2])


def norm_back_kernel(count, *refs):
    grads, (rows_ref, cot_ref, gain_ref) = refs[:count], refs[count : count + 3]
    out_ref, *rounded_ref, sums_ref = refs[count + 3 :]
    grad = grads[0][...].astype(F32)
    for other in grads[1:]:
        grad += other[...].astype(F32)
    rows = rows_ref[...].astype(F32)
    center = rows - jnp.mean(rows, axis=-1, keepdims=True)
    spread = lax.rsqrt(jnp.mean(center * center, axis=-1, keepdims=True) + EPS)
    normed = center * spread
    cot = cot_ref[...].astype(F32)
    out = cot + norm_back(grad, normed, spread, gain_ref[...])
    out_ref[...] = out
    for ref in rounded_ref:
        ref[...] = out.astype(BF16)

    @pl.when(pl.program_id(0) == 0)
    def _():
        sums_ref[...] = jnp.zeros_like(sums_ref)

    for i, value in enumerate((grad * normed, grad, out, cot)):
        sums_ref[i : i + 1, :] += jnp.sum(value, axis=0, keepdims=True)


def norm_back_rows(grads, rows, cot, gain, rounded, tile=128):
    count, width = rows.shape
    step = pl.BlockSpec((tile, width), lambda i: (i, 0))
    extra = [pltpu.HBM((count, width), BF16)] if rounded else []
    return pl.pallas_call(
        functools.partial(norm_back_kernel, len(grads)),
        grid=(count // tile,),
        in_specs=[step] * (len(grads) + 2) + [pl.BlockSpec((1, width), lambda i: (0, 0))],
        out_specs=[step] * (1 + len(extra)) + [pl.BlockSpec((8, width), lambda i: (0, 0))],
        out_shape=[
            pltpu.HBM((count, width), F32),
            *extra,
            jax.ShapeDtypeStruct((8, width), F32),
        ],
        compiler_params=pltpu.CompilerParams(vmem_limit_bytes=16 << 20),
        cost_estimate=pl.CostEstimate(
            flops=30 * count * width,
            bytes_accessed=count * width * (2 * len(grads) + 12),
            transcendentals=count,
        ),
        name="norm_back",
    )(*grads, far(rows), far(cot), gain)


def norm_kernel(count, *refs):
    parts, (shift_ref, gain_ref, bias_ref) = refs[:count], refs[count : count + 3]
    rows_ref, out_ref = refs[count + 3 :]
    rows = parts[0][...].astype(F32) + shift_ref[...]
    for part in parts[1:]:
        rows += part[...].astype(F32)
    rows_ref[...] = rows
    out_ref[...] = norm_rows(rows, gain_ref[...], bias_ref[...])[0].astype(BF16)


def norm_sum(parts, shift, gain, bias, tile=128):
    count, width = parts[0].shape
    step = pl.BlockSpec((tile, width), lambda i: (i, 0))
    row = pl.BlockSpec((1, width), lambda i: (0, 0))
    return pl.pallas_call(
        functools.partial(norm_kernel, len(parts)),
        grid=(count // tile,),
        in_specs=[step] * len(parts) + [row] * 3,
        out_specs=[step, step],
        out_shape=[pltpu.HBM((count, width), F32), jax.ShapeDtypeStruct((count, width), BF16)],
        compiler_params=pltpu.CompilerParams(vmem_limit_bytes=16 << 20),
        cost_estimate=pl.CostEstimate(
            flops=12 * count * width,
            bytes_accessed=count * width * (2 * len(parts) + 6),
            transcendentals=count,
        ),
        name="norm_sum",
    )(*parts, shift, gain, bias)


def pack_kernel(where_ref, first_ref, second_ref, *refs):
    units, bias_ref, out_ref = refs[:-2], refs[-2], refs[-1]
    out_ref[...] = jnp.zeros_like(out_ref)
    width = first_ref.shape[1]
    for spot, ref, row in (
        (0, first_ref, 0), (1, second_ref, 0), (2, first_ref, 1),
        (3, second_ref, 2), (4, second_ref, 1), (5, second_ref, 3),
    ):
        out_ref[spot : spot + 1, :width] = ref[row : row + 1, :]
    core = where_ref[0]
    for n, unit in enumerate(units):
        lanes = unit.shape[1]
        spot = 7 + 2 * where_ref[2 + n]
        sums = jnp.concatenate([unit[0:1, :], unit[1:2, :]], axis=1)

        @pl.when(core == 0)
        def _():
            out_ref[pl.ds(spot, 1), : 2 * lanes] = sums

        @pl.when(core != 0)
        def _():
            out_ref[pl.ds(spot, 1), 2 * lanes : 4 * lanes] = sums

    out_ref[pl.ds(6 + 2 * where_ref[1], 1), : bias_ref.shape[1]] = bias_ref[...]


def pack_small(where, vectors, units, bias, spots):
    lanes = max(x.shape[1] for x in [*vectors, bias])
    rows = -(-(6 + 2 * spots) // 8) * 8
    return pl.pallas_call(
        pack_kernel,
        in_specs=[pl.BlockSpec(memory_space=pltpu.SMEM)]
        + [pl.BlockSpec(memory_space=pltpu.VMEM)] * (len(vectors) + len(units) + 1),
        out_specs=pl.BlockSpec(memory_space=pltpu.VMEM),
        out_shape=jax.ShapeDtypeStruct((rows, lanes), F32),
        name="pack_small",
    )(where, *vectors, *units, bias)


def make_body(ndp, nt):
    nz = ndp // 2
    bits = nt.bit_length() - 1
    top = nt // 2
    low = nt // 2

    def perm(move):
        pairs = []
        for d in range(ndp):
            for t in range(nt):
                d2, t2 = move(d, t)
                pairs.append((d * nt + t, d2 * nt + t2))
        return pairs

    def send(value, move):
        return lax.ppermute(value, AXES, perm(move))

    def swap_core(value):
        return send(value, lambda d, t: (d ^ 1, t))

    def swap_tensor(value, i):
        return send(value, lambda d, t: (d, t ^ i))

    def shift_z(value, k):
        return send(value, lambda d, t: ((d + 2 * k) % ndp, t))

    def stage(value, i):
        return send(
            value, lambda d, t: (d, t ^ ((1 << i) if d % 2 == 0 else (1 << (bits - 1 - i))))
        )

    def reverse_bits(p):
        return sum(((p >> i) & 1) << (bits - 1 - i) for i in range(bits))

    def swap_top(value):
        pairs = [(d * nt + t, d * nt + (t ^ top)) for d in range(1, ndp, 2) for t in range(nt)]
        return lax.ppermute(value, AXES, pairs)

    def gather_z(value, z):
        out = jnp.zeros((nz,) + value.shape, value.dtype)
        out = lax.dynamic_update_slice_in_dim(out, value[None], z, 0)
        for k in range(1, nz):
            got = shift_z(value, k)
            out = lax.dynamic_update_slice_in_dim(out, got[None], lax.rem(z - k + nz, nz), 0)
        return out

    def pick(selector, items):
        total = jnp.where(selector == 0, items[0], 0)
        for i in range(1, len(items)):
            total = total + jnp.where(selector == i, items[i], 0)
        return total

    def body(
        tokens, norm_gains, row_biases, w_qkv, head_bias, w_out, w_fc1, fc1_bias, w_fc2, cotangent
    ):
        d = lax.axis_index("dp")
        t = lax.axis_index("tensor")
        z, c = d // 2, d % 2
        core0 = c == 0
        _, width = tokens.shape
        block = w_qkv.shape[2]
        hh = block // 2
        part = w_qkv.shape[1]
        ff = w_fc1.shape[1]

        def by_core(zero, one):
            return jnp.where(core0, zero, one)

        w_out_t = w_out.T

        cols = Columns(hh)
        packed, heads = cols.packed, cols.heads
        wide = padded(ff)

        def half(h):
            sl = slice(h * hh, (h + 1) * hh)
            cols = [w_qkv[0][:, sl], w_qkv[1][:, sl], w_qkv[2][:, sl], w_out_t[:, sl]]
            return jnp.pad(jnp.concatenate(cols, axis=1), ((0, 0), (0, packed - 4 * hh)))

        gathered = lax.all_gather(jnp.stack([half(0), half(1)]), "dp", axis=1, tiled=True)
        others = range(1, low)
        cot_far = [swap_tensor(cotangent, i) for i in others]

        gain_count, shift_count = norm_gains.shape[0], row_biases.shape[0]
        vec_count = gain_count + shift_count
        piece = norm_gains.shape[1]
        small = jnp.concatenate(
            [norm_gains.reshape(-1), row_biases.reshape(-1), head_bias.reshape(-1), fc1_bias]
        )
        smalls = [small] + [swap_tensor(small, i) for i in range(1, nt)]
        vec_size = vec_count * piece
        vecs = jnp.stack([pick(t ^ i, [s[:vec_size] for s in smalls]) for i in range(nt)])
        vecs = gather_z(vecs, z)
        vecs_other = swap_core(vecs)
        vecs = jnp.stack([by_core(vecs, vecs_other), by_core(vecs_other, vecs)], axis=1)
        vecs = spread(vecs.reshape(nz * 2 * nt, vec_size), vec_count, width)
        gain_rows, shifts = vecs[:gain_count], vecs[gain_count:]
        head_biases = jnp.stack([s[vec_size : vec_size + 2 * block] for s in smalls])
        turned = jnp.stack(
            [smalls[reverse_bits(p)][vec_size : vec_size + 2 * block] for p in range(nt)]
        )
        unit_bias = by_core(head_biases, turned).reshape(nt, 2, 2, hh)
        unit_bias = by_core(unit_bias[:, :, 0], unit_bias[:, :, 1])
        unit_bias = jnp.concatenate(
            [
                unit_bias[:, 0],
                jnp.zeros((nt, hh), F32),
                unit_bias[:, 1],
                jnp.zeros((nt, cols.three - 3 * hh), F32),
            ],
            axis=1,
        ).reshape(nt, 1, cols.three)
        scale = jnp.where(jnp.arange(cols.three) < hh, HD ** (-0.5), 1.0).astype(F32)
        scale = scale.reshape(1, cols.three)
        ff_bias = by_core(smalls[0][vec_size + 2 * block :], smalls[top][vec_size + 2 * block :])
        ff_bias = jnp.pad(ff_bias, (0, wide - ff)).reshape(1, wide)

        inputs_f = tokens.astype(F32)
        first = norm_rows(inputs_f, gain_rows[0], shifts[0])[0].astype(BF16)
        first_chip = jnp.concatenate([first, swap_core(first)], axis=0)

        cots = [(g, swap_core(g)) for g in [cotangent, *cot_far]]
        early = (first_chip, unit_bias, ff_bias)
        attn_w = [lax.dynamic_index_in_dim(tie(gathered, *early), c, 0, keepdims=False)]
        saved = [attend(cols, first_chip, attn_w[0], scale, unit_bias[0])]
        cot_rows = [jnp.concatenate([tie(g, saved[0][1]), o], axis=0) for g, o in cots]
        for i in range(bits):
            sent = list(attn_w)
            if i:
                sent[-1] = tie(sent[-1], *cot_rows)
            attn_w = attn_w + [stage(b, i) for b in sent]

        def gather_ff(own):
            return lax.all_gather(
                jnp.pad(own, ((0, 0), (0, wide - ff))), "dp", axis=0, tiled=True
            )

        fc1_own, fc2_own = gather_ff(w_fc1), gather_ff(tie(w_fc2.T, *vecs))

        for p in range(1, nt):
            before = None
            if p == nt - 1:
                before = ([s[1] for s in saved], attn_w[:p])
            saved.append(attend(cols, first_chip, attn_w[p], scale, unit_bias[p], before))
        attn_mine, attn_other = saved[-1][3:]
        fc1_got = swap_top(tie(fc1_own, attn_w[nt - 1], attn_w[nt - 2]))
        fc2_got = swap_top(fc2_own)
        hidden_one, second = norm_sum(
            [tokens, attn_mine, swap_core(attn_other)], shifts[1], gain_rows[1], shifts[2]
        )

        core = c.astype(jnp.int32).reshape(1)
        second_far = [swap_tensor(second, i) for i in others]
        fc1 = by_core(fc1_own, fc1_got)
        ins = [None] * low
        ins[0] = feed_in((second, swap_core(second)), fc1, ff_bias)
        grad_fc2_t = dot_tn(cot_rows[0], ins[0][1])
        for i, rows_far in zip(others, second_far):
            rows_far = tie(rows_far, grad_fc2_t)
            ins[i] = feed_in((rows_far, swap_core(rows_far)), fc1, ff_bias)

        outs, grad_sums, pres, grad_fc1_bias = [None] * low, [None] * low, [None] * low, 0
        after = []
        for i in reversed(range(low)):
            act, slope = ins[i][1:]
            if i == 0 or i == low - 1:
                slope = tie(slope, *after)
            pres[i], out0, out1, grad0, grad1, sums = feed_out(
                core, cots[i], act, slope, (fc1, fc2_own, fc2_got)
            )
            grad_fc1_bias = grad_fc1_bias + sums
            got = swap_core(grad1)
            got_out = swap_core(out1).astype(F32)
            if i:
                grad_fc2_t = grad_fc2_t + dot_tn(cot_rows[i], tie(ins[i][1], pres[i]))
                got = tie(got, grad_fc2_t)
            if i:
                got = (grad0.astype(F32) + got.astype(F32)).astype(BF16)
            grad_sums[i] = got
            grad_near = grad0
            if i == 1:
                grad_fc2_t = tie(grad_fc2_t, grad_sums[i]).astype(BF16)
            outs[i] = out0.astype(F32) + got_out
            if i:
                outs[i] = tie(outs[i].astype(BF16), grad_sums[i])
            after = [grad_sums[i], grad_fc2_t, outs[i]]
        got_fc2 = swap_top(grad_fc2_t)
        grad_fc1 = 0
        for i in reversed(range(low)):
            grad_fc1 = grad_fc1 + dot_tn(ins[i][0], tie(pres[i], grad_sums[0]))
        grad_fc1 = grad_fc1.astype(BF16)
        got_fc1 = swap_top(grad_fc1)

        def scatter_ff(partial):
            own = lax.psum_scatter(partial, "dp", scatter_dimension=0, tiled=True)
            return lax.optimization_barrier(own)[:, :ff].astype(F32)

        grad_fc2_t = by_core(grad_fc2_t, tie(got_fc2, grad_fc1))
        grad_fc2_own = scatter_ff(grad_fc2_t).T

        grad_second = [grad_near, grad_sums[0]]
        for i in others:
            got = swap_tensor(grad_sums[i], i)
            grad_second.append(tie(got, grad_fc1, grad_fc2_t))
        mlp_out = outs[0]
        for i in others:
            mlp_out = mlp_out + swap_tensor(outs[i], i).astype(F32)

        grad_hidden, hidden_in, second_sums = norm_back_rows(
            grad_second, hidden_one, cotangent, gain_rows[1], True
        )
        hidden_pair = (hidden_in, swap_core(hidden_in))
        back, after = {}, None
        no_sum = jnp.zeros(attn_w[0].shape, BF16)
        grad_w = [None] * nt
        got_w = {}
        for p in reversed(range(nt)):
            qkv, mix, lse = saved[p][:3]
            if after is not None:
                lse = tie(lse, *after)
            come = sorted((q for q in got_w if got_w[q][0] == p and (p or q > 1)), reverse=True)
            extra = [got_w[q][1] for q in come] or [no_sum]
            back[p] = attend_back(cols, hidden_pair, first_chip, attn_w[p], qkv, mix, lse, extra)
            value = back[p][1]
            grad_w[p] = value
            after = [value]
            if p == 1:
                parts = [q for q in range(nt) if q > 1]
                first_part = sum_nt(
                    [tie(back[q][0], value) for q in parts], [attn_w[q] for q in parts]
                )
                after = [value, first_part[0]]
            if p == nt - 2:
                grad_fc1 = by_core(grad_fc1, tie(got_fc1, value))
                grad_fc1_own = scatter_ff(grad_fc1)
                after = [value, grad_fc1]
            if p == 0:
                break
            i = p.bit_length() - 1
            got_w[p] = (p - (1 << i), stage(value, i))
        grad_w = [(grad_w[0].astype(F32) + got_w[1][1].astype(F32)).astype(BF16)]
        first_mine, first_other = sum_nt(
            [tie(back[q][0], grad_w[0]) for q in (1, 0)], attn_w[1::-1], first_part
        )
        own_half = lax.psum_scatter(
            grad_w[0],
            "dp",
            scatter_dimension=0,
            axis_index_groups=[list(range(0, ndp, 2)), list(range(1, ndp, 2))],
            tiled=True,
        )
        own_half = tie(own_half, grad_fc1_own, grad_fc2_own).reshape(2, part, packed)
        kept = by_core(own_half[0], own_half[1]).astype(F32)
        got = swap_core(by_core(own_half[1], own_half[0])).astype(F32)
        halves = [by_core(kept, got), by_core(got, kept)]
        grad_qkv_own = jnp.stack(
            [
                jnp.concatenate([g[:, k * hh : (k + 1) * hh] for g in halves], axis=1)
                for k in range(3)
            ]
        )
        grad_out_own = jnp.concatenate([g[:, 3 * hh : 4 * hh] for g in halves], axis=1).T

        grad_tokens, first_sums = norm_back_rows(
            [first_mine, swap_core(first_other)], tokens, grad_hidden, gain_rows[0], False
        )

        spots = [by_core(t ^ p, t ^ reverse_bits(p)) for p in range(nt)]
        where = jnp.stack([c, by_core(t, t ^ top)] + spots).astype(jnp.int32)
        total = pack_small(
            where,
            [first_sums, second_sums],
            [back[p][2] for p in range(nt)],
            grad_fc1_bias,
            nt,
        )
        output = hidden_one + tie(mlp_out, total) + shifts[3]
        total = functools.reduce(jnp.add, [swap_tensor(total, i) for i in range(1, nt)], total)
        total = tie(total, grad_tokens, output)
        total = functools.reduce(jnp.add, [shift_z(total, k) for k in range(1, nz)], total)
        total = tie(total, output, grad_fc1_own, grad_fc2_own, grad_qkv_own, grad_out_own)
        total = total + swap_core(total)
        own = lax.dynamic_slice_in_dim(
            total[:vec_count, :width], (d * nt + t) * piece, piece, axis=1
        )
        mine = lax.dynamic_slice_in_dim(total, 6 + 2 * t, 2, axis=0)
        bias_total = mine[0, :ff]
        units = mine[1, : 4 * heads * LANES].reshape(2, 2, heads, LANES)[:, :, :, :HD]
        head_total = units.transpose(1, 0, 2, 3).reshape(2, block)
        return (
            output,
            grad_tokens,
            own[:gain_count],
            own[gain_count:],
            grad_qkv_own,
            head_total,
            grad_out_own,
            grad_fc1_own,
            bias_total,
            grad_fc2_own,
        )

    return body


def solution(mesh):
    in_specs = (
        P(("dp", "tensor"), None),
        P(None, ("dp", "tensor")),
        P(None, ("dp", "tensor")),
        P(None, "dp", "tensor"),
        P(None, "tensor"),
        P("tensor", "dp"),
        P("dp", "tensor"),
        P("tensor"),
        P("tensor", "dp"),
        P(("dp", "tensor"), None),
    )
    out_specs = (
        P(("dp", "tensor"), None),
        P(("dp", "tensor"), None),
        P(None, ("dp", "tensor")),
        P(None, ("dp", "tensor")),
        P(None, "dp", "tensor"),
        P(None, "tensor"),
        P("tensor", "dp"),
        P("dp", "tensor"),
        P("tensor"),
        P("tensor", "dp"),
    )
    body = make_body(mesh.shape["dp"], mesh.shape["tensor"])

    return jax.shard_map(body, mesh=mesh, in_specs=in_specs, out_specs=out_specs, check_vma=False)
```

```python
import functools

import jax
import jax.numpy as jnp
from jax import lax
from jax.experimental import pallas as pl
from jax.experimental.pallas import tpu as pltpu
from jax.sharding import PartitionSpec as P


HD = 72
SEQ = 256
EPS = 1e-06
F32 = jnp.float32
BF16 = jnp.bfloat16
AXES = ("dp", "tensor")


def norm_rows(values, gain_row, shifts):
    center = values - jnp.mean(values, axis=-1, keepdims=True)
    spread = lax.rsqrt(jnp.mean(center * center, axis=-1, keepdims=True) + EPS)
    normed = center * spread
    return (normed * gain_row + shifts, normed, spread)


def norm_back(grad_rows, normed, spread, gain_row):
    scaled = grad_rows * gain_row
    return spread * (
        scaled
        - jnp.mean(scaled, axis=-1, keepdims=True)
        - normed * jnp.mean(scaled * normed, axis=-1, keepdims=True)
    )


def tie(value, *others):
    return lax.optimization_barrier((value, *others))[0]


def dot_nn(a, b):
    return lax.dot_general(a, b, (((1,), (0,)), ((), ())), preferred_element_type=F32)


def dot_nt(a, b):
    return lax.dot_general(a, b, (((1,), (1,)), ((), ())), preferred_element_type=F32)


def dot_tn(a, b):
    return lax.dot_general(a, b, (((0,), (0,)), ((), ())), preferred_element_type=F32)


LANES = 128
ATTEND_VMEM = 22 << 20
BACK_VMEM = 30 << 20
FEED_VMEM = 18 << 20
FEED_OUT_VMEM = 24 << 20
SUM_VMEM = 20 << 20


def far(x):
    return pltpu.with_memory_space_constraint(x, pltpu.HBM)


def near(x):
    return pltpu.with_memory_space_constraint(x, pltpu.VMEM)


def padded(size):
    return -(-size // LANES) * LANES


class Columns:
    def __init__(self, hh):
        self.hh = hh
        self.heads = hh // HD
        self.packed = padded(4 * hh)
        self.three = padded(3 * hh + LANES - HD)
        self.low = 3 * hh // LANES * LANES
        self.window = self.packed - self.low
        self.shift = 3 * hh - self.low


def cut(array, start):
    lane = lax.broadcasted_iota(jnp.int32, (1, LANES), 1)
    piece = array[:, start : start + LANES]
    return jnp.where(lane < HD, piece, jnp.zeros_like(piece))


def place(pieces, before, width):
    rows = pieces[0].shape[0]
    parts = [piece[:, :HD] for piece in pieces]
    if before:
        parts.insert(0, jnp.zeros((rows, before), pieces[0].dtype))
    after = width - before - HD * len(pieces)
    if after:
        parts.append(jnp.zeros((rows, after), pieces[0].dtype))
    return jnp.concatenate(parts, axis=1)


def attend_kernel(cols, images, before, rows_ref, w_ref, scale_ref, bias_ref, *refs):
    lefts, rights = refs[:before], refs[before : 3 * before + 2]
    outs = refs[3 * before + 2 :] if before else refs
    qkv_ref, mixed_ref, lse_ref = outs[:3]
    heads, hh = cols.heads, cols.hh
    proj = dot_nn(rows_ref[...], w_ref[...])
    qkv = ((proj + bias_ref[...]) * scale_ref[...]).astype(BF16)
    qkv_ref[...] = qkv
    units = [(m, h) for m in range(images) for h in range(heads)]

    def unit(kind, m, h):
        return cut(qkv[m * SEQ : (m + 1) * SEQ], kind * hh + h * HD)

    scores = [dot_nt(unit(0, m, h), unit(1, m, h)) for m, h in units]
    tops = [jnp.max(s, axis=-1, keepdims=True) for s in scores]
    exps = [jnp.exp(s - top) for s, top in zip(scores, tops)]
    sums = [jnp.sum(e, axis=-1, keepdims=True) for e in exps]
    probs = [(e * (1.0 / total)).astype(BF16) for e, total in zip(exps, sums)]
    mixed = [dot_nn(p, unit(2, m, h)).astype(BF16) for (m, h), p in zip(units, probs)]
    for m in range(images):
        rows = slice(m * SEQ, (m + 1) * SEQ)
        group = slice(m * heads, (m + 1) * heads)
        mixed_ref[rows, :] = place(mixed[group], cols.shift, cols.window)
        lse = [top + jnp.log(total) for top, total in zip(tops[group], sums[group])]
        lane = lax.broadcasted_iota(jnp.int32, (1, LANES), 1)
        wide = jnp.broadcast_to(lse[0], (SEQ, LANES))
        for h in range(1, heads):
            wide = jnp.where(lane == h, lse[h], wide)
        lse_ref[rows, :] = wide
    if len(outs) == 3:
        return
    mine_ref, other_ref = outs[3:]
    total = 0.0
    for n, left in enumerate([*lefts, mixed_ref]):
        right = jnp.concatenate([rights[2 * n][...], rights[2 * n + 1][...]], axis=1)
        total += dot_nt(left[...], right)
    value = total.astype(BF16)

    @pl.when(pl.program_id(0) == 0)
    def _():
        other_ref[...] = value

    @pl.when(pl.program_id(0) != 0)
    def _():
        mine_ref[...] = value


def attend(cols, rows, weight, scale, bias, before=None):
    total, width = rows.shape
    last = before is not None
    mixeds, weights = before if last else ((), ())
    tile = total // 2
    images = tile // SEQ
    turn = (lambda i: (lax.rem(i + 1, 2), 0)) if last else (lambda i: (i, 0))
    whole = lambda i: (0, 0)
    block = cols.low // LANES
    assert not last or cols.window == 2 * LANES
    rights = [w for w in [*weights, weight] for _ in range(2)] if last else []
    out_specs = [
        pl.BlockSpec((tile, cols.three), turn),
        pl.BlockSpec((tile, cols.window), turn),
        pl.BlockSpec((tile, LANES), turn),
    ]
    out_shape = [
        pltpu.HBM((total, cols.three), BF16),
        pltpu.HBM((total, cols.window), BF16),
        pltpu.HBM((total, LANES), F32),
    ]
    if last:
        out_specs += [pl.BlockSpec((tile, width), whole)] * 2
        out_shape += [jax.ShapeDtypeStruct((tile, width), BF16), pltpu.HBM((tile, width), BF16)]
    return pl.pallas_call(
        functools.partial(attend_kernel, cols, images, len(mixeds)),
        grid=(2,),
        in_specs=[
            pl.BlockSpec((tile, width), turn),
            pl.BlockSpec((width, cols.three), whole),
            pl.BlockSpec(scale.shape, whole),
            pl.BlockSpec(bias.shape, whole),
        ]
        + [pl.BlockSpec((tile, cols.window), turn)] * len(mixeds)
        + [
            pl.BlockSpec((width, LANES), lambda i, j=n % 2: (0, block + j))
            for n in range(len(rights))
        ],
        out_specs=out_specs,
        out_shape=out_shape,
        compiler_params=pltpu.CompilerParams(vmem_limit_bytes=ATTEND_VMEM),
        cost_estimate=pl.CostEstimate(
            flops=2 * total * width * cols.packed + 4 * total * SEQ * LANES * cols.heads,
            bytes_accessed=2 * (total * (width + 4 * cols.hh) + weight.size),
            transcendentals=total * SEQ * cols.heads,
        ),
        name="attend",
    )(far(rows), weight, scale, bias, *[far(m) for m in mixeds], *rights)


def attend_back_kernel(
    cols, images, extras, own_ref, other_hbm, rows_ref, w0_ref, w1_ref, qkv_ref, mixed_ref,
    lse_ref, *refs
):
    extra_hbm = refs[:extras]
    proj_ref, gw_ref, sums_ref, acc, grad, other, sems = refs[extras : extras + 7]
    extra = refs[extras + 7 :]
    heads, hh = cols.heads, cols.hh
    step = pl.program_id(0)
    copies = [pltpu.make_async_copy(other_hbm, other, sems.at[0])] + [
        pltpu.make_async_copy(source, target, sems.at[1 + i])
        for i, (source, target) in enumerate(zip(extra_hbm, extra))
    ]

    @pl.when(step == 0)
    def _():
        for copy in copies:
            copy.start()
        grad[...] = own_ref[...]

    @pl.when(step != 0)
    def _():
        copies[0].wait()
        grad[...] = other[...]

    gh = grad[...]
    gmix = dot_nn(gh, jnp.concatenate([w0_ref[...], w1_ref[...]], axis=1)).astype(BF16)
    units = [(m, h) for m in range(images) for h in range(heads)]

    def unit(kind, m, h):
        return cut(qkv_ref[m * SEQ : (m + 1) * SEQ, :], kind * hh + h * HD)

    query = [unit(0, m, h) for m, h in units]
    keys = [unit(1, m, h) for m, h in units]
    vals = [unit(2, m, h) for m, h in units]
    gm = [cut(gmix[m * SEQ : (m + 1) * SEQ], cols.shift + h * HD) for m, h in units]
    lse = [lse_ref[m * SEQ : (m + 1) * SEQ, h : h + 1] for m, h in units]
    probs = [jnp.exp(dot_nt(q, k) - top) for q, k, top in zip(query, keys, lse)]
    dprobs = [dot_nt(g, v) for g, v in zip(gm, vals)]
    dots = [jnp.sum(p * dp, axis=-1, keepdims=True) for p, dp in zip(probs, dprobs)]
    dscores = [(p * (dp - dt)).astype(BF16) for p, dp, dt in zip(probs, dprobs, dots)]
    grads = [
        (
            dot_nn(dscores[n], keys[n]) * HD ** (-0.5),
            dot_tn(dscores[n], query[n]),
            dot_tn(probs[n].astype(BF16), gm[n]),
        )
        for n in range(len(units))
    ]
    sums = [[0.0] * heads for _ in range(2)]
    for n, (m, h) in enumerate(units):
        for row, kind in enumerate((0, 2)):
            sums[row][h] = sums[row][h] + jnp.sum(grads[n][kind], axis=0, keepdims=True)
    sums = jnp.concatenate([jnp.concatenate(s, axis=1) for s in sums], axis=0)
    for m in range(images):
        pieces = [
            grads[m * heads + h][kind].astype(BF16) for kind in range(3) for h in range(heads)
        ]
        proj_ref[m * SEQ : (m + 1) * SEQ, :] = place(pieces, 0, cols.three)
    gw_qkv = dot_tn(rows_ref[...], proj_ref[...])
    gw_out = dot_tn(gh, mixed_ref[...])

    @pl.when(step == 0)
    def _():
        acc[...] = jnp.zeros_like(acc)
        sums_ref[...] = sums

    @pl.when(step > 0)
    def _():
        sums_ref[...] += sums

    acc[:, : cols.three] += gw_qkv
    acc[:, cols.low :] += gw_out

    @pl.when(step != 0)
    def _():
        total = acc[...]
        for i in range(extras):
            copies[1 + i].wait()
            total += extra[i][...].astype(F32)
        gw_ref[...] = total.astype(BF16)


def attend_back(cols, grad_rows, rows, weight, qkv, mixed, lse, extra):
    total, width = rows.shape
    tile = total // 2
    images = tile // SEQ
    step = lambda i: (i, 0)
    whole = lambda i: (0, 0)
    lanes = cols.heads * LANES
    block = cols.low // LANES
    assert cols.window == 2 * LANES
    anywhere = pl.BlockSpec(memory_space=pl.ANY)
    own, other = grad_rows
    return pl.pallas_call(
        functools.partial(attend_back_kernel, cols, images, len(extra)),
        grid=(2,),
        in_specs=[
            pl.BlockSpec((tile, width), whole),
            anywhere,
            pl.BlockSpec((tile, width), step),
            pl.BlockSpec((width, LANES), lambda i: (0, block)),
            pl.BlockSpec((width, LANES), lambda i: (0, block + 1)),
            pl.BlockSpec((tile, cols.three), step),
            pl.BlockSpec((tile, cols.window), step),
            pl.BlockSpec((tile, LANES), step),
        ]
        + [anywhere] * len(extra),
        out_specs=[
            pl.BlockSpec((tile, cols.three), step),
            pl.BlockSpec(weight.shape, whole),
            pl.BlockSpec((2, lanes), whole),
        ],
        out_shape=[
            pltpu.HBM((total, cols.three), BF16),
            pltpu.HBM(weight.shape, BF16),
            jax.ShapeDtypeStruct((2, lanes), F32),
        ],
        scratch_shapes=[
            pltpu.VMEM(weight.shape, F32),
            pltpu.VMEM((tile, width), BF16),
            pltpu.VMEM((tile, width), BF16),
            pltpu.SemaphoreType.DMA((1 + len(extra),)),
        ]
        + [pltpu.VMEM(weight.shape, BF16)] * len(extra),
        compiler_params=pltpu.CompilerParams(vmem_limit_bytes=BACK_VMEM),
        cost_estimate=pl.CostEstimate(
            flops=2 * total * width * (cols.packed + cols.window) + 10 * total * SEQ * lanes,
            bytes_accessed=2 * (2 * total * width + 7 * total * cols.hh + 2 * weight.size),
            transcendentals=total * SEQ * cols.heads,
        ),
        name="attend_back",
    )(
        far(own), far(other), far(rows), far(weight), far(weight), far(qkv), far(mixed), far(lse),
        *map(far, extra),
    )


def sum_nt_kernel(count, *refs):
    lefts, rights = refs[:count], refs[count : 2 * count]
    before, (mine_ref, other_ref) = refs[2 * count : -2], refs[-2:]
    total = dot_nt(lefts[0][...], rights[0][...])
    for left, right in zip(lefts[1:], rights[1:]):
        total += dot_nt(left[...], right[...])
    half = pl.num_programs(0) // 2

    def store(target, source):
        value = total + source[0][...].astype(F32) if source else total
        target[...] = value.astype(BF16)

    @pl.when(pl.program_id(0) < half)
    def _():
        store(other_ref, before[1:])

    @pl.when(pl.program_id(0) >= half)
    def _():
        store(mine_ref, before[:1])


def sum_nt(lefts, rights, before=(), tile=SEQ):
    count = len(lefts)
    total, inner = lefts[0].shape
    width = rights[0].shape[0]
    half = total // 2 // tile
    rows_specs = [
        pl.BlockSpec((tile, width), lambda i: (jnp.maximum(i - half, 0), 0)),
        pl.BlockSpec((tile, width), lambda i: (jnp.minimum(i, half - 1), 0)),
    ]
    return pl.pallas_call(
        functools.partial(sum_nt_kernel, count),
        grid=(2 * half,),
        in_specs=[pl.BlockSpec((tile, inner), lambda i: (lax.rem(i + half, 2 * half), 0))] * count
        + [
            pl.BlockSpec((width, inner), lambda i: (0, 0), pipeline_mode=pl.Buffered(1))
        ]
        * count
        + rows_specs[: len(before)],
        out_specs=rows_specs,
        out_shape=[pltpu.HBM((total // 2, width), BF16)] * 2,
        compiler_params=pltpu.CompilerParams(vmem_limit_bytes=SUM_VMEM),
        cost_estimate=pl.CostEstimate(
            flops=2 * total * inner * width * count,
            bytes_accessed=2 * (count * (total + width) * inner + total * width),
            transcendentals=0,
        ),
        name="sum_nt",
    )(*map(far, lefts), *map(far, rights), *map(far, before))


def spread_kernel(count, in_ref, *out_refs):
    blocks = in_ref.shape[0]
    piece = out_refs[0].shape[1] // blocks
    for v in range(count):
        for i in range(blocks):
            out_refs[v][:, i * piece : (i + 1) * piece] = in_ref[
                i : i + 1, v * piece : (v + 1) * piece
            ]


def spread(vecs, count, width):
    return pl.pallas_call(
        functools.partial(spread_kernel, count),
        in_specs=[pl.BlockSpec(memory_space=pltpu.VMEM)],
        out_specs=[pl.BlockSpec(memory_space=pltpu.VMEM)] * count,
        out_shape=[jax.ShapeDtypeStruct((1, width), F32)] * count,
        name="spread",
    )(vecs)


def fetch_weights(core_ref, own, got, kept, sems):
    def fetch(sources):
        copies = [
            pltpu.make_async_copy(source, target, sems.at[i])
            for i, (source, target) in enumerate(zip(sources, kept))
        ]
        for copy in copies:
            copy.start()
        for copy in copies:
            copy.wait()

    @pl.when(core_ref[0] == 0)
    def _():
        fetch(own)

    @pl.when(core_ref[0] != 0)
    def _():
        fetch(got)


def feed_in_kernel(half, rows0, rows1, w1, bias_ref, rows_ref, act_ref, slope_ref):
    step = pl.program_id(0)
    rows = jnp.where(step < half, rows0[...], rows1[...])
    rows_ref[...] = rows
    pre = dot_nn(rows, w1[...]) + bias_ref[...]
    root = (2.0 / jnp.pi) ** 0.5
    square = pre * pre
    tanh = jnp.tanh(root * (pre + 0.044715 * (pre * square)))
    gate = 0.5 * (1.0 + tanh)
    slope = gate + 0.5 * pre * (1.0 - tanh * tanh) * (root * (1.0 + 3 * 0.044715 * square))
    act_ref[...] = (pre * gate).astype(BF16)
    slope_ref[...] = slope.astype(BF16)


def feed_in(rows, weight, bias, tile=SEQ):
    count, width = rows[0].shape
    ff = weight.shape[1]
    half = count // tile
    step = lambda i: (i, 0)
    whole = lambda i: (0, 0)
    return pl.pallas_call(
        functools.partial(feed_in_kernel, half),
        grid=(2 * half,),
        in_specs=[
            pl.BlockSpec((tile, width), lambda i: (jnp.minimum(i, half - 1), 0)),
            pl.BlockSpec((tile, width), lambda i: (jnp.maximum(i - half, 0), 0)),
            pl.BlockSpec((width, ff), whole, pipeline_mode=pl.Buffered(1)),
            pl.BlockSpec((1, ff), whole),
        ],
        out_specs=[
            pl.BlockSpec((tile, width), step),
            pl.BlockSpec((tile, ff), step),
            pl.BlockSpec((tile, ff), step),
        ],
        out_shape=[
            jax.ShapeDtypeStruct((2 * count, width), BF16),
            jax.ShapeDtypeStruct((2 * count, ff), BF16),
            jax.ShapeDtypeStruct((2 * count, ff), BF16),
        ],
        compiler_params=pltpu.CompilerParams(vmem_limit_bytes=FEED_VMEM),
        cost_estimate=pl.CostEstimate(
            flops=4 * count * width * ff,
            bytes_accessed=2 * (width * ff + 4 * count * (width + ff)),
            transcendentals=2 * count * ff,
        ),
        name="feed_in",
    )(*rows, near(weight), bias)


def feed_out_kernel(
    half, core_ref, cot0, cot1, act_ref, slope_ref, w1, w2_own, w2_got,
    gpre_ref, out0, out1, grad0, grad1, sums_ref, w2, sems,
):
    step = pl.program_id(0)

    @pl.when(step == 0)
    def _():
        fetch_weights(core_ref, [w2_own], [w2_got], [w2], sems)

    first = step < half
    cot = jnp.where(first, cot0[...], cot1[...])
    grad_pre = dot_nn(cot, w2[...]) * slope_ref[...].astype(F32)
    sums = jnp.sum(grad_pre, axis=0, keepdims=True)
    grad_in = grad_pre.astype(BF16)
    gpre_ref[...] = grad_in
    grad = dot_nt(grad_in, w1[...]).astype(BF16)
    out = dot_nt(act_ref[...], w2[...]).astype(BF16)

    @pl.when(step == 0)
    def _():
        sums_ref[...] = sums

    @pl.when(step > 0)
    def _():
        sums_ref[...] += sums

    @pl.when(first)
    def _():
        out0[...] = out
        grad0[...] = grad

    @pl.when(jnp.logical_not(first))
    def _():
        out1[...] = out
        grad1[...] = grad


def feed_out(core, cots, act, slope, weights, tile=SEQ):
    count, width = cots[0].shape
    ff = act.shape[1]
    half = count // tile
    low = lambda i: (jnp.minimum(i, half - 1), 0)
    high = lambda i: (jnp.maximum(i - half, 0), 0)
    step = lambda i: (i, 0)
    anywhere = pl.BlockSpec(memory_space=pl.ANY)
    return pl.pallas_call(
        functools.partial(feed_out_kernel, half),
        grid=(2 * half,),
        in_specs=[
            pl.BlockSpec(memory_space=pltpu.SMEM),
            pl.BlockSpec((tile, width), low),
            pl.BlockSpec((tile, width), high),
            pl.BlockSpec((tile, ff), step),
            pl.BlockSpec((tile, ff), step),
        ]
        + [pl.BlockSpec((width, ff), lambda i: (0, 0), pipeline_mode=pl.Buffered(1))]
        + [anywhere] * 2,
        out_specs=[
            pl.BlockSpec((tile, ff), step),
            pl.BlockSpec((tile, width), low),
            pl.BlockSpec((tile, width), high),
            pl.BlockSpec((tile, width), low),
            pl.BlockSpec((tile, width), high),
            pl.BlockSpec((1, ff), lambda i: (0, 0)),
        ],
        out_shape=[jax.ShapeDtypeStruct((2 * count, ff), BF16)]
        + [jax.ShapeDtypeStruct((count, width), BF16)] * 4
        + [jax.ShapeDtypeStruct((1, ff), F32)],
        scratch_shapes=[pltpu.VMEM((width, ff), BF16), pltpu.SemaphoreType.DMA((1,))],
        compiler_params=pltpu.CompilerParams(vmem_limit_bytes=FEED_OUT_VMEM),
        cost_estimate=pl.CostEstimate(
            flops=12 * count * width * ff,
            bytes_accessed=2 * (2 * width * ff + 2 * count * (3 * width + 3 * ff)),
            transcendentals=0,
        ),
        name="feed_out",
    )(core, *cots, act, slope, near(weights[0]), far(weights[1]), weights[2])


def norm_back_kernel(count, *refs):
    grads, (rows_ref, cot_ref, gain_ref) = refs[:count], refs[count : count + 3]
    out_ref, *rounded_ref, sums_ref = refs[count + 3 :]
    grad = grads[0][...].astype(F32)
    for other in grads[1:]:
        grad += other[...].astype(F32)
    rows = rows_ref[...].astype(F32)
    center = rows - jnp.mean(rows, axis=-1, keepdims=True)
    spread = lax.rsqrt(jnp.mean(center * center, axis=-1, keepdims=True) + EPS)
    normed = center * spread
    cot = cot_ref[...].astype(F32)
    out = cot + norm_back(grad, normed, spread, gain_ref[...])
    out_ref[...] = out
    for ref in rounded_ref:
        ref[...] = out.astype(BF16)

    @pl.when(pl.program_id(0) == 0)
    def _():
        sums_ref[...] = jnp.zeros_like(sums_ref)

    for i, value in enumerate((grad * normed, grad, out, cot)):
        sums_ref[i : i + 1, :] += jnp.sum(value, axis=0, keepdims=True)


def norm_back_rows(grads, rows, cot, gain, rounded, tile=128):
    count, width = rows.shape
    step = pl.BlockSpec((tile, width), lambda i: (i, 0))
    extra = [pltpu.HBM((count, width), BF16)] if rounded else []
    return pl.pallas_call(
        functools.partial(norm_back_kernel, len(grads)),
        grid=(count // tile,),
        in_specs=[step] * (len(grads) + 2) + [pl.BlockSpec((1, width), lambda i: (0, 0))],
        out_specs=[step] * (1 + len(extra)) + [pl.BlockSpec((8, width), lambda i: (0, 0))],
        out_shape=[
            pltpu.HBM((count, width), F32),
            *extra,
            jax.ShapeDtypeStruct((8, width), F32),
        ],
        compiler_params=pltpu.CompilerParams(vmem_limit_bytes=16 << 20),
        cost_estimate=pl.CostEstimate(
            flops=30 * count * width,
            bytes_accessed=count * width * (2 * len(grads) + 12),
            transcendentals=count,
        ),
        name="norm_back",
    )(*grads, far(rows), far(cot), gain)


def norm_kernel(count, *refs):
    parts, (shift_ref, gain_ref, bias_ref) = refs[:count], refs[count : count + 3]
    rows_ref, out_ref = refs[count + 3 :]
    rows = parts[0][...].astype(F32) + shift_ref[...]
    for part in parts[1:]:
        rows += part[...].astype(F32)
    rows_ref[...] = rows
    out_ref[...] = norm_rows(rows, gain_ref[...], bias_ref[...])[0].astype(BF16)


def norm_sum(parts, shift, gain, bias, tile=128):
    count, width = parts[0].shape
    step = pl.BlockSpec((tile, width), lambda i: (i, 0))
    row = pl.BlockSpec((1, width), lambda i: (0, 0))
    return pl.pallas_call(
        functools.partial(norm_kernel, len(parts)),
        grid=(count // tile,),
        in_specs=[step] * len(parts) + [row] * 3,
        out_specs=[step, step],
        out_shape=[pltpu.HBM((count, width), F32), jax.ShapeDtypeStruct((count, width), BF16)],
        compiler_params=pltpu.CompilerParams(vmem_limit_bytes=16 << 20),
        cost_estimate=pl.CostEstimate(
            flops=12 * count * width,
            bytes_accessed=count * width * (2 * len(parts) + 6),
            transcendentals=count,
        ),
        name="norm_sum",
    )(*parts, shift, gain, bias)


def pack_kernel(where_ref, first_ref, second_ref, *refs):
    units, bias_ref, out_ref = refs[:-2], refs[-2], refs[-1]
    out_ref[...] = jnp.zeros_like(out_ref)
    width = first_ref.shape[1]
    for spot, ref, row in (
        (0, first_ref, 0), (1, second_ref, 0), (2, first_ref, 1),
        (3, second_ref, 2), (4, second_ref, 1), (5, second_ref, 3),
    ):
        out_ref[spot : spot + 1, :width] = ref[row : row + 1, :]
    core = where_ref[0]
    for n, unit in enumerate(units):
        lanes = unit.shape[1]
        spot = 7 + 2 * where_ref[2 + n]
        sums = jnp.concatenate([unit[0:1, :], unit[1:2, :]], axis=1)

        @pl.when(core == 0)
        def _():
            out_ref[pl.ds(spot, 1), : 2 * lanes] = sums

        @pl.when(core != 0)
        def _():
            out_ref[pl.ds(spot, 1), 2 * lanes : 4 * lanes] = sums

    out_ref[pl.ds(6 + 2 * where_ref[1], 1), : bias_ref.shape[1]] = bias_ref[...]


def pack_small(where, vectors, units, bias, spots):
    lanes = max(x.shape[1] for x in [*vectors, bias])
    rows = -(-(6 + 2 * spots) // 8) * 8
    return pl.pallas_call(
        pack_kernel,
        in_specs=[pl.BlockSpec(memory_space=pltpu.SMEM)]
        + [pl.BlockSpec(memory_space=pltpu.VMEM)] * (len(vectors) + len(units) + 1),
        out_specs=pl.BlockSpec(memory_space=pltpu.VMEM),
        out_shape=jax.ShapeDtypeStruct((rows, lanes), F32),
        name="pack_small",
    )(where, *vectors, *units, bias)


def make_body(ndp, nt):
    nz = ndp // 2
    bits = nt.bit_length() - 1
    top = nt // 2
    low = nt // 2

    def perm(move):
        pairs = []
        for d in range(ndp):
            for t in range(nt):
                d2, t2 = move(d, t)
                pairs.append((d * nt + t, d2 * nt + t2))
        return pairs

    def send(value, move):
        return lax.ppermute(value, AXES, perm(move))

    def swap_core(value):
        return send(value, lambda d, t: (d ^ 1, t))

    def swap_tensor(value, i):
        return send(value, lambda d, t: (d, t ^ i))

    def shift_z(value, k):
        return send(value, lambda d, t: ((d + 2 * k) % ndp, t))

    def stage(value, i):
        return send(
            value, lambda d, t: (d, t ^ ((1 << i) if d % 2 == 0 else (1 << (bits - 1 - i))))
        )

    def reverse_bits(p):
        return sum(((p >> i) & 1) << (bits - 1 - i) for i in range(bits))

    def swap_top(value):
        pairs = [(d * nt + t, d * nt + (t ^ top)) for d in range(1, ndp, 2) for t in range(nt)]
        return lax.ppermute(value, AXES, pairs)

    def gather_z(value, z):
        out = jnp.zeros((nz,) + value.shape, value.dtype)
        out = lax.dynamic_update_slice_in_dim(out, value[None], z, 0)
        for k in range(1, nz):
            got = shift_z(value, k)
            out = lax.dynamic_update_slice_in_dim(out, got[None], lax.rem(z - k + nz, nz), 0)
        return out

    def pick(selector, items):
        total = jnp.where(selector == 0, items[0], 0)
        for i in range(1, len(items)):
            total = total + jnp.where(selector == i, items[i], 0)
        return total

    def body(
        tokens, norm_gains, row_biases, w_qkv, head_bias, w_out, w_fc1, fc1_bias, w_fc2, cotangent
    ):
        d = lax.axis_index("dp")
        t = lax.axis_index("tensor")
        z, c = d // 2, d % 2
        core0 = c == 0
        _, width = tokens.shape
        block = w_qkv.shape[2]
        hh = block // 2
        part = w_qkv.shape[1]
        ff = w_fc1.shape[1]

        def by_core(zero, one):
            return jnp.where(core0, zero, one)

        w_out_t = w_out.T

        cols = Columns(hh)
        packed, heads = cols.packed, cols.heads
        wide = padded(ff)

        def half(h):
            sl = slice(h * hh, (h + 1) * hh)
            cols = [w_qkv[0][:, sl], w_qkv[1][:, sl], w_qkv[2][:, sl], w_out_t[:, sl]]
            return jnp.pad(jnp.concatenate(cols, axis=1), ((0, 0), (0, packed - 4 * hh)))

        gathered = lax.all_gather(jnp.stack([half(0), half(1)]), "dp", axis=1, tiled=True)
        others = range(1, low)
        cot_far = [swap_tensor(cotangent, i) for i in others]

        gain_count, shift_count = norm_gains.shape[0], row_biases.shape[0]
        vec_count = gain_count + shift_count
        piece = norm_gains.shape[1]
        small = jnp.concatenate(
            [norm_gains.reshape(-1), row_biases.reshape(-1), head_bias.reshape(-1), fc1_bias]
        )
        smalls = [small] + [swap_tensor(small, i) for i in range(1, nt)]
        vec_size = vec_count * piece
        vecs = jnp.stack([pick(t ^ i, [s[:vec_size] for s in smalls]) for i in range(nt)])
        vecs = gather_z(vecs, z)
        vecs_other = swap_core(vecs)
        vecs = jnp.stack([by_core(vecs, vecs_other), by_core(vecs_other, vecs)], axis=1)
        vecs = spread(vecs.reshape(nz * 2 * nt, vec_size), vec_count, width)
        gain_rows, shifts = vecs[:gain_count], vecs[gain_count:]
        head_biases = jnp.stack([s[vec_size : vec_size + 2 * block] for s in smalls])
        turned = jnp.stack(
            [smalls[reverse_bits(p)][vec_size : vec_size + 2 * block] for p in range(nt)]
        )
        unit_bias = by_core(head_biases, turned).reshape(nt, 2, 2, hh)
        unit_bias = by_core(unit_bias[:, :, 0], unit_bias[:, :, 1])
        unit_bias = jnp.concatenate(
            [
                unit_bias[:, 0],
                jnp.zeros((nt, hh), F32),
                unit_bias[:, 1],
                jnp.zeros((nt, cols.three - 3 * hh), F32),
            ],
            axis=1,
        ).reshape(nt, 1, cols.three)
        scale = jnp.where(jnp.arange(cols.three) < hh, HD ** (-0.5), 1.0).astype(F32)
        scale = scale.reshape(1, cols.three)
        ff_bias = by_core(smalls[0][vec_size + 2 * block :], smalls[top][vec_size + 2 * block :])
        ff_bias = jnp.pad(ff_bias, (0, wide - ff)).reshape(1, wide)

        inputs_f = tokens.astype(F32)
        first = norm_rows(inputs_f, gain_rows[0], shifts[0])[0].astype(BF16)
        first_chip = jnp.concatenate([first, swap_core(first)], axis=0)

        cots = [(g, swap_core(g)) for g in [cotangent, *cot_far]]
        early = (first_chip, unit_bias, ff_bias)
        attn_w = [lax.dynamic_index_in_dim(tie(gathered, *early), c, 0, keepdims=False)]
        saved = [attend(cols, first_chip, attn_w[0], scale, unit_bias[0])]
        cot_rows = [jnp.concatenate([tie(g, saved[0][1]), o], axis=0) for g, o in cots]
        no_sum = lax.optimization_barrier(jnp.zeros(attn_w[0].shape, BF16))
        for i in range(bits):
            sent = list(attn_w)
            if i:
                sent[-1] = tie(sent[-1], *cot_rows, no_sum)
            attn_w = attn_w + [stage(b, i) for b in sent]

        def gather_ff(own):
            return lax.all_gather(
                jnp.pad(own, ((0, 0), (0, wide - ff))), "dp", axis=0, tiled=True
            )

        fc1_own, fc2_own = gather_ff(w_fc1), gather_ff(tie(w_fc2.T, *vecs))

        for p in range(1, nt):
            before = None
            if p == nt - 1:
                before = ([s[1] for s in saved], attn_w[:p])
            saved.append(attend(cols, first_chip, attn_w[p], scale, unit_bias[p], before))
        attn_mine, attn_other = saved[-1][3:]
        fc1_got = swap_top(tie(fc1_own, attn_w[nt - 1], attn_w[nt - 2]))
        fc2_got = swap_top(fc2_own)
        hidden_one, second = norm_sum(
            [tokens, attn_mine, swap_core(attn_other)], shifts[1], gain_rows[1], shifts[2]
        )

        core = c.astype(jnp.int32).reshape(1)
        second_far = [swap_tensor(second, i) for i in others]
        fc1 = by_core(fc1_own, fc1_got)
        ins = [None] * low
        ins[0] = feed_in((second, swap_core(second)), fc1, ff_bias)
        grad_fc2_t = dot_tn(cot_rows[0], ins[0][1])
        for i, rows_far in zip(others, second_far):
            rows_far = tie(rows_far, grad_fc2_t)
            ins[i] = feed_in((rows_far, swap_core(rows_far)), fc1, ff_bias)

        outs, grad_sums, pres, grad_fc1_bias = [None] * low, [None] * low, [None] * low, 0
        after = []
        for i in reversed(range(low)):
            act, slope = ins[i][1:]
            if i == 0 or i == low - 1:
                slope = tie(slope, *after)
            pres[i], out0, out1, grad0, grad1, sums = feed_out(
                core, cots[i], act, slope, (fc1, fc2_own, fc2_got)
            )
            grad_fc1_bias = grad_fc1_bias + sums
            got = swap_core(grad1)
            got_out = swap_core(out1).astype(F32)
            if i:
                grad_fc2_t = grad_fc2_t + dot_tn(cot_rows[i], tie(ins[i][1], pres[i]))
                got = tie(got, grad_fc2_t)
            if i:
                got = (grad0.astype(F32) + got.astype(F32)).astype(BF16)
            grad_sums[i] = got
            grad_near = grad0
            if i == 1:
                grad_fc2_t = tie(grad_fc2_t, grad_sums[i]).astype(BF16)
            outs[i] = out0.astype(F32) + got_out
            if i:
                outs[i] = tie(outs[i].astype(BF16), grad_sums[i])
            after = [grad_sums[i], grad_fc2_t, outs[i]]
        got_fc2 = swap_top(grad_fc2_t)
        grad_fc1 = 0
        for i in reversed(range(low)):
            grad_fc1 = grad_fc1 + dot_tn(ins[i][0], tie(pres[i], grad_sums[0]))
        grad_fc1 = grad_fc1.astype(BF16)
        got_fc1 = swap_top(grad_fc1)

        def scatter_ff(partial):
            own = lax.psum_scatter(partial, "dp", scatter_dimension=0, tiled=True)
            return lax.optimization_barrier(own)

        grad_fc2_t = by_core(grad_fc2_t, tie(got_fc2, grad_fc1))
        sum_fc2 = scatter_ff(grad_fc2_t)

        grad_second = [grad_near, grad_sums[0]]
        for i in others:
            got = swap_tensor(grad_sums[i], i)
            grad_second.append(tie(got, grad_fc1, grad_fc2_t))
        mlp_out = outs[0]
        for i in others:
            mlp_out = mlp_out + swap_tensor(outs[i], i).astype(F32)

        grad_hidden, hidden_in, second_sums = norm_back_rows(
            grad_second, hidden_one, cotangent, gain_rows[1], True
        )
        hidden_pair = (hidden_in, swap_core(hidden_in))
        back, after = {}, None
        grad_w = [None] * nt
        got_w = {}
        for p in reversed(range(nt)):
            qkv, mix, lse = saved[p][:3]
            if after is not None:
                lse = tie(lse, *after)
            come = sorted((q for q in got_w if got_w[q][0] == p and (p or q > 1)), reverse=True)
            extra = [got_w[q][1] for q in come] or [no_sum]
            back[p] = attend_back(cols, hidden_pair, first_chip, attn_w[p], qkv, mix, lse, extra)
            value = back[p][1]
            grad_w[p] = value
            after = [value]
            if p == 1:
                parts = [q for q in range(nt) if q > 1]
                first_part = sum_nt(
                    [tie(back[q][0], value) for q in parts], [attn_w[q] for q in parts]
                )
                after = [value, first_part[0]]
            if p == nt - 2:
                grad_fc1 = by_core(grad_fc1, tie(got_fc1, value))
                sum_fc1 = scatter_ff(grad_fc1)
                after = [value, grad_fc1]
            if p == 0:
                break
            i = p.bit_length() - 1
            got_w[p] = (p - (1 << i), stage(value, i))
        grad_w = [(grad_w[0].astype(F32) + got_w[1][1].astype(F32)).astype(BF16)]
        first_mine, first_other = sum_nt(
            [tie(back[q][0], grad_w[0]) for q in (1, 0)], attn_w[1::-1], first_part
        )
        own_half = lax.psum_scatter(
            grad_w[0],
            "dp",
            scatter_dimension=0,
            axis_index_groups=[list(range(0, ndp, 2)), list(range(1, ndp, 2))],
            tiled=True,
        )
        own_half = own_half.reshape(2, part, packed)
        sent_half = by_core(own_half[1], own_half[0])
        kept = by_core(own_half[0], own_half[1]).astype(F32)
        got = swap_core(sent_half).astype(F32)
        halves = [by_core(kept, got), by_core(got, kept)]
        grad_qkv_own = jnp.stack(
            [
                jnp.concatenate([g[:, k * hh : (k + 1) * hh] for g in halves], axis=1)
                for k in range(3)
            ]
        )
        grad_out_own = jnp.concatenate([g[:, 3 * hh : 4 * hh] for g in halves], axis=1).T

        grad_tokens, first_sums = norm_back_rows(
            [first_mine, swap_core(first_other)], tokens, grad_hidden, gain_rows[0], False
        )

        spots = [by_core(t ^ p, t ^ reverse_bits(p)) for p in range(nt)]
        where = jnp.stack([c, by_core(t, t ^ top)] + spots).astype(jnp.int32)
        total = pack_small(
            where,
            [first_sums, second_sums],
            [back[p][2] for p in range(nt)],
            grad_fc1_bias,
            nt,
        )
        output = hidden_one + tie(mlp_out, total) + shifts[3]
        total = functools.reduce(jnp.add, [swap_tensor(total, i) for i in range(1, nt)], total)
        total = tie(total, grad_tokens, output)
        grad_fc2_own = sum_fc2[:, :ff].astype(F32).T
        grad_fc1_own = sum_fc1[:, :ff].astype(F32)
        total = functools.reduce(jnp.add, [shift_z(total, k) for k in range(1, nz)], total)
        total = tie(total, output, grad_fc1_own, grad_fc2_own, grad_qkv_own, grad_out_own)
        total = total + swap_core(total)
        own = lax.dynamic_slice_in_dim(
            total[:vec_count, :width], (d * nt + t) * piece, piece, axis=1
        )
        mine = lax.dynamic_slice_in_dim(total, 6 + 2 * t, 2, axis=0)
        bias_total = mine[0, :ff]
        units = mine[1, : 4 * heads * LANES].reshape(2, 2, heads, LANES)[:, :, :, :HD]
        head_total = units.transpose(1, 0, 2, 3).reshape(2, block)
        return (
            output,
            grad_tokens,
            own[:gain_count],
            own[gain_count:],
            grad_qkv_own,
            head_total,
            grad_out_own,
            grad_fc1_own,
            bias_total,
            grad_fc2_own,
        )

    return body


def solution(mesh):
    in_specs = (
        P(("dp", "tensor"), None),
        P(None, ("dp", "tensor")),
        P(None, ("dp", "tensor")),
        P(None, "dp", "tensor"),
        P(None, "tensor"),
        P("tensor", "dp"),
        P("dp", "tensor"),
        P("tensor"),
        P("tensor", "dp"),
        P(("dp", "tensor"), None),
    )
    out_specs = (
        P(("dp", "tensor"), None),
        P(("dp", "tensor"), None),
        P(None, ("dp", "tensor")),
        P(None, ("dp", "tensor")),
        P(None, "dp", "tensor"),
        P(None, "tensor"),
        P("tensor", "dp"),
        P("dp", "tensor"),
        P("tensor"),
        P("tensor", "dp"),
    )
    body = make_body(mesh.shape["dp"], mesh.shape["tensor"])

    return jax.shard_map(body, mesh=mesh, in_specs=in_specs, out_specs=out_specs, check_vma=False)
```
